256 devices in a mesh: req: 64 (over x, z, y_lo), kv: 4 (over y_hi, core).
Axes of the slice: x: 4, y: 4 (y_hi: 2, y_lo: 2; y = y_hi * 2 + y_lo), z: 8, core: 2. Of those that a mesh axis runs over, the one named last changes fastest.
Arguments:
- hidden: bfloat16 [64, 1024, 1536], P('req', 'kv'), may hold values from -6 to 6
- lengths: int32 [64], P('req'), may hold values from 1 to 2048, as said below
- key_cache: bfloat16 [64, 2048, 768], P('req', 'kv'), may hold values from -180 to 180
- value_cache: bfloat16 [64, 2048, 768], P('req', 'kv'), may hold values from -6 to 6
- norm_gain: bfloat16 [1536], replicated, may hold values from 0.099609375 to 1.8984375
- w_query: bfloat16 [1536, 1536], P('req', 'kv'), may hold values from -0.15625 to 0.15625
- w_key: bfloat16 [1536, 768], P('req', 'kv'), may hold values from -0.15625 to 0.15625
- w_value: bfloat16 [1536, 768], P('req', 'kv'), may hold values from -0.15625 to 0.15625
- w_out: bfloat16 [1536, 1536], P('req', 'kv'), may hold values from -0.15625 to 0.15625
Outputs:
- attended: bfloat16 [64, 1024, 1536], P('req', 'kv')
- new_keys: bfloat16 [64, 1024, 768], P('req', 'kv')
- new_values: bfloat16 [64, 1024, 768], P('req', 'kv')
The draws below stay inside these ranges and needn't reach their ends.
Inputs may be any that keep to these rules, and one draw needn't show every extreme that they name: `lengths`: at least a quarter of the requests (one or more) hold more than 1792 tokens, one of them exactly 2048; the others hold fewer than 512.
All inputs are finite; a program needn't handle non-finite values.
Results may differ from the reference program's by a relative error of at most 0.011.
Values may be sent and summed in bfloat16 or wider, within the bound.
A program may use at most 192 MiB of HBM per device.

```python
import jax
import jax.numpy as jnp
from jax import lax

D = 1536
H = 16
KVH = 8
HD = 96
APPEND = 1024
CACHE_DEV = 512
REQ = 64
CACHE = 2048
N_KV = 4


def draw_lengths(key, part):
    key_order = jax.random.fold_in(key, 11)
    key_long = jax.random.fold_in(key, 12)
    key_short = jax.random.fold_in(key, 13)
    order = jax.random.permutation(key_order, REQ).astype(jnp.int32)
    longer = order < max(REQ // 4, 1)
    long_lengths = CACHE - jax.random.randint(key_long, (REQ,), 0, CACHE_DEV // 2)
    short_lengths = jax.random.randint(key_short, (REQ,), 1, CACHE_DEV)
    chosen = jnp.where(longer, long_lengths, short_lengths)
    return jnp.where(order == 0, CACHE, chosen).astype(jnp.int32)


def draw_key_cache(key, part):
    key_base = jax.random.fold_in(key, 21)
    shape = (REQ, CACHE, KVH * HD)
    base = jnp.clip(jax.random.normal(key_base, shape, jnp.float32), -6.0, 6.0) * 2.0
    return base.astype(jnp.bfloat16)


def block_scale(rng, shape, cuts, low, largest):
    level, own = 1.0, jax.random.fold_in(rng, 6)
    for axis_at, blocks in cuts:
        heights = jnp.exp(jax.random.uniform(jax.random.fold_in(own, axis_at), (blocks,), jnp.float32, low / len(cuts), largest / len(cuts)))
        level = level * jnp.repeat(heights, shape[axis_at] // blocks).reshape([-1 if axis == axis_at else 1 for axis in range(len(shape))])
    return level


def scatter_about(stream_key, dims, deviation, limit, split=(), held_as=jnp.bfloat16):
    drawn = jax.random.normal(stream_key, dims, jnp.float32) * deviation
    if len(split) > 0:
        drawn = block_scale(stream_key, dims, split, -0.22, 0.18) * drawn
    return jnp.clip(drawn, min=-limit, max=limit).astype(held_as)


def setup_inputs(seed: int = 0) -> dict:
    seeds = jax.random.split(jax.random.key(seed), 10)
    return {
        "hidden": scatter_about(seeds[0], (REQ, APPEND, D), 1.0, 6.0, ((0, 64), (1, 4))),
        "lengths": draw_lengths(jax.random.fold_in(seeds[9], 71), 0),
        "key_cache": draw_key_cache(jax.random.fold_in(seeds[9], 71), 0),
        "value_cache": scatter_about(seeds[3], (REQ, CACHE, KVH * HD), 1.0, 6.0, ((0, 64), (1, 4))),
        "norm_gain": jnp.clip(1.0 + 0.18 * jax.random.normal(seeds[4], (D,), jnp.float32), 0.099609375, 1.8984375).astype(jnp.bfloat16),
        "w_query": scatter_about(seeds[5], (D, H * HD), D ** -0.5, 0.15625, ((0, 64), (1, 4))),
        "w_key": scatter_about(seeds[6], (D, KVH * HD), D ** -0.5, 0.15625, ((0, 64), (1, 4))),
        "w_value": scatter_about(seeds[7], (D, KVH * HD), D ** -0.5, 0.15625, ((0, 64), (1, 4))),
        "w_out": scatter_about(seeds[8], (H * HD, D), (H * HD) ** -0.5, 0.15625, ((0, 64), (1, 4))),
    }


rope_base = 100000.0
masked_score = -1e+30

def rms_norm(states, gain):
    mean_square = lax.optimization_barrier(jnp.mean(states * states, axis=-1, keepdims=True))
    scaled = states * lax.rsqrt(mean_square + 1e-05) * gain.astype(jnp.float32)
    return scaled.astype(jnp.bfloat16)

def rotate(values, positions):
    count = values.shape[0]
    heads = values.shape[1] // HD
    half = HD // 2
    frequency = rope_base ** (-(jnp.arange(half, dtype=jnp.float32) * 2.0 / HD))
    angle = positions[:, None] * frequency[None, :]
    cosine = jnp.cos(angle)[:, None, :]
    sine = jnp.sin(angle)[:, None, :]
    shaped = values.reshape(count, heads, HD)
    first = shaped[..., :half]
    second = shaped[..., half:]
    turned = jnp.concatenate([first * cosine - second * sine, second * cosine + first * sine], axis=-1)
    return turned.reshape(count, heads * HD)

def reference(hidden, lengths, key_cache, value_cache, norm_gain, w_query, w_key, w_value, w_out):
    groups = H // KVH
    scale = HD ** (-0.5)
    rows_block = APPEND // N_KV

    def one_request(operands):
        states, length, keys_old, values_old = operands
        normed = rms_norm(states.astype(jnp.float32), norm_gain)
        positions = (length + jnp.arange(APPEND, dtype=jnp.int32)).astype(jnp.float32)
        queries = rotate(jnp.dot(normed, w_query, preferred_element_type=jnp.float32), positions).astype(jnp.bfloat16)
        keys_new = rotate(jnp.dot(normed, w_key, preferred_element_type=jnp.float32), positions).astype(jnp.bfloat16)
        values_new = jnp.dot(normed, w_value, preferred_element_type=jnp.float32).astype(jnp.bfloat16)
        query_index = jnp.arange(APPEND, dtype=jnp.int32)
        query_heads = queries.reshape(APPEND, KVH, groups, HD).astype(jnp.float32)
        peaks, outputs, totals = ([], [], [])
        for block in range(N_KV):
            keys_block = jnp.concatenate([keys_old[block * CACHE_DEV:(block + 1) * CACHE_DEV], keys_new[block * rows_block:(block + 1) * rows_block]], axis=0)
            values_block = jnp.concatenate([values_old[block * CACHE_DEV:(block + 1) * CACHE_DEV], values_new[block * rows_block:(block + 1) * rows_block]], axis=0)
            cache_live = block * CACHE_DEV + jnp.arange(CACHE_DEV, dtype=jnp.int32) < length
            own_index = block * rows_block + jnp.arange(rows_block, dtype=jnp.int32)
            visible = jnp.concatenate([jnp.broadcast_to(cache_live[None, :], (APPEND, CACHE_DEV)), own_index[None, :] <= query_index[:, None]], axis=1)
            key_heads = keys_block.reshape(-1, KVH, HD).astype(jnp.float32)
            value_heads = values_block.reshape(-1, KVH, HD).astype(jnp.float32)
            score = jnp.einsum('qhgd,khd->hgqk', query_heads, key_heads) * scale
            score = jnp.where(visible, score, masked_score)
            peak = lax.optimization_barrier(jnp.max(score, axis=-1))
            weights = jnp.where(visible, jnp.exp(score - peak[..., None]), 0.0)
            total = lax.optimization_barrier(jnp.sum(weights, axis=-1))
            rounded = lax.optimization_barrier(weights.astype(jnp.bfloat16))
            context = jnp.einsum('hgqk,khd->qhgd', rounded.astype(jnp.float32), value_heads)
            divisor = jnp.transpose(jnp.maximum(total, 1.0), (2, 0, 1))[..., None]
            output = lax.optimization_barrier((context / divisor).astype(jnp.bfloat16))
            peaks.append(peak)
            outputs.append(output.astype(jnp.float32))
            totals.append(total)
        peaks = jnp.stack(peaks)
        outputs = jnp.stack(outputs)
        totals = jnp.stack(totals)
        peak_all = lax.optimization_barrier(jnp.max(peaks, axis=0))
        share = jnp.exp(peaks - peak_all[None]) * totals
        numerator = lax.optimization_barrier(jnp.sum(outputs * jnp.transpose(share, (0, 3, 1, 2))[..., None], axis=0))
        denominator = lax.optimization_barrier(jnp.sum(share, axis=0))
        context = (numerator / jnp.transpose(denominator, (2, 0, 1))[..., None]).reshape(APPEND, H * HD).astype(jnp.bfloat16)
        attended = jnp.dot(context, w_out, preferred_element_type=jnp.float32).astype(jnp.bfloat16)
        return (attended, keys_new, values_new)
    return lax.map(one_request, (hidden, lengths, key_cache, value_cache))
```

```python
import jax
import jax.numpy as jnp
from jax import lax
from jax.sharding import PartitionSpec as P

H = 16
KVH = 8
HD = 96


rope_base = 100000.0
masked_score = -1e30


def rms_norm(states, gain):
    mean_square = jnp.mean(states * states, axis=-1, keepdims=True)
    scaled = states * lax.rsqrt(mean_square + 1e-05) * gain.astype(jnp.float32)
    return scaled.astype(jnp.bfloat16)


def rotate(values, positions):
    count = values.shape[0]
    heads = values.shape[1] // HD
    half = HD // 2
    frequency = rope_base ** (-(jnp.arange(half, dtype=jnp.float32) * 2.0 / HD))
    angle = positions[:, None] * frequency[None, :]
    cosine = jnp.cos(angle)[:, None, :]
    sine = jnp.sin(angle)[:, None, :]
    shaped = values.reshape(count, heads, HD)
    first = shaped[..., :half]
    second = shaped[..., half:]
    turned = jnp.concatenate(
        [first * cosine - second * sine, second * cosine + first * sine], axis=-1
    )
    return turned.reshape(count, heads * HD)


def body(hidden, lengths, key_cache, value_cache, norm_gain, w_query, w_key, w_value, w_out):
    rows_here = hidden.shape[1]
    kv_count = lax.axis_size("kv")
    appended = rows_here * kv_count
    slots = key_cache.shape[1]
    groups = H // KVH
    scale = HD ** (-0.5)
    length = lengths[0]
    q_cols = w_query.shape[1]
    k_cols = w_key.shape[1]
    v_cols = w_value.shape[1]
    heads_here = q_cols // HD
    kv_heads_here = k_cols // HD

    normed = rms_norm(hidden[0].astype(jnp.float32), norm_gain)
    normed_all = lax.all_gather(normed, "kv", axis=0, tiled=True)

    pieces = jnp.concatenate([w_query, w_key, w_value, w_out], axis=1)
    cols = lax.all_gather(pieces, "req", axis=0, tiled=True)
    wq = cols[:, :q_cols]
    wk = cols[:, q_cols:q_cols + k_cols]
    wv = cols[:, q_cols + k_cols:q_cols + k_cols + v_cols]
    wo = cols[:, q_cols + k_cols + v_cols:]

    positions = (length + jnp.arange(appended, dtype=jnp.int32)).astype(jnp.float32)
    proj_q = jnp.dot(normed_all, wq, preferred_element_type=jnp.float32)
    proj_k = jnp.dot(normed_all, wk, preferred_element_type=jnp.float32)
    proj_v = jnp.dot(normed_all, wv, preferred_element_type=jnp.float32)
    queries = rotate(proj_q, positions).astype(jnp.bfloat16)
    keys_new = rotate(proj_k, positions).astype(jnp.bfloat16)
    values_new = proj_v.astype(jnp.bfloat16)

    new_keys = lax.all_to_all(keys_new, "kv", split_axis=0, concat_axis=1, tiled=True)
    new_values = lax.all_to_all(values_new, "kv", split_axis=0, concat_axis=1, tiled=True)

    keys_old = lax.all_to_all(key_cache[0], "kv", split_axis=1, concat_axis=0, tiled=True)
    values_old = lax.all_to_all(value_cache[0], "kv", split_axis=1, concat_axis=0, tiled=True)
    cache_slots = keys_old.shape[0]

    keys_all = jnp.concatenate([keys_old, keys_new], axis=0)
    values_all = jnp.concatenate([values_old, values_new], axis=0)
    key_count = keys_all.shape[0]
    query_index = jnp.arange(appended, dtype=jnp.int32)
    cache_live = jnp.arange(cache_slots, dtype=jnp.int32) < length
    visible = jnp.concatenate(
        [
            jnp.broadcast_to(cache_live[None, :], (appended, cache_slots)),
            query_index[None, :] <= query_index[:, None],
        ],
        axis=1,
    )
    query_heads = jnp.transpose(
        queries.reshape(appended, kv_heads_here, groups, HD), (1, 0, 2, 3)
    )
    key_heads = jnp.transpose(keys_all.reshape(key_count, kv_heads_here, HD), (1, 0, 2))
    value_heads = jnp.transpose(values_all.reshape(key_count, kv_heads_here, HD), (1, 0, 2))

    def attend(operands):
        query_block, key_block, value_block = operands
        score = (
            jnp.einsum("qgd,kd->gqk", query_block, key_block, preferred_element_type=jnp.float32)
            * scale
        )
        score = jnp.where(visible[None], score, masked_score)
        peak = jnp.max(score, axis=-1)
        weights = jnp.where(visible[None], jnp.exp(score - peak[..., None]), 0.0)
        total = jnp.sum(weights, axis=-1)
        context = jnp.einsum(
            "gqk,kd->qgd",
            weights.astype(jnp.bfloat16),
            value_block,
            preferred_element_type=jnp.float32,
        )
        return context / jnp.transpose(total)[:, :, None]

    contexts = lax.map(attend, (query_heads, key_heads, value_heads))
    context = (
        jnp.transpose(contexts, (1, 0, 2, 3)).reshape(appended, heads_here * HD).astype(jnp.bfloat16)
    )
    context_all = lax.all_gather(context, "kv", axis=1, tiled=True)
    attended_cols = jnp.dot(context_all, wo, preferred_element_type=jnp.float32).astype(jnp.bfloat16)
    attended = lax.all_to_all(attended_cols, "kv", split_axis=0, concat_axis=1, tiled=True)
    return (attended[None], new_keys[None], new_values[None])


def solution(mesh):
    return jax.shard_map(
        body,
        mesh=mesh,
        in_specs=(
            P("req", "kv", None),
            P("req"),
            P("req", "kv", None),
            P("req", "kv", None),
            P(),
            P("req", "kv"),
            P("req", "kv"),
            P("req", "kv"),
            P("req", "kv"),
        ),
        out_specs=(P("req", "kv", None), P("req", "kv", None), P("req", "kv", None)),
        check_vma=False,
    )
```

```python
import functools

import jax
import jax.numpy as jnp
from jax import lax
from jax.sharding import PartitionSpec as P
from jax.experimental import pallas as pl
from jax.experimental.pallas import tpu as pltpu

H = 16
KVH = 8
HD = 96


rope_base = 100000.0
masked_score = -1e30


def rms_norm(states, gain):
    mean_square = jnp.mean(states * states, axis=-1, keepdims=True)
    scaled = states * lax.rsqrt(mean_square + 1e-05) * gain.astype(jnp.float32)
    return scaled.astype(jnp.bfloat16)


def rotate(values, positions):
    count = values.shape[0]
    heads = values.shape[1] // HD
    half = HD // 2
    frequency = rope_base ** (-(jnp.arange(half, dtype=jnp.float32) * 2.0 / HD))
    angle = positions[:, None] * frequency[None, :]
    cosine = jnp.cos(angle)[:, None, :]
    sine = jnp.sin(angle)[:, None, :]
    shaped = values.reshape(count, heads, HD)
    first = shaped[..., :half]
    second = shaped[..., half:]
    turned = jnp.concatenate(
        [first * cosine - second * sine, second * cosine + first * sine], axis=-1
    )
    return turned.reshape(count, heads * HD)


def fan_out_kernel(count, src_ref, out_ref, send_sem, recv_sem, local_sem):
    me = lax.axis_index("req")
    kv = lax.axis_index("kv")
    barrier = pltpu.get_barrier_semaphore()

    def greet(step, carry):
        peer = lax.rem(me + step, count)
        pl.semaphore_signal(
            barrier, inc=1, device_id=(peer, kv), device_id_type=pl.DeviceIdType.MESH
        )
        return carry

    lax.fori_loop(1, count, greet, 0)
    pl.semaphore_wait(barrier, count - 1)

    local = pltpu.make_async_copy(src_ref, out_ref.at[me], local_sem)
    local.start()

    def send(step, carry):
        peer = lax.rem(me + step, count)
        pltpu.make_async_remote_copy(
            src_ref=src_ref,
            dst_ref=out_ref.at[me],
            send_sem=send_sem.at[step - 1],
            recv_sem=recv_sem.at[step - 1],
            device_id=(peer, kv),
            device_id_type=pl.DeviceIdType.MESH,
        ).start()
        return carry

    lax.fori_loop(1, count, send, 0)

    def finish(step, carry):
        peer = lax.rem(me + step, count)
        source = lax.rem(me + count - step, count)
        pltpu.make_async_remote_copy(
            src_ref=src_ref,
            dst_ref=out_ref.at[me],
            send_sem=send_sem.at[step - 1],
            recv_sem=recv_sem.at[step - 1],
            device_id=(peer, kv),
            device_id_type=pl.DeviceIdType.MESH,
        ).wait_send()
        pltpu.make_async_remote_copy(
            src_ref=src_ref,
            dst_ref=out_ref.at[source],
            send_sem=send_sem.at[step - 1],
            recv_sem=recv_sem.at[step - 1],
            device_id=(source, kv),
            device_id_type=pl.DeviceIdType.MESH,
        ).wait_recv()
        return carry

    lax.fori_loop(1, count, finish, 0)
    local.wait()


def gather_req(piece):
    count = lax.axis_size("req")
    rows, width = piece.shape
    gathered = pl.pallas_call(
        functools.partial(fan_out_kernel, count),
        out_shape=jax.ShapeDtypeStruct((count, rows, width), piece.dtype),
        in_specs=[pl.BlockSpec(memory_space=pl.ANY)],
        out_specs=pl.BlockSpec(memory_space=pl.ANY),
        scratch_shapes=[
            pltpu.SemaphoreType.DMA((count - 1,)),
            pltpu.SemaphoreType.DMA((count - 1,)),
            pltpu.SemaphoreType.DMA,
        ],
        compiler_params=pltpu.CompilerParams(collective_id=0, has_side_effects=True),
    )(piece)
    return gathered.reshape(count * rows, width)


def body(hidden, lengths, key_cache, value_cache, norm_gain, w_query, w_key, w_value, w_out):
    rows_here = hidden.shape[1]
    kv_count = lax.axis_size("kv")
    appended = rows_here * kv_count
    slots = key_cache.shape[1]
    groups = H // KVH
    scale = HD ** (-0.5)
    length = lengths[0]
    q_cols = w_query.shape[1]
    k_cols = w_key.shape[1]
    v_cols = w_value.shape[1]
    heads_here = q_cols // HD
    kv_heads_here = k_cols // HD

    normed = rms_norm(hidden[0].astype(jnp.float32), norm_gain)
    normed_all = lax.all_gather(normed, "kv", axis=0, tiled=True)

    pieces = jnp.concatenate([w_query, w_key, w_value, w_out], axis=1)
    cols = gather_req(pieces)
    wq = cols[:, :q_cols]
    wk = cols[:, q_cols:q_cols + k_cols]
    wv = cols[:, q_cols + k_cols:q_cols + k_cols + v_cols]
    wo = cols[:, q_cols + k_cols + v_cols:]

    positions = (length + jnp.arange(appended, dtype=jnp.int32)).astype(jnp.float32)
    proj_q = jnp.dot(normed_all, wq, preferred_element_type=jnp.float32)
    proj_k = jnp.dot(normed_all, wk, preferred_element_type=jnp.float32)
    proj_v = jnp.dot(normed_all, wv, preferred_element_type=jnp.float32)
    queries = rotate(proj_q, positions).astype(jnp.bfloat16)
    keys_new = rotate(proj_k, positions).astype(jnp.bfloat16)
    values_new = proj_v.astype(jnp.bfloat16)

    new_keys = lax.all_to_all(keys_new, "kv", split_axis=0, concat_axis=1, tiled=True)
    new_values = lax.all_to_all(values_new, "kv", split_axis=0, concat_axis=1, tiled=True)

    keys_old = lax.all_to_all(key_cache[0], "kv", split_axis=1, concat_axis=0, tiled=True)
    values_old = lax.all_to_all(value_cache[0], "kv", split_axis=1, concat_axis=0, tiled=True)
    cache_slots = keys_old.shape[0]

    keys_all = jnp.concatenate([keys_old, keys_new], axis=0)
    values_all = jnp.concatenate([values_old, values_new], axis=0)
    key_count = keys_all.shape[0]
    query_index = jnp.arange(appended, dtype=jnp.int32)
    cache_live = jnp.arange(cache_slots, dtype=jnp.int32) < length
    visible = jnp.concatenate(
        [
            jnp.broadcast_to(cache_live[None, :], (appended, cache_slots)),
            query_index[None, :] <= query_index[:, None],
        ],
        axis=1,
    )
    query_heads = jnp.transpose(
        queries.reshape(appended, kv_heads_here, groups, HD), (1, 0, 2, 3)
    )
    key_heads = jnp.transpose(keys_all.reshape(key_count, kv_heads_here, HD), (1, 0, 2))
    value_heads = jnp.transpose(values_all.reshape(key_count, kv_heads_here, HD), (1, 0, 2))

    def attend(operands):
        query_block, key_block, value_block = operands
        score = (
            jnp.einsum("qgd,kd->gqk", query_block, key_block, preferred_element_type=jnp.float32)
            * scale
        )
        score = jnp.where(visible[None], score, masked_score)
        peak = jnp.max(score, axis=-1)
        weights = jnp.where(visible[None], jnp.exp(score - peak[..., None]), 0.0)
        total = jnp.sum(weights, axis=-1)
        context = jnp.einsum(
            "gqk,kd->qgd",
            weights.astype(jnp.bfloat16),
            value_block,
            preferred_element_type=jnp.float32,
        )
        return context / jnp.transpose(total)[:, :, None]

    contexts = lax.map(attend, (query_heads, key_heads, value_heads))
    context = (
        jnp.transpose(contexts, (1, 0, 2, 3)).reshape(appended, heads_here * HD).astype(jnp.bfloat16)
    )
    context_all = lax.all_gather(context, "kv", axis=1, tiled=True)
    attended_cols = jnp.dot(context_all, wo, preferred_element_type=jnp.float32).astype(jnp.bfloat16)
    attended = lax.all_to_all(attended_cols, "kv", split_axis=0, concat_axis=1, tiled=True)
    return (attended[None], new_keys[None], new_values[None])


def solution(mesh):
    return jax.shard_map(
        body,
        mesh=mesh,
        in_specs=(
            P("req", "kv", None),
            P("req"),
            P("req", "kv", None),
            P("req", "kv", None),
            P(),
            P("req", "kv"),
            P("req", "kv"),
            P("req", "kv"),
            P("req", "kv"),
        ),
        out_specs=(P("req", "kv", None), P("req", "kv", None), P("req", "kv", None)),
        check_vma=False,
    )
```

```python
import functools

import jax
import jax.numpy as jnp
from jax import lax
from jax.sharding import PartitionSpec as P
from jax.experimental import pallas as pl
from jax.experimental.pallas import tpu as pltpu

H = 16
KVH = 8
HD = 96


rope_base = 100000.0
masked_score = -1e30


def rms_norm(states, gain):
    mean_square = jnp.mean(states * states, axis=-1, keepdims=True)
    scaled = states * lax.rsqrt(mean_square + 1e-05) * gain.astype(jnp.float32)
    return scaled.astype(jnp.bfloat16)


def rotate(values, positions):
    count = values.shape[0]
    heads = values.shape[1] // HD
    half = HD // 2
    frequency = rope_base ** (-(jnp.arange(half, dtype=jnp.float32) * 2.0 / HD))
    angle = positions[:, None] * frequency[None, :]
    cosine = jnp.cos(angle)[:, None, :]
    sine = jnp.sin(angle)[:, None, :]
    shaped = values.reshape(count, heads, HD)
    first = shaped[..., :half]
    second = shaped[..., half:]
    turned = jnp.concatenate(
        [first * cosine - second * sine, second * cosine + first * sine], axis=-1
    )
    return turned.reshape(count, heads * HD)


Z_RUN = 8
Y_RUN = 2
MESH = pl.DeviceIdType.MESH


def remote(src, dst, send, recv, device):
    return pltpu.make_async_remote_copy(
        src_ref=src, dst_ref=dst, send_sem=send, recv_sem=recv,
        device_id=device, device_id_type=MESH,
    )


def plane_ring_kernel(planes, runs, src_ref, out_ref, s1_send, s1_recv, r_send, r_recv,
                      l_send, l_recv, local_sem):
    me = lax.axis_index("req")
    kv = lax.axis_index("kv")
    y_me = lax.rem(me, Y_RUN)
    z_me = lax.rem(me // Y_RUN, runs)
    x_me = me // (Y_RUN * runs)
    q_me = x_me * Y_RUN + y_me
    right_hops = runs // 2
    left_hops = runs - 1 - right_hops

    def plane_peer(q):
        return ((q // Y_RUN) * runs + z_me) * Y_RUN + lax.rem(q, Y_RUN)

    def ring_peer(z):
        return (x_me * runs + z) * Y_RUN + y_me

    z_right = lax.rem(z_me + 1, runs)
    z_left = lax.rem(z_me + runs - 1, runs)

    barrier = pltpu.get_barrier_semaphore()

    def greet(step, carry):
        q = lax.rem(q_me + step, planes)
        pl.semaphore_signal(barrier, inc=1, device_id=(plane_peer(q), kv), device_id_type=MESH)
        return carry

    lax.fori_loop(1, planes, greet, 0)
    pl.semaphore_signal(barrier, inc=1, device_id=(ring_peer(z_right), kv), device_id_type=MESH)
    pl.semaphore_signal(barrier, inc=1, device_id=(ring_peer(z_left), kv), device_id_type=MESH)
    pl.semaphore_wait(barrier, planes + 1)

    local = pltpu.make_async_copy(src_ref, out_ref.at[z_me, q_me], local_sem)
    local.start()

    def send(step, carry):
        q = lax.rem(q_me + step, planes)
        remote(src_ref, out_ref.at[z_me, q_me], s1_send.at[step - 1], s1_recv.at[step - 1],
               (plane_peer(q), kv)).start()
        return carry

    lax.fori_loop(1, planes, send, 0)

    def finish(step, carry):
        q = lax.rem(q_me + step, planes)
        source = lax.rem(q_me + planes - step, planes)
        remote(src_ref, out_ref.at[z_me, q_me], s1_send.at[step - 1], s1_recv.at[step - 1],
               (plane_peer(q), kv)).wait_send()
        remote(src_ref, out_ref.at[z_me, source], s1_send.at[step - 1], s1_recv.at[step - 1],
               (plane_peer(source), kv)).wait_recv()
        return carry

    lax.fori_loop(1, planes, finish, 0)
    local.wait()

    sent = []
    if right_hops > 0:
        c = remote(out_ref.at[z_me], out_ref.at[z_me], r_send.at[0], r_recv.at[0],
                   (ring_peer(z_right), kv))
        c.start()
        sent.append(c)
    if left_hops > 0:
        c = remote(out_ref.at[z_me], out_ref.at[z_me], l_send.at[0], l_recv.at[0],
                   (ring_peer(z_left), kv))
        c.start()
        sent.append(c)
    for k in range(1, max(right_hops, left_hops) + 1):
        if k <= right_hops:
            z_from = lax.rem(z_me + runs - k, runs)
            remote(out_ref.at[z_from], out_ref.at[z_from], r_send.at[k - 1], r_recv.at[k - 1],
                   (ring_peer(z_right), kv)).wait_recv()
            if k < right_hops:
                c = remote(out_ref.at[z_from], out_ref.at[z_from], r_send.at[k], r_recv.at[k],
                           (ring_peer(z_right), kv))
                c.start()
                sent.append(c)
        if k <= left_hops:
            z_from = lax.rem(z_me + k, runs)
            remote(out_ref.at[z_from], out_ref.at[z_from], l_send.at[k - 1], l_recv.at[k - 1],
                   (ring_peer(z_left), kv)).wait_recv()
            if k < left_hops:
                c = remote(out_ref.at[z_from], out_ref.at[z_from], l_send.at[k], l_recv.at[k],
                           (ring_peer(z_left), kv))
                c.start()
                sent.append(c)
    for c in sent:
        c.wait_send()


def gather_req(piece):
    count = lax.axis_size("req")
    runs = min(Z_RUN, count // Y_RUN)
    planes = count // runs
    rows, width = piece.shape
    hops = max(runs - 1, 1)
    gathered = pl.pallas_call(
        functools.partial(plane_ring_kernel, planes, runs),
        out_shape=jax.ShapeDtypeStruct((runs, planes, rows, width), piece.dtype),
        in_specs=[pl.BlockSpec(memory_space=pl.ANY)],
        out_specs=pl.BlockSpec(memory_space=pl.ANY),
        scratch_shapes=[
            pltpu.SemaphoreType.DMA((planes - 1,)),
            pltpu.SemaphoreType.DMA((planes - 1,)),
            pltpu.SemaphoreType.DMA((hops,)),
            pltpu.SemaphoreType.DMA((hops,)),
            pltpu.SemaphoreType.DMA((hops,)),
            pltpu.SemaphoreType.DMA((hops,)),
            pltpu.SemaphoreType.DMA,
        ],
        compiler_params=pltpu.CompilerParams(collective_id=0, has_side_effects=True),
    )(piece)
    x_count = planes // Y_RUN
    ordered = jnp.transpose(
        gathered.reshape(runs, x_count, Y_RUN, rows, width), (1, 0, 2, 3, 4)
    )
    return ordered.reshape(count * rows, width)


def body(hidden, lengths, key_cache, value_cache, norm_gain, w_query, w_key, w_value, w_out):
    rows_here = hidden.shape[1]
    kv_count = lax.axis_size("kv")
    appended = rows_here * kv_count
    slots = key_cache.shape[1]
    groups = H // KVH
    scale = HD ** (-0.5)
    length = lengths[0]
    q_cols = w_query.shape[1]
    k_cols = w_key.shape[1]
    v_cols = w_value.shape[1]
    heads_here = q_cols // HD
    kv_heads_here = k_cols // HD

    normed = rms_norm(hidden[0].astype(jnp.float32), norm_gain)
    normed_all = lax.all_gather(normed, "kv", axis=0, tiled=True)

    pieces = jnp.concatenate([w_query, w_key, w_value, w_out], axis=1)
    cols = gather_req(pieces)
    wq = cols[:, :q_cols]
    wk = cols[:, q_cols:q_cols + k_cols]
    wv = cols[:, q_cols + k_cols:q_cols + k_cols + v_cols]
    wo = cols[:, q_cols + k_cols + v_cols:]

    positions = (length + jnp.arange(appended, dtype=jnp.int32)).astype(jnp.float32)
    proj_q = jnp.dot(normed_all, wq, preferred_element_type=jnp.float32)
    proj_k = jnp.dot(normed_all, wk, preferred_element_type=jnp.float32)
    proj_v = jnp.dot(normed_all, wv, preferred_element_type=jnp.float32)
    queries = rotate(proj_q, positions).astype(jnp.bfloat16)
    keys_new = rotate(proj_k, positions).astype(jnp.bfloat16)
    values_new = proj_v.astype(jnp.bfloat16)

    new_keys = lax.all_to_all(keys_new, "kv", split_axis=0, concat_axis=1, tiled=True)
    new_values = lax.all_to_all(values_new, "kv", split_axis=0, concat_axis=1, tiled=True)

    keys_old = lax.all_to_all(key_cache[0], "kv", split_axis=1, concat_axis=0, tiled=True)
    values_old = lax.all_to_all(value_cache[0], "kv", split_axis=1, concat_axis=0, tiled=True)
    cache_slots = keys_old.shape[0]

    keys_all = jnp.concatenate([keys_old, keys_new], axis=0)
    values_all = jnp.concatenate([values_old, values_new], axis=0)
    key_count = keys_all.shape[0]
    query_index = jnp.arange(appended, dtype=jnp.int32)
    cache_live = jnp.arange(cache_slots, dtype=jnp.int32) < length
    visible = jnp.concatenate(
        [
            jnp.broadcast_to(cache_live[None, :], (appended, cache_slots)),
            query_index[None, :] <= query_index[:, None],
        ],
        axis=1,
    )
    query_heads = jnp.transpose(
        queries.reshape(appended, kv_heads_here, groups, HD), (1, 0, 2, 3)
    )
    key_heads = jnp.transpose(keys_all.reshape(key_count, kv_heads_here, HD), (1, 0, 2))
    value_heads = jnp.transpose(values_all.reshape(key_count, kv_heads_here, HD), (1, 0, 2))

    def attend(operands):
        query_block, key_block, value_block = operands
        score = (
            jnp.einsum("qgd,kd->gqk", query_block, key_block, preferred_element_type=jnp.float32)
            * scale
        )
        score = jnp.where(visible[None], score, masked_score)
        peak = jnp.max(score, axis=-1)
        weights = jnp.where(visible[None], jnp.exp(score - peak[..., None]), 0.0)
        total = jnp.sum(weights, axis=-1)
        context = jnp.einsum(
            "gqk,kd->qgd",
            weights.astype(jnp.bfloat16),
            value_block,
            preferred_element_type=jnp.float32,
        )
        return context / jnp.transpose(total)[:, :, None]

    contexts = lax.map(attend, (query_heads, key_heads, value_heads))
    context = (
        jnp.transpose(contexts, (1, 0, 2, 3)).reshape(appended, heads_here * HD).astype(jnp.bfloat16)
    )
    context_all = lax.all_gather(context, "kv", axis=1, tiled=True)
    attended_cols = jnp.dot(context_all, wo, preferred_element_type=jnp.float32).astype(jnp.bfloat16)
    attended = lax.all_to_all(attended_cols, "kv", split_axis=0, concat_axis=1, tiled=True)
    return (attended[None], new_keys[None], new_values[None])


def solution(mesh):
    return jax.shard_map(
        body,
        mesh=mesh,
        in_specs=(
            P("req", "kv", None),
            P("req"),
            P("req", "kv", None),
            P("req", "kv", None),
            P(),
            P("req", "kv"),
            P("req", "kv"),
            P("req", "kv"),
            P("req", "kv"),
        ),
        out_specs=(P("req", "kv", None), P("req", "kv", None), P("req", "kv", None)),
        check_vma=False,
    )
```

```python
import functools

import jax
import jax.numpy as jnp
from jax import lax
from jax.sharding import PartitionSpec as P
from jax.experimental import pallas as pl
from jax.experimental.pallas import tpu as pltpu

H = 16
KVH = 8
HD = 96


rope_base = 100000.0
masked_score = -1e30


def rms_norm(states, gain):
    mean_square = jnp.mean(states * states, axis=-1, keepdims=True)
    scaled = states * lax.rsqrt(mean_square + 1e-05) * gain.astype(jnp.float32)
    return scaled.astype(jnp.bfloat16)


def rotate(values, positions):
    count = values.shape[0]
    heads = values.shape[1] // HD
    half = HD // 2
    frequency = rope_base ** (-(jnp.arange(half, dtype=jnp.float32) * 2.0 / HD))
    angle = positions[:, None] * frequency[None, :]
    cosine = jnp.cos(angle)[:, None, :]
    sine = jnp.sin(angle)[:, None, :]
    shaped = values.reshape(count, heads, HD)
    first = shaped[..., :half]
    second = shaped[..., half:]
    turned = jnp.concatenate(
        [first * cosine - second * sine, second * cosine + first * sine], axis=-1
    )
    return turned.reshape(count, heads * HD)


Z_RUN = 8
Y_RUN = 2
MESH = pl.DeviceIdType.MESH


def remote(src, dst, send, recv, device):
    return pltpu.make_async_remote_copy(
        src_ref=src, dst_ref=dst, send_sem=send, recv_sem=recv,
        device_id=device, device_id_type=MESH,
    )


def plane_ring_kernel(planes, runs, src_ref, out_ref, s1_send, s1_recv, r_send, r_recv,
                      l_send, l_recv, local_sem):
    me = lax.axis_index("req")
    kv = lax.axis_index("kv")
    y_me = lax.rem(me, Y_RUN)
    z_me = lax.rem(me // Y_RUN, runs)
    x_me = me // (Y_RUN * runs)
    q_me = x_me * Y_RUN + y_me
    right_hops = runs // 2
    left_hops = runs - 1 - right_hops

    def plane_peer(q):
        return ((q // Y_RUN) * runs + z_me) * Y_RUN + lax.rem(q, Y_RUN)

    def ring_peer(z):
        return (x_me * runs + z) * Y_RUN + y_me

    z_right = lax.rem(z_me + 1, runs)
    z_left = lax.rem(z_me + runs - 1, runs)

    barrier = pltpu.get_barrier_semaphore()

    def greet(step, carry):
        q = lax.rem(q_me + step, planes)
        pl.semaphore_signal(barrier, inc=1, device_id=(plane_peer(q), kv), device_id_type=MESH)
        return carry

    lax.fori_loop(1, planes, greet, 0)
    pl.semaphore_signal(barrier, inc=1, device_id=(ring_peer(z_right), kv), device_id_type=MESH)
    pl.semaphore_signal(barrier, inc=1, device_id=(ring_peer(z_left), kv), device_id_type=MESH)
    pl.semaphore_wait(barrier, planes + 1)

    local = pltpu.make_async_copy(src_ref, out_ref.at[z_me, q_me], local_sem)
    local.start()

    def send(step, carry):
        q = lax.rem(q_me + step, planes)
        remote(src_ref, out_ref.at[z_me, q_me], s1_send.at[step - 1], s1_recv.at[step - 1],
               (plane_peer(q), kv)).start()
        return carry

    lax.fori_loop(1, planes, send, 0)

    def finish(step, carry):
        q = lax.rem(q_me + step, planes)
        source = lax.rem(q_me + planes - step, planes)
        remote(src_ref, out_ref.at[z_me, q_me], s1_send.at[step - 1], s1_recv.at[step - 1],
               (plane_peer(q), kv)).wait_send()
        remote(src_ref, out_ref.at[z_me, source], s1_send.at[step - 1], s1_recv.at[step - 1],
               (plane_peer(source), kv)).wait_recv()
        return carry

    lax.fori_loop(1, planes, finish, 0)
    local.wait()

    sent = []
    if right_hops > 0:
        c = remote(out_ref.at[z_me], out_ref.at[z_me], r_send.at[0], r_recv.at[0],
                   (ring_peer(z_right), kv))
        c.start()
        sent.append(c)
    if left_hops > 0:
        c = remote(out_ref.at[z_me], out_ref.at[z_me], l_send.at[0], l_recv.at[0],
                   (ring_peer(z_left), kv))
        c.start()
        sent.append(c)
    for k in range(1, max(right_hops, left_hops) + 1):
        if k <= right_hops:
            z_from = lax.rem(z_me + runs - k, runs)
            remote(out_ref.at[z_from], out_ref.at[z_from], r_send.at[k - 1], r_recv.at[k - 1],
                   (ring_peer(z_right), kv)).wait_recv()
            if k < right_hops:
                c = remote(out_ref.at[z_from], out_ref.at[z_from], r_send.at[k], r_recv.at[k],
                           (ring_peer(z_right), kv))
                c.start()
                sent.append(c)
        if k <= left_hops:
            z_from = lax.rem(z_me + k, runs)
            remote(out_ref.at[z_from], out_ref.at[z_from], l_send.at[k - 1], l_recv.at[k - 1],
                   (ring_peer(z_left), kv)).wait_recv()
            if k < left_hops:
                c = remote(out_ref.at[z_from], out_ref.at[z_from], l_send.at[k], l_recv.at[k],
                           (ring_peer(z_left), kv))
                c.start()
                sent.append(c)
    for c in sent:
        c.wait_send()


def gather_req(piece):
    count = lax.axis_size("req")
    runs = min(Z_RUN, count // Y_RUN)
    planes = count // runs
    rows, width = piece.shape
    hops = max(runs - 1, 1)
    gathered = pl.pallas_call(
        functools.partial(plane_ring_kernel, planes, runs),
        out_shape=jax.ShapeDtypeStruct((runs, planes, rows, width), piece.dtype),
        in_specs=[pl.BlockSpec(memory_space=pl.ANY)],
        out_specs=pl.BlockSpec(memory_space=pl.ANY),
        scratch_shapes=[
            pltpu.SemaphoreType.DMA((planes - 1,)),
            pltpu.SemaphoreType.DMA((planes - 1,)),
            pltpu.SemaphoreType.DMA((hops,)),
            pltpu.SemaphoreType.DMA((hops,)),
            pltpu.SemaphoreType.DMA((hops,)),
            pltpu.SemaphoreType.DMA((hops,)),
            pltpu.SemaphoreType.DMA,
        ],
        compiler_params=pltpu.CompilerParams(collective_id=0, has_side_effects=True),
    )(piece)
    x_count = planes // Y_RUN
    ordered = jnp.transpose(
        gathered.reshape(runs, x_count, Y_RUN, rows, width), (1, 0, 2, 3, 4)
    )
    return ordered.reshape(count * rows, width)


def body(hidden, lengths, key_cache, value_cache, norm_gain, w_query, w_key, w_value, w_out):
    rows_here = hidden.shape[1]
    kv_count = lax.axis_size("kv")
    appended = rows_here * kv_count
    slots = key_cache.shape[1]
    groups = H // KVH
    scale = HD ** (-0.5)
    length = lengths[0]
    q_cols = w_query.shape[1]
    k_cols = w_key.shape[1]
    v_cols = w_value.shape[1]
    heads_here = q_cols // HD
    kv_heads_here = k_cols // HD

    normed = rms_norm(hidden[0].astype(jnp.float32), norm_gain)
    normed_all = lax.all_gather(normed, "kv", axis=0, tiled=True)

    pieces = jnp.concatenate([w_query, w_key, w_value, w_out], axis=1)
    cols = gather_req(pieces)
    wq = cols[:, :q_cols]
    wk = cols[:, q_cols:q_cols + k_cols]
    wv = cols[:, q_cols + k_cols:q_cols + k_cols + v_cols]
    wo = cols[:, q_cols + k_cols + v_cols:]

    wo_full = lax.all_gather(wo, "kv", axis=1, tiled=True)

    positions = (length + jnp.arange(appended, dtype=jnp.int32)).astype(jnp.float32)
    proj_q = jnp.dot(normed_all, wq, preferred_element_type=jnp.float32)
    proj_k = jnp.dot(normed_all, wk, preferred_element_type=jnp.float32)
    proj_v = jnp.dot(normed_all, wv, preferred_element_type=jnp.float32)
    queries = rotate(proj_q, positions).astype(jnp.bfloat16)
    keys_new = rotate(proj_k, positions).astype(jnp.bfloat16)
    values_new = proj_v.astype(jnp.bfloat16)

    new_keys = lax.all_to_all(keys_new, "kv", split_axis=0, concat_axis=1, tiled=True)
    new_values = lax.all_to_all(values_new, "kv", split_axis=0, concat_axis=1, tiled=True)

    keys_old = lax.all_to_all(key_cache[0], "kv", split_axis=1, concat_axis=0, tiled=True)
    values_old = lax.all_to_all(value_cache[0], "kv", split_axis=1, concat_axis=0, tiled=True)
    cache_slots = keys_old.shape[0]

    keys_all = jnp.concatenate([keys_old, keys_new], axis=0)
    values_all = jnp.concatenate([values_old, values_new], axis=0)
    key_count = keys_all.shape[0]
    query_index = jnp.arange(appended, dtype=jnp.int32)
    cache_live = jnp.arange(cache_slots, dtype=jnp.int32) < length
    visible = jnp.concatenate(
        [
            jnp.broadcast_to(cache_live[None, :], (appended, cache_slots)),
            query_index[None, :] <= query_index[:, None],
        ],
        axis=1,
    )
    query_heads = jnp.transpose(
        queries.reshape(appended, kv_heads_here, groups, HD), (1, 0, 2, 3)
    )
    key_heads = jnp.transpose(keys_all.reshape(key_count, kv_heads_here, HD), (1, 0, 2))
    value_heads = jnp.transpose(values_all.reshape(key_count, kv_heads_here, HD), (1, 0, 2))

    def attend(operands):
        query_block, key_block, value_block = operands
        score = (
            jnp.einsum("qgd,kd->gqk", query_block, key_block, preferred_element_type=jnp.float32)
            * scale
        )
        score = jnp.where(visible[None], score, masked_score)
        peak = jnp.max(score, axis=-1)
        weights = jnp.where(visible[None], jnp.exp(score - peak[..., None]), 0.0)
        total = jnp.sum(weights, axis=-1)
        context = jnp.einsum(
            "gqk,kd->qgd",
            weights.astype(jnp.bfloat16),
            value_block,
            preferred_element_type=jnp.float32,
        )
        return context / jnp.transpose(total)[:, :, None]

    contexts = lax.map(attend, (query_heads, key_heads, value_heads))
    context = (
        jnp.transpose(contexts, (1, 0, 2, 3)).reshape(appended, heads_here * HD).astype(jnp.bfloat16)
    )
    context_rows = lax.all_to_all(context, "kv", split_axis=0, concat_axis=1, tiled=True)
    attended = jnp.dot(context_rows, wo_full, preferred_element_type=jnp.float32).astype(jnp.bfloat16)
    return (attended[None], new_keys[None], new_values[None])


def solution(mesh):
    return jax.shard_map(
        body,
        mesh=mesh,
        in_specs=(
            P("req", "kv", None),
            P("req"),
            P("req", "kv", None),
            P("req", "kv", None),
            P(),
            P("req", "kv"),
            P("req", "kv"),
            P("req", "kv"),
            P("req", "kv"),
        ),
        out_specs=(P("req", "kv", None), P("req", "kv", None), P("req", "kv", None)),
        check_vma=False,
    )
```

```python
import functools

import jax
import jax.numpy as jnp
from jax import lax
from jax.sharding import PartitionSpec as P
from jax.experimental import pallas as pl
from jax.experimental.pallas import tpu as pltpu

H = 16
KVH = 8
HD = 96


rope_base = 100000.0
masked_score = -1e30


def rms_norm(states, gain):
    mean_square = jnp.mean(states * states, axis=-1, keepdims=True)
    scaled = states * lax.rsqrt(mean_square + 1e-05) * gain.astype(jnp.float32)
    return scaled.astype(jnp.bfloat16)


def rotate(values, positions):
    count = values.shape[0]
    heads = values.shape[1] // HD
    half = HD // 2
    frequency = rope_base ** (-(jnp.arange(half, dtype=jnp.float32) * 2.0 / HD))
    angle = positions[:, None] * frequency[None, :]
    cosine = jnp.cos(angle)[:, None, :]
    sine = jnp.sin(angle)[:, None, :]
    shaped = values.reshape(count, heads, HD)
    first = shaped[..., :half]
    second = shaped[..., half:]
    turned = jnp.concatenate(
        [first * cosine - second * sine, second * cosine + first * sine], axis=-1
    )
    return turned.reshape(count, heads * HD)


Z_RUN = 8
Y_RUN = 2
MESH = pl.DeviceIdType.MESH


def remote(src, dst, send, recv, device):
    return pltpu.make_async_remote_copy(
        src_ref=src, dst_ref=dst, send_sem=send, recv_sem=recv,
        device_id=device, device_id_type=MESH,
    )


def plane_ring_kernel(planes, runs, src_ref, out_ref, s1_send, s1_recv, r_send, r_recv,
                      l_send, l_recv, local_sem):
    me = lax.axis_index("req")
    kv = lax.axis_index("kv")
    y_me = lax.rem(me, Y_RUN)
    z_me = lax.rem(me // Y_RUN, runs)
    x_me = me // (Y_RUN * runs)
    q_me = x_me * Y_RUN + y_me
    right_hops = runs // 2
    left_hops = runs - 1 - right_hops

    def plane_peer(q):
        return ((q // Y_RUN) * runs + z_me) * Y_RUN + lax.rem(q, Y_RUN)

    def ring_peer(z):
        return (x_me * runs + z) * Y_RUN + y_me

    z_right = lax.rem(z_me + 1, runs)
    z_left = lax.rem(z_me + runs - 1, runs)

    barrier = pltpu.get_barrier_semaphore()

    def greet(step, carry):
        q = lax.rem(q_me + step, planes)
        pl.semaphore_signal(barrier, inc=1, device_id=(plane_peer(q), kv), device_id_type=MESH)
        return carry

    lax.fori_loop(1, planes, greet, 0)
    pl.semaphore_signal(barrier, inc=1, device_id=(ring_peer(z_right), kv), device_id_type=MESH)
    pl.semaphore_signal(barrier, inc=1, device_id=(ring_peer(z_left), kv), device_id_type=MESH)
    pl.semaphore_wait(barrier, planes + 1)

    local = pltpu.make_async_copy(src_ref, out_ref.at[z_me, q_me], local_sem)
    local.start()

    def send(step, carry):
        q = lax.rem(q_me + step, planes)
        remote(src_ref, out_ref.at[z_me, q_me], s1_send.at[step - 1], s1_recv.at[step - 1],
               (plane_peer(q), kv)).start()
        return carry

    lax.fori_loop(1, planes, send, 0)

    def finish(step, carry):
        q = lax.rem(q_me + step, planes)
        source = lax.rem(q_me + planes - step, planes)
        remote(src_ref, out_ref.at[z_me, q_me], s1_send.at[step - 1], s1_recv.at[step - 1],
               (plane_peer(q), kv)).wait_send()
        remote(src_ref, out_ref.at[z_me, source], s1_send.at[step - 1], s1_recv.at[step - 1],
               (plane_peer(source), kv)).wait_recv()
        return carry

    lax.fori_loop(1, planes, finish, 0)
    local.wait()

    sent = []
    if right_hops > 0:
        c = remote(out_ref.at[z_me], out_ref.at[z_me], r_send.at[0], r_recv.at[0],
                   (ring_peer(z_right), kv))
        c.start()
        sent.append(c)
    if left_hops > 0:
        c = remote(out_ref.at[z_me], out_ref.at[z_me], l_send.at[0], l_recv.at[0],
                   (ring_peer(z_left), kv))
        c.start()
        sent.append(c)
    for k in range(1, max(right_hops, left_hops) + 1):
        if k <= right_hops:
            z_from = lax.rem(z_me + runs - k, runs)
            remote(out_ref.at[z_from], out_ref.at[z_from], r_send.at[k - 1], r_recv.at[k - 1],
                   (ring_peer(z_right), kv)).wait_recv()
            if k < right_hops:
                c = remote(out_ref.at[z_from], out_ref.at[z_from], r_send.at[k], r_recv.at[k],
                           (ring_peer(z_right), kv))
                c.start()
                sent.append(c)
        if k <= left_hops:
            z_from = lax.rem(z_me + k, runs)
            remote(out_ref.at[z_from], out_ref.at[z_from], l_send.at[k - 1], l_recv.at[k - 1],
                   (ring_peer(z_left), kv)).wait_recv()
            if k < left_hops:
                c = remote(out_ref.at[z_from], out_ref.at[z_from], l_send.at[k], l_recv.at[k],
                           (ring_peer(z_left), kv))
                c.start()
                sent.append(c)
    for c in sent:
        c.wait_send()


def gather_req(piece):
    count = lax.axis_size("req")
    runs = min(Z_RUN, count // Y_RUN)
    planes = count // runs
    rows, width = piece.shape
    hops = max(runs - 1, 1)
    gathered = pl.pallas_call(
        functools.partial(plane_ring_kernel, planes, runs),
        out_shape=jax.ShapeDtypeStruct((runs, planes, rows, width), piece.dtype),
        in_specs=[pl.BlockSpec(memory_space=pl.ANY)],
        out_specs=pl.BlockSpec(memory_space=pl.ANY),
        scratch_shapes=[
            pltpu.SemaphoreType.DMA((planes - 1,)),
            pltpu.SemaphoreType.DMA((planes - 1,)),
            pltpu.SemaphoreType.DMA((hops,)),
            pltpu.SemaphoreType.DMA((hops,)),
            pltpu.SemaphoreType.DMA((hops,)),
            pltpu.SemaphoreType.DMA((hops,)),
            pltpu.SemaphoreType.DMA,
        ],
        compiler_params=pltpu.CompilerParams(collective_id=0, has_side_effects=True),
    )(piece)
    x_count = planes // Y_RUN
    ordered = jnp.transpose(
        gathered.reshape(runs, x_count, Y_RUN, rows, width), (1, 0, 2, 3, 4)
    )
    return ordered.reshape(count * rows, width)


BLOCK_Q = 512
BLOCK_K = 512


def flash_kernel(tokens, scale, len_ref, q_ref, kc_ref, vc_ref, kn_ref, vn_ref, o_ref):
    block_q = q_ref.shape[1]
    block_k = BLOCK_K
    width = q_ref.shape[2]
    i = pl.program_id(1)
    length = len_ref[0]
    first = lax.rem(i * block_q, tokens)
    q = q_ref[0]
    query_index = first + lax.broadcasted_iota(jnp.int32, (block_q, block_k), 0)
    key_offset = lax.broadcasted_iota(jnp.int32, (block_q, block_k), 1)

    def step(keys, values, visible, carry):
        peak, total, acc = carry
        score = lax.dot_general(
            q, keys, (((1,), (1,)), ((), ())), preferred_element_type=jnp.float32
        ) * scale
        score = jnp.where(visible, score, masked_score)
        new_peak = jnp.maximum(peak, jnp.max(score, axis=1, keepdims=True))
        alpha = jnp.exp(peak - new_peak)
        weights = jnp.where(visible, jnp.exp(score - new_peak), 0.0)
        total = alpha * total + jnp.sum(weights, axis=1, keepdims=True)
        acc = alpha * acc + jnp.dot(
            weights.astype(jnp.bfloat16), values, preferred_element_type=jnp.float32
        )
        return new_peak, total, acc

    def cache_step(block, carry):
        start = pl.multiple_of(block * block_k, block_k)
        keys = kc_ref[0, pl.ds(start, block_k), :]
        values = vc_ref[0, pl.ds(start, block_k), :]
        visible = start + key_offset < length
        return step(keys, values, visible, carry)

    def new_step(block, carry):
        start = pl.multiple_of(block * block_k, block_k)
        keys = kn_ref[0, pl.ds(start, block_k), :]
        values = vn_ref[0, pl.ds(start, block_k), :]
        visible = start + key_offset <= query_index
        return step(keys, values, visible, carry)

    carry = (
        jnp.full((block_q, 1), -jnp.inf, jnp.float32),
        jnp.zeros((block_q, 1), jnp.float32),
        jnp.zeros((block_q, width), jnp.float32),
    )
    live_blocks = (length + block_k - 1) // block_k
    carry = lax.fori_loop(0, live_blocks, cache_step, carry)
    new_blocks = (first + block_q - 1) // block_k + 1
    peak, total, acc = lax.fori_loop(0, new_blocks, new_step, carry)
    o_ref[0] = (acc / total).astype(o_ref.dtype)


def flash_attention(lengths, queries, keys_old, values_old, keys_new, values_new, tokens, scale):
    heads, rows, width = queries.shape
    slots = keys_old.shape[1]
    block_q = min(BLOCK_Q, tokens)
    grid = (heads, rows // block_q)
    whole_cache = pl.BlockSpec((1, slots, width), lambda c, i, n: (c, 0, 0))
    whole_new = pl.BlockSpec((1, tokens, width), lambda c, i, n: (c, 0, 0))
    return pl.pallas_call(
        functools.partial(flash_kernel, tokens, scale),
        out_shape=jax.ShapeDtypeStruct((heads, rows, width), jnp.bfloat16),
        grid_spec=pltpu.PrefetchScalarGridSpec(
            num_scalar_prefetch=1,
            grid=grid,
            in_specs=[
                pl.BlockSpec((1, block_q, width), lambda c, i, n: (c, i, 0)),
                whole_cache, whole_cache, whole_new, whole_new,
            ],
            out_specs=pl.BlockSpec((1, block_q, width), lambda c, i, n: (c, i, 0)),
        ),
        cost_estimate=pl.CostEstimate(
            flops=4 * heads * rows * (slots + tokens) * width,
            transcendentals=heads * rows * (slots + tokens),
            bytes_accessed=2 * width * heads * (2 * rows + 2 * slots + 2 * tokens),
        ),
    )(lengths, queries, keys_old, values_old, keys_new, values_new)


def body(hidden, lengths, key_cache, value_cache, norm_gain, w_query, w_key, w_value, w_out):
    rows_here = hidden.shape[1]
    kv_count = lax.axis_size("kv")
    appended = rows_here * kv_count
    slots = key_cache.shape[1]
    groups = H // KVH
    scale = HD ** (-0.5)
    length = lengths[0]
    q_cols = w_query.shape[1]
    k_cols = w_key.shape[1]
    v_cols = w_value.shape[1]
    heads_here = q_cols // HD
    kv_heads_here = k_cols // HD

    normed = rms_norm(hidden[0].astype(jnp.float32), norm_gain)
    normed_all = lax.all_gather(normed, "kv", axis=0, tiled=True)

    pieces = jnp.concatenate([w_query, w_key, w_value, w_out], axis=1)
    cols = gather_req(pieces)
    wq = cols[:, :q_cols]
    wk = cols[:, q_cols:q_cols + k_cols]
    wv = cols[:, q_cols + k_cols:q_cols + k_cols + v_cols]
    wo = cols[:, q_cols + k_cols + v_cols:]

    wo_full = lax.all_gather(wo, "kv", axis=1, tiled=True)

    positions = (length + jnp.arange(appended, dtype=jnp.int32)).astype(jnp.float32)
    proj_q = jnp.dot(normed_all, wq, preferred_element_type=jnp.float32)
    proj_k = jnp.dot(normed_all, wk, preferred_element_type=jnp.float32)
    proj_v = jnp.dot(normed_all, wv, preferred_element_type=jnp.float32)
    queries = rotate(proj_q, positions).astype(jnp.bfloat16)
    keys_new = rotate(proj_k, positions).astype(jnp.bfloat16)
    values_new = proj_v.astype(jnp.bfloat16)

    new_keys = lax.all_to_all(keys_new, "kv", split_axis=0, concat_axis=1, tiled=True)
    new_values = lax.all_to_all(values_new, "kv", split_axis=0, concat_axis=1, tiled=True)

    keys_old = lax.all_to_all(key_cache[0], "kv", split_axis=1, concat_axis=0, tiled=True)
    values_old = lax.all_to_all(value_cache[0], "kv", split_axis=1, concat_axis=0, tiled=True)
    cache_slots = keys_old.shape[0]

    def by_head(values):
        count = values.shape[0]
        return jnp.transpose(values.reshape(count, kv_heads_here, HD), (1, 0, 2))

    query_heads = jnp.transpose(
        queries.reshape(appended, kv_heads_here, groups, HD), (1, 2, 0, 3)
    ).reshape(kv_heads_here, groups * appended, HD)
    contexts = flash_attention(
        lengths, query_heads, by_head(keys_old), by_head(values_old),
        by_head(keys_new), by_head(values_new), appended, scale,
    )
    context = jnp.transpose(
        contexts.reshape(kv_heads_here, groups, appended, HD), (2, 0, 1, 3)
    ).reshape(appended, heads_here * HD)
    context_rows = lax.all_to_all(context, "kv", split_axis=0, concat_axis=1, tiled=True)
    attended = jnp.dot(context_rows, wo_full, preferred_element_type=jnp.float32).astype(jnp.bfloat16)
    return (attended[None], new_keys[None], new_values[None])


def solution(mesh):
    return jax.shard_map(
        body,
        mesh=mesh,
        in_specs=(
            P("req", "kv", None),
            P("req"),
            P("req", "kv", None),
            P("req", "kv", None),
            P(),
            P("req", "kv"),
            P("req", "kv"),
            P("req", "kv"),
            P("req", "kv"),
        ),
        out_specs=(P("req", "kv", None), P("req", "kv", None), P("req", "kv", None)),
        check_vma=False,
    )
```

```python
import functools

import jax
import jax.numpy as jnp
from jax import lax
from jax.sharding import PartitionSpec as P
from jax.experimental import pallas as pl
from jax.experimental.pallas import tpu as pltpu

H = 16
KVH = 8
HD = 96


rope_base = 100000.0
masked_score = -1e30


def rms_norm(states, gain):
    mean_square = jnp.mean(states * states, axis=-1, keepdims=True)
    scaled = states * lax.rsqrt(mean_square + 1e-05) * gain.astype(jnp.float32)
    return scaled.astype(jnp.bfloat16)


def rotate(values, positions):
    count = values.shape[0]
    heads = values.shape[1] // HD
    half = HD // 2
    frequency = rope_base ** (-(jnp.arange(half, dtype=jnp.float32) * 2.0 / HD))
    angle = positions[:, None] * frequency[None, :]
    cosine = jnp.cos(angle)[:, None, :]
    sine = jnp.sin(angle)[:, None, :]
    shaped = values.reshape(count, heads, HD)
    first = shaped[..., :half]
    second = shaped[..., half:]
    turned = jnp.concatenate(
        [first * cosine - second * sine, second * cosine + first * sine], axis=-1
    )
    return turned.reshape(count, heads * HD)


Z_RUN = 8
Y_RUN = 2
MESH = pl.DeviceIdType.MESH


def remote(src, dst, send, recv, device):
    return pltpu.make_async_remote_copy(
        src_ref=src, dst_ref=dst, send_sem=send, recv_sem=recv,
        device_id=device, device_id_type=MESH,
    )


def plane_ring_kernel(planes, runs, src_ref, kc_ref, vc_ref, out_ref, kc_out, vc_out, s1_send,
                      s1_recv, r_send, r_recv, l_send, l_recv, local_sem, kv_send, kv_recv, kv_local):
    me = lax.axis_index("req")
    kv = lax.axis_index("kv")
    y_me = lax.rem(me, Y_RUN)
    z_me = lax.rem(me // Y_RUN, runs)
    x_me = me // (Y_RUN * runs)
    q_me = x_me * Y_RUN + y_me
    right_hops = runs // 2
    left_hops = runs - 1 - right_hops

    def plane_peer(q):
        return ((q // Y_RUN) * runs + z_me) * Y_RUN + lax.rem(q, Y_RUN)

    def ring_peer(z):
        return (x_me * runs + z) * Y_RUN + y_me

    z_right = lax.rem(z_me + 1, runs)
    z_left = lax.rem(z_me + runs - 1, runs)

    barrier = pltpu.get_barrier_semaphore()

    def greet(step, carry):
        q = lax.rem(q_me + step, planes)
        pl.semaphore_signal(barrier, inc=1, device_id=(plane_peer(q), kv), device_id_type=MESH)
        return carry

    lax.fori_loop(1, planes, greet, 0)
    pl.semaphore_signal(barrier, inc=1, device_id=(ring_peer(z_right), kv), device_id_type=MESH)
    pl.semaphore_signal(barrier, inc=1, device_id=(ring_peer(z_left), kv), device_id_type=MESH)
    kv_count = lax.axis_size("kv")

    def greet_kv(step, carry):
        peer = lax.rem(kv + step, kv_count)
        pl.semaphore_signal(barrier, inc=1, device_id=(me, peer), device_id_type=MESH)
        return carry

    lax.fori_loop(1, kv_count, greet_kv, 0)
    pl.semaphore_wait(barrier, planes + 1 + kv_count - 1)

    local = pltpu.make_async_copy(src_ref, out_ref.at[z_me, q_me], local_sem)
    local.start()
    caches = ((kc_ref, kc_out), (vc_ref, vc_out))
    local_cache = []
    for which, (cache_src, cache_dst) in enumerate(caches):
        c = pltpu.make_async_copy(cache_src.at[kv], cache_dst.at[kv], kv_local.at[which])
        c.start()
        local_cache.append(c)

    def send_kv(step, carry):
        peer = lax.rem(kv + step, kv_count)
        for which, (cache_src, cache_dst) in enumerate(caches):
            remote(cache_src.at[peer], cache_dst.at[kv], kv_send.at[which, step - 1],
                   kv_recv.at[which, step - 1], (me, peer)).start()
        return carry

    lax.fori_loop(1, kv_count, send_kv, 0)

    def send(step, carry):
        q = lax.rem(q_me + step, planes)
        remote(src_ref, out_ref.at[z_me, q_me], s1_send.at[step - 1], s1_recv.at[step - 1],
               (plane_peer(q), kv)).start()
        return carry

    lax.fori_loop(1, planes, send, 0)

    def finish(step, carry):
        q = lax.rem(q_me + step, planes)
        source = lax.rem(q_me + planes - step, planes)
        remote(src_ref, out_ref.at[z_me, q_me], s1_send.at[step - 1], s1_recv.at[step - 1],
               (plane_peer(q), kv)).wait_send()
        remote(src_ref, out_ref.at[z_me, source], s1_send.at[step - 1], s1_recv.at[step - 1],
               (plane_peer(source), kv)).wait_recv()
        return carry

    lax.fori_loop(1, planes, finish, 0)
    local.wait()

    sent = []
    if right_hops > 0:
        c = remote(out_ref.at[z_me], out_ref.at[z_me], r_send.at[0], r_recv.at[0],
                   (ring_peer(z_right), kv))
        c.start()
        sent.append(c)
    if left_hops > 0:
        c = remote(out_ref.at[z_me], out_ref.at[z_me], l_send.at[0], l_recv.at[0],
                   (ring_peer(z_left), kv))
        c.start()
        sent.append(c)
    for k in range(1, max(right_hops, left_hops) + 1):
        if k <= right_hops:
            z_from = lax.rem(z_me + runs - k, runs)
            remote(out_ref.at[z_from], out_ref.at[z_from], r_send.at[k - 1], r_recv.at[k - 1],
                   (ring_peer(z_right), kv)).wait_recv()
            if k < right_hops:
                c = remote(out_ref.at[z_from], out_ref.at[z_from], r_send.at[k], r_recv.at[k],
                           (ring_peer(z_right), kv))
                c.start()
                sent.append(c)
        if k <= left_hops:
            z_from = lax.rem(z_me + k, runs)
            remote(out_ref.at[z_from], out_ref.at[z_from], l_send.at[k - 1], l_recv.at[k - 1],
                   (ring_peer(z_left), kv)).wait_recv()
            if k < left_hops:
                c = remote(out_ref.at[z_from], out_ref.at[z_from], l_send.at[k], l_recv.at[k],
                           (ring_peer(z_left), kv))
                c.start()
                sent.append(c)
    for c in sent:
        c.wait_send()

    def finish_kv(step, carry):
        peer = lax.rem(kv + step, kv_count)
        source = lax.rem(kv + kv_count - step, kv_count)
        for which, (cache_src, cache_dst) in enumerate(caches):
            remote(cache_src.at[peer], cache_dst.at[kv], kv_send.at[which, step - 1],
                   kv_recv.at[which, step - 1], (me, peer)).wait_send()
            remote(cache_src.at[kv], cache_dst.at[source], kv_send.at[which, step - 1],
                   kv_recv.at[which, step - 1], (me, source)).wait_recv()
        return carry

    lax.fori_loop(1, kv_count, finish_kv, 0)
    for c in local_cache:
        c.wait()


def gather_req(piece, keys_send, values_send):
    count = lax.axis_size("req")
    kv_count = lax.axis_size("kv")
    runs = min(Z_RUN, count // Y_RUN)
    planes = count // runs
    rows, width = piece.shape
    hops = max(runs - 1, 1)
    anywhere = pl.BlockSpec(memory_space=pl.ANY)
    gathered, keys_old, values_old = pl.pallas_call(
        functools.partial(plane_ring_kernel, planes, runs),
        out_shape=(
            jax.ShapeDtypeStruct((runs, planes, rows, width), piece.dtype),
            jax.ShapeDtypeStruct(keys_send.shape, keys_send.dtype),
            jax.ShapeDtypeStruct(values_send.shape, values_send.dtype),
        ),
        in_specs=[anywhere, anywhere, anywhere],
        out_specs=(anywhere, anywhere, anywhere),
        scratch_shapes=[
            pltpu.SemaphoreType.DMA((planes - 1,)),
            pltpu.SemaphoreType.DMA((planes - 1,)),
            pltpu.SemaphoreType.DMA((hops,)),
            pltpu.SemaphoreType.DMA((hops,)),
            pltpu.SemaphoreType.DMA((hops,)),
            pltpu.SemaphoreType.DMA((hops,)),
            pltpu.SemaphoreType.DMA,
            pltpu.SemaphoreType.DMA((2, kv_count - 1)),
            pltpu.SemaphoreType.DMA((2, kv_count - 1)),
            pltpu.SemaphoreType.DMA((2,)),
        ],
        compiler_params=pltpu.CompilerParams(collective_id=0, has_side_effects=True),
    )(piece, keys_send, values_send)
    x_count = planes // Y_RUN
    ordered = jnp.transpose(
        gathered.reshape(runs, x_count, Y_RUN, rows, width), (1, 0, 2, 3, 4)
    )
    return ordered.reshape(count * rows, width), keys_old, values_old


BLOCK_Q = 512
BLOCK_K = 512


def flash_kernel(tokens, scale, len_ref, q_ref, kc_ref, vc_ref, kn_ref, vn_ref, o_ref):
    block_q = q_ref.shape[1]
    block_k = kc_ref.shape[2]
    width = q_ref.shape[2]
    i = pl.program_id(1)
    length = len_ref[0]
    first = lax.rem(i * block_q, tokens)
    q = q_ref[0]
    query_index = first + lax.broadcasted_iota(jnp.int32, (block_q, block_k), 0)
    key_offset = lax.broadcasted_iota(jnp.int32, (block_q, block_k), 1)

    def step(keys, values, visible, carry):
        peak, total, acc = carry
        score = lax.dot_general(
            q, keys, (((1,), (1,)), ((), ())), preferred_element_type=jnp.float32
        ) * scale
        score = jnp.where(visible, score, masked_score)
        new_peak = jnp.maximum(peak, jnp.max(score, axis=1, keepdims=True))
        alpha = jnp.exp(peak - new_peak)
        weights = jnp.where(visible, jnp.exp(score - new_peak), 0.0)
        total = alpha * total + jnp.sum(weights, axis=1, keepdims=True)
        acc = alpha * acc + jnp.dot(
            weights.astype(jnp.bfloat16), values, preferred_element_type=jnp.float32
        )
        return new_peak, total, acc

    def cache_step(block, carry):
        start = pl.multiple_of(block * block_k, block_k)
        keys = kc_ref[block, 0]
        values = vc_ref[block, 0]
        visible = start + key_offset < length
        return step(keys, values, visible, carry)

    def new_step(block, carry):
        start = pl.multiple_of(block * block_k, block_k)
        keys = kn_ref[0, pl.ds(start, block_k), :]
        values = vn_ref[0, pl.ds(start, block_k), :]
        visible = start + key_offset <= query_index
        return step(keys, values, visible, carry)

    carry = (
        jnp.full((block_q, 1), -jnp.inf, jnp.float32),
        jnp.zeros((block_q, 1), jnp.float32),
        jnp.zeros((block_q, width), jnp.float32),
    )
    live_blocks = (length + block_k - 1) // block_k
    carry = lax.fori_loop(0, live_blocks, cache_step, carry)
    new_blocks = (first + block_q - 1) // block_k + 1
    peak, total, acc = lax.fori_loop(0, new_blocks, new_step, carry)
    o_ref[0] = (acc / total).astype(o_ref.dtype)


def flash_attention(lengths, queries, keys_old, values_old, keys_new, values_new, tokens, scale):
    heads, rows, width = queries.shape
    blocks, _, block_k, _ = keys_old.shape
    slots = blocks * block_k
    block_q = min(BLOCK_Q, tokens)
    grid = (heads, rows // block_q)
    whole_cache = pl.BlockSpec((blocks, 1, block_k, width), lambda c, i, n: (0, c, 0, 0))
    whole_new = pl.BlockSpec((1, tokens, width), lambda c, i, n: (c, 0, 0))
    return pl.pallas_call(
        functools.partial(flash_kernel, tokens, scale),
        out_shape=jax.ShapeDtypeStruct((heads, rows, width), jnp.bfloat16),
        grid_spec=pltpu.PrefetchScalarGridSpec(
            num_scalar_prefetch=1,
            grid=grid,
            in_specs=[
                pl.BlockSpec((1, block_q, width), lambda c, i, n: (c, i, 0)),
                whole_cache, whole_cache, whole_new, whole_new,
            ],
            out_specs=pl.BlockSpec((1, block_q, width), lambda c, i, n: (c, i, 0)),
        ),
        cost_estimate=pl.CostEstimate(
            flops=4 * heads * rows * (slots + tokens) * width,
            transcendentals=heads * rows * (slots + tokens),
            bytes_accessed=2 * width * heads * (2 * rows + 2 * slots + 2 * tokens),
        ),
    )(lengths, queries, keys_old, values_old, keys_new, values_new)


def body(hidden, lengths, key_cache, value_cache, norm_gain, w_query, w_key, w_value, w_out):
    rows_here = hidden.shape[1]
    kv_count = lax.axis_size("kv")
    appended = rows_here * kv_count
    slots = key_cache.shape[1]
    groups = H // KVH
    scale = HD ** (-0.5)
    length = lengths[0]
    q_cols = w_query.shape[1]
    k_cols = w_key.shape[1]
    v_cols = w_value.shape[1]
    heads_here = q_cols // HD
    kv_heads_here = k_cols // HD

    normed = rms_norm(hidden[0].astype(jnp.float32), norm_gain)
    normed_all = lax.all_gather(normed, "kv", axis=0, tiled=True)

    pieces = jnp.concatenate([w_query, w_key, w_value, w_out], axis=1)
    def to_peers(cache):
        return jnp.transpose(
            cache.reshape(slots, kv_count, kv_heads_here, HD), (1, 2, 0, 3)
        )

    cols, keys_old, values_old = gather_req(
        pieces, to_peers(key_cache[0]), to_peers(value_cache[0])
    )
    wq = cols[:, :q_cols]
    wk = cols[:, q_cols:q_cols + k_cols]
    wv = cols[:, q_cols + k_cols:q_cols + k_cols + v_cols]
    wo = cols[:, q_cols + k_cols + v_cols:]

    wo_full = lax.all_gather(wo, "kv", axis=1, tiled=True)

    positions = (length + jnp.arange(appended, dtype=jnp.int32)).astype(jnp.float32)
    proj_q = jnp.dot(normed_all, wq, preferred_element_type=jnp.float32)
    proj_k = jnp.dot(normed_all, wk, preferred_element_type=jnp.float32)
    proj_v = jnp.dot(normed_all, wv, preferred_element_type=jnp.float32)
    queries = rotate(proj_q, positions).astype(jnp.bfloat16)
    keys_new = rotate(proj_k, positions).astype(jnp.bfloat16)
    values_new = proj_v.astype(jnp.bfloat16)

    new_keys = lax.all_to_all(keys_new, "kv", split_axis=0, concat_axis=1, tiled=True)
    new_values = lax.all_to_all(values_new, "kv", split_axis=0, concat_axis=1, tiled=True)


    def by_head(values):
        count = values.shape[0]
        return jnp.transpose(values.reshape(count, kv_heads_here, HD), (1, 0, 2))

    query_heads = jnp.transpose(
        queries.reshape(appended, kv_heads_here, groups, HD), (1, 2, 0, 3)
    ).reshape(kv_heads_here, groups * appended, HD)
    contexts = flash_attention(
        lengths, query_heads, keys_old, values_old,
        by_head(keys_new), by_head(values_new), appended, scale,
    )
    context = jnp.transpose(
        contexts.reshape(kv_heads_here, groups, appended, HD), (2, 0, 1, 3)
    ).reshape(appended, heads_here * HD)
    context_rows = lax.all_to_all(context, "kv", split_axis=0, concat_axis=1, tiled=True)
    attended = jnp.dot(context_rows, wo_full, preferred_element_type=jnp.float32).astype(jnp.bfloat16)
    return (attended[None], new_keys[None], new_values[None])


def solution(mesh):
    return jax.shard_map(
        body,
        mesh=mesh,
        in_specs=(
            P("req", "kv", None),
            P("req"),
            P("req", "kv", None),
            P("req", "kv", None),
            P(),
            P("req", "kv"),
            P("req", "kv"),
            P("req", "kv"),
            P("req", "kv"),
        ),
        out_specs=(P("req", "kv", None), P("req", "kv", None), P("req", "kv", None)),
        check_vma=False,
    )
```

```python
import functools

import jax
import jax.numpy as jnp
from jax import lax
from jax.sharding import PartitionSpec as P
from jax.experimental import pallas as pl
from jax.experimental.pallas import tpu as pltpu

H = 16
KVH = 8
HD = 96


rope_base = 100000.0
masked_score = -1e30


def rms_norm(states, gain):
    mean_square = jnp.mean(states * states, axis=-1, keepdims=True)
    scaled = states * lax.rsqrt(mean_square + 1e-05) * gain.astype(jnp.float32)
    return scaled.astype(jnp.bfloat16)


def rotate(values, positions):
    count = values.shape[0]
    heads = values.shape[1] // HD
    half = HD // 2
    frequency = rope_base ** (-(jnp.arange(half, dtype=jnp.float32) * 2.0 / HD))
    angle = positions[:, None] * frequency[None, :]
    cosine = jnp.cos(angle)[:, None, :]
    sine = jnp.sin(angle)[:, None, :]
    shaped = values.reshape(count, heads, HD)
    first = shaped[..., :half]
    second = shaped[..., half:]
    turned = jnp.concatenate(
        [first * cosine - second * sine, second * cosine + first * sine], axis=-1
    )
    return turned.reshape(count, heads * HD)


Z_RUN = 8
Y_RUN = 2
MESH = pl.DeviceIdType.MESH


def remote(src, dst, send, recv, device):
    return pltpu.make_async_remote_copy(
        src_ref=src, dst_ref=dst, send_sem=send, recv_sem=recv,
        device_id=device, device_id_type=MESH,
    )


def plane_ring_kernel(planes, runs, src_ref, kc_ref, vc_ref, out_ref, kc_out, vc_out, s1_send,
                      s1_recv, r_send, r_recv, l_send, l_recv, local_sem, kv_send, kv_recv, kv_local):
    me = lax.axis_index("req")
    kv = lax.axis_index("kv")
    y_me = lax.rem(me, Y_RUN)
    z_me = lax.rem(me // Y_RUN, runs)
    x_me = me // (Y_RUN * runs)
    q_me = x_me * Y_RUN + y_me
    right_hops = runs // 2
    left_hops = runs - 1 - right_hops

    def plane_peer(q):
        return ((q // Y_RUN) * runs + z_me) * Y_RUN + lax.rem(q, Y_RUN)

    def ring_peer(z):
        return (x_me * runs + z) * Y_RUN + y_me

    z_right = lax.rem(z_me + 1, runs)
    z_left = lax.rem(z_me + runs - 1, runs)

    barrier = pltpu.get_barrier_semaphore()

    def greet(step, carry):
        q = lax.rem(q_me + step, planes)
        pl.semaphore_signal(barrier, inc=1, device_id=(plane_peer(q), kv), device_id_type=MESH)
        return carry

    lax.fori_loop(1, planes, greet, 0)
    pl.semaphore_signal(barrier, inc=1, device_id=(ring_peer(z_right), kv), device_id_type=MESH)
    pl.semaphore_signal(barrier, inc=1, device_id=(ring_peer(z_left), kv), device_id_type=MESH)
    kv_count = lax.axis_size("kv")

    def greet_kv(step, carry):
        peer = lax.rem(kv + step, kv_count)
        pl.semaphore_signal(barrier, inc=1, device_id=(me, peer), device_id_type=MESH)
        return carry

    lax.fori_loop(1, kv_count, greet_kv, 0)
    pl.semaphore_wait(barrier, planes + 1 + kv_count - 1)

    local = pltpu.make_async_copy(src_ref, out_ref.at[z_me, q_me], local_sem)
    local.start()
    caches = ((kc_ref, kc_out), (vc_ref, vc_out))
    local_cache = []
    for which, (cache_src, cache_dst) in enumerate(caches):
        c = pltpu.make_async_copy(cache_src.at[kv], cache_dst.at[kv], kv_local.at[which])
        c.start()
        local_cache.append(c)


    def send(step, carry):
        q = lax.rem(q_me + step, planes)
        remote(src_ref, out_ref.at[z_me, q_me], s1_send.at[step - 1], s1_recv.at[step - 1],
               (plane_peer(q), kv)).start()
        return carry

    lax.fori_loop(1, planes, send, 0)

    def finish(step, carry):
        q = lax.rem(q_me + step, planes)
        source = lax.rem(q_me + planes - step, planes)
        remote(src_ref, out_ref.at[z_me, q_me], s1_send.at[step - 1], s1_recv.at[step - 1],
               (plane_peer(q), kv)).wait_send()
        remote(src_ref, out_ref.at[z_me, source], s1_send.at[step - 1], s1_recv.at[step - 1],
               (plane_peer(source), kv)).wait_recv()
        return carry

    lax.fori_loop(1, planes, finish, 0)
    local.wait()

    sent = []
    if right_hops > 0:
        c = remote(out_ref.at[z_me], out_ref.at[z_me], r_send.at[0], r_recv.at[0],
                   (ring_peer(z_right), kv))
        c.start()
        sent.append(c)
    if left_hops > 0:
        c = remote(out_ref.at[z_me], out_ref.at[z_me], l_send.at[0], l_recv.at[0],
                   (ring_peer(z_left), kv))
        c.start()
        sent.append(c)
    def send_kv(step, carry):
        peer = lax.rem(kv + step, kv_count)
        for which, (cache_src, cache_dst) in enumerate(caches):
            remote(cache_src.at[peer], cache_dst.at[kv], kv_send.at[which, step - 1],
                   kv_recv.at[which, step - 1], (me, peer)).start()
        return carry

    lax.fori_loop(1, kv_count, send_kv, 0)
    for k in range(1, max(right_hops, left_hops) + 1):
        if k <= right_hops:
            z_from = lax.rem(z_me + runs - k, runs)
            remote(out_ref.at[z_from], out_ref.at[z_from], r_send.at[k - 1], r_recv.at[k - 1],
                   (ring_peer(z_right), kv)).wait_recv()
            if k < right_hops:
                c = remote(out_ref.at[z_from], out_ref.at[z_from], r_send.at[k], r_recv.at[k],
                           (ring_peer(z_right), kv))
                c.start()
                sent.append(c)
        if k <= left_hops:
            z_from = lax.rem(z_me + k, runs)
            remote(out_ref.at[z_from], out_ref.at[z_from], l_send.at[k - 1], l_recv.at[k - 1],
                   (ring_peer(z_left), kv)).wait_recv()
            if k < left_hops:
                c = remote(out_ref.at[z_from], out_ref.at[z_from], l_send.at[k], l_recv.at[k],
                           (ring_peer(z_left), kv))
                c.start()
                sent.append(c)
    for c in sent:
        c.wait_send()

    def finish_kv(step, carry):
        peer = lax.rem(kv + step, kv_count)
        source = lax.rem(kv + kv_count - step, kv_count)
        for which, (cache_src, cache_dst) in enumerate(caches):
            remote(cache_src.at[peer], cache_dst.at[kv], kv_send.at[which, step - 1],
                   kv_recv.at[which, step - 1], (me, peer)).wait_send()
            remote(cache_src.at[kv], cache_dst.at[source], kv_send.at[which, step - 1],
                   kv_recv.at[which, step - 1], (me, source)).wait_recv()
        return carry

    lax.fori_loop(1, kv_count, finish_kv, 0)
    for c in local_cache:
        c.wait()


def gather_req(piece, keys_send, values_send):
    count = lax.axis_size("req")
    kv_count = lax.axis_size("kv")
    runs = min(Z_RUN, count // Y_RUN)
    planes = count // runs
    rows, width = piece.shape
    hops = max(runs - 1, 1)
    anywhere = pl.BlockSpec(memory_space=pl.ANY)
    gathered, keys_old, values_old = pl.pallas_call(
        functools.partial(plane_ring_kernel, planes, runs),
        out_shape=(
            jax.ShapeDtypeStruct((runs, planes, rows, width), piece.dtype),
            jax.ShapeDtypeStruct(keys_send.shape, keys_send.dtype),
            jax.ShapeDtypeStruct(values_send.shape, values_send.dtype),
        ),
        in_specs=[anywhere, anywhere, anywhere],
        out_specs=(anywhere, anywhere, anywhere),
        scratch_shapes=[
            pltpu.SemaphoreType.DMA((planes - 1,)),
            pltpu.SemaphoreType.DMA((planes - 1,)),
            pltpu.SemaphoreType.DMA((hops,)),
            pltpu.SemaphoreType.DMA((hops,)),
            pltpu.SemaphoreType.DMA((hops,)),
            pltpu.SemaphoreType.DMA((hops,)),
            pltpu.SemaphoreType.DMA,
            pltpu.SemaphoreType.DMA((2, kv_count - 1)),
            pltpu.SemaphoreType.DMA((2, kv_count - 1)),
            pltpu.SemaphoreType.DMA((2,)),
        ],
        compiler_params=pltpu.CompilerParams(collective_id=0, has_side_effects=True),
    )(piece, keys_send, values_send)
    x_count = planes // Y_RUN
    ordered = jnp.transpose(
        gathered.reshape(runs, x_count, Y_RUN, rows, width), (1, 0, 2, 3, 4)
    )
    return ordered.reshape(count * rows, width), keys_old, values_old


BLOCK_Q = 512
BLOCK_K = 512


def flash_kernel(tokens, scale, len_ref, q_ref, kc_ref, vc_ref, kn_ref, vn_ref, o_ref):
    block_q = q_ref.shape[1]
    block_k = kc_ref.shape[2]
    width = q_ref.shape[2]
    i = pl.program_id(1)
    length = len_ref[0]
    first = lax.rem(i * block_q, tokens)
    q = q_ref[0]
    query_index = first + lax.broadcasted_iota(jnp.int32, (block_q, block_k), 0)
    key_offset = lax.broadcasted_iota(jnp.int32, (block_q, block_k), 1)

    def step(keys, values, visible, carry):
        peak, total, acc = carry
        score = lax.dot_general(
            q, keys, (((1,), (1,)), ((), ())), preferred_element_type=jnp.float32
        ) * scale
        score = jnp.where(visible, score, masked_score)
        new_peak = jnp.maximum(peak, jnp.max(score, axis=1, keepdims=True))
        alpha = jnp.exp(peak - new_peak)
        weights = jnp.where(visible, jnp.exp(score - new_peak), 0.0)
        total = alpha * total + jnp.sum(weights, axis=1, keepdims=True)
        acc = alpha * acc + jnp.dot(
            weights.astype(jnp.bfloat16), values, preferred_element_type=jnp.float32
        )
        return new_peak, total, acc

    def cache_step(block, carry):
        start = pl.multiple_of(block * block_k, block_k)
        keys = kc_ref[block, 0]
        values = vc_ref[block, 0]
        visible = start + key_offset < length
        return step(keys, values, visible, carry)

    def new_step(block, carry):
        start = pl.multiple_of(block * block_k, block_k)
        keys = kn_ref[0, pl.ds(start, block_k), :]
        values = vn_ref[0, pl.ds(start, block_k), :]
        visible = start + key_offset <= query_index
        return step(keys, values, visible, carry)

    carry = (
        jnp.full((block_q, 1), -jnp.inf, jnp.float32),
        jnp.zeros((block_q, 1), jnp.float32),
        jnp.zeros((block_q, width), jnp.float32),
    )
    live_blocks = (length + block_k - 1) // block_k
    carry = lax.fori_loop(0, live_blocks, cache_step, carry)
    new_blocks = (first + block_q - 1) // block_k + 1
    peak, total, acc = lax.fori_loop(0, new_blocks, new_step, carry)
    o_ref[0] = (acc / total).astype(o_ref.dtype)


def flash_attention(lengths, queries, keys_old, values_old, keys_new, values_new, tokens, scale):
    heads, rows, width = queries.shape
    blocks, _, block_k, _ = keys_old.shape
    slots = blocks * block_k
    block_q = min(BLOCK_Q, tokens)
    grid = (heads, rows // block_q)
    whole_cache = pl.BlockSpec((blocks, 1, block_k, width), lambda c, i, n: (0, c, 0, 0))
    whole_new = pl.BlockSpec((1, tokens, width), lambda c, i, n: (c, 0, 0))
    return pl.pallas_call(
        functools.partial(flash_kernel, tokens, scale),
        out_shape=jax.ShapeDtypeStruct((heads, rows, width), jnp.bfloat16),
        grid_spec=pltpu.PrefetchScalarGridSpec(
            num_scalar_prefetch=1,
            grid=grid,
            in_specs=[
                pl.BlockSpec((1, block_q, width), lambda c, i, n: (c, i, 0)),
                whole_cache, whole_cache, whole_new, whole_new,
            ],
            out_specs=pl.BlockSpec((1, block_q, width), lambda c, i, n: (c, i, 0)),
        ),
        cost_estimate=pl.CostEstimate(
            flops=4 * heads * rows * (slots + tokens) * width,
            transcendentals=heads * rows * (slots + tokens),
            bytes_accessed=2 * width * heads * (2 * rows + 2 * slots + 2 * tokens),
        ),
    )(lengths, queries, keys_old, values_old, keys_new, values_new)


def body(hidden, lengths, key_cache, value_cache, norm_gain, w_query, w_key, w_value, w_out):
    rows_here = hidden.shape[1]
    kv_count = lax.axis_size("kv")
    appended = rows_here * kv_count
    slots = key_cache.shape[1]
    groups = H // KVH
    scale = HD ** (-0.5)
    length = lengths[0]
    q_cols = w_query.shape[1]
    k_cols = w_key.shape[1]
    v_cols = w_value.shape[1]
    heads_here = q_cols // HD
    kv_heads_here = k_cols // HD

    normed = rms_norm(hidden[0].astype(jnp.float32), norm_gain)
    normed_all = lax.all_gather(normed, "kv", axis=0, tiled=True)

    pieces = jnp.concatenate([w_query, w_key, w_value, w_out], axis=1)
    def to_peers(cache):
        return jnp.transpose(
            cache.reshape(slots, kv_count, kv_heads_here, HD), (1, 2, 0, 3)
        )

    cols, keys_old, values_old = gather_req(
        pieces, to_peers(key_cache[0]), to_peers(value_cache[0])
    )
    wq = cols[:, :q_cols]
    wk = cols[:, q_cols:q_cols + k_cols]
    wv = cols[:, q_cols + k_cols:q_cols + k_cols + v_cols]
    wo = cols[:, q_cols + k_cols + v_cols:]

    wo_full = lax.all_gather(wo, "kv", axis=1, tiled=True)

    positions = (length + jnp.arange(appended, dtype=jnp.int32)).astype(jnp.float32)
    proj_q = jnp.dot(normed_all, wq, preferred_element_type=jnp.float32)
    proj_k = jnp.dot(normed_all, wk, preferred_element_type=jnp.float32)
    proj_v = jnp.dot(normed_all, wv, preferred_element_type=jnp.float32)
    queries = rotate(proj_q, positions).astype(jnp.bfloat16)
    keys_new = rotate(proj_k, positions).astype(jnp.bfloat16)
    values_new = proj_v.astype(jnp.bfloat16)

    new_keys = lax.all_to_all(keys_new, "kv", split_axis=0, concat_axis=1, tiled=True)
    new_values = lax.all_to_all(values_new, "kv", split_axis=0, concat_axis=1, tiled=True)


    def by_head(values):
        count = values.shape[0]
        return jnp.transpose(values.reshape(count, kv_heads_here, HD), (1, 0, 2))

    query_heads = jnp.transpose(
        queries.reshape(appended, kv_heads_here, groups, HD), (1, 2, 0, 3)
    ).reshape(kv_heads_here, groups * appended, HD)
    contexts = flash_attention(
        lengths, query_heads, keys_old, values_old,
        by_head(keys_new), by_head(values_new), appended, scale,
    )
    context = jnp.transpose(
        contexts.reshape(kv_heads_here, groups, appended, HD), (2, 0, 1, 3)
    ).reshape(appended, heads_here * HD)
    context_rows = lax.all_to_all(context, "kv", split_axis=0, concat_axis=1, tiled=True)
    attended = jnp.dot(context_rows, wo_full, preferred_element_type=jnp.float32).astype(jnp.bfloat16)
    return (attended[None], new_keys[None], new_values[None])


def solution(mesh):
    return jax.shard_map(
        body,
        mesh=mesh,
        in_specs=(
            P("req", "kv", None),
            P("req"),
            P("req", "kv", None),
            P("req", "kv", None),
            P(),
            P("req", "kv"),
            P("req", "kv"),
            P("req", "kv"),
            P("req", "kv"),
        ),
        out_specs=(P("req", "kv", None), P("req", "kv", None), P("req", "kv", None)),
        check_vma=False,
    )
```

```python
import functools

import jax
import jax.numpy as jnp
from jax import lax
from jax.sharding import PartitionSpec as P
from jax.experimental import pallas as pl
from jax.experimental.pallas import tpu as pltpu

H = 16
KVH = 8
HD = 96


rope_base = 100000.0
masked_score = -1e30


def rms_norm(states, gain):
    mean_square = jnp.mean(states * states, axis=-1, keepdims=True)
    scaled = states * lax.rsqrt(mean_square + 1e-05) * gain.astype(jnp.float32)
    return scaled.astype(jnp.bfloat16)


def rotate(values, positions):
    count = values.shape[0]
    heads = values.shape[1] // HD
    half = HD // 2
    frequency = rope_base ** (-(jnp.arange(half, dtype=jnp.float32) * 2.0 / HD))
    angle = positions[:, None] * frequency[None, :]
    cosine = jnp.cos(angle)[:, None, :]
    sine = jnp.sin(angle)[:, None, :]
    shaped = values.reshape(count, heads, HD)
    first = shaped[..., :half]
    second = shaped[..., half:]
    turned = jnp.concatenate(
        [first * cosine - second * sine, second * cosine + first * sine], axis=-1
    )
    return turned.reshape(count, heads * HD)


Z_RUN = 8
Y_RUN = 2
MESH = pl.DeviceIdType.MESH


def remote(src, dst, send, recv, device):
    return pltpu.make_async_remote_copy(
        src_ref=src, dst_ref=dst, send_sem=send, recv_sem=recv,
        device_id=device, device_id_type=MESH,
    )


def plane_ring_kernel(planes, runs, src_ref, kc_ref, vc_ref, out_ref, kc_out, vc_out, s1_send,
                      s1_recv, r_send, r_recv, l_send, l_recv, local_sem, kv_send, kv_recv, kv_local):
    me = lax.axis_index("req")
    kv = lax.axis_index("kv")
    y_me = lax.rem(me, Y_RUN)
    z_me = lax.rem(me // Y_RUN, runs)
    x_me = me // (Y_RUN * runs)
    q_me = x_me * Y_RUN + y_me
    right_hops = runs // 2
    left_hops = runs - 1 - right_hops

    def plane_peer(q):
        return ((q // Y_RUN) * runs + z_me) * Y_RUN + lax.rem(q, Y_RUN)

    def ring_peer(z):
        return (x_me * runs + z) * Y_RUN + y_me

    z_right = lax.rem(z_me + 1, runs)
    z_left = lax.rem(z_me + runs - 1, runs)

    barrier = pltpu.get_barrier_semaphore()

    def greet(step, carry):
        q = lax.rem(q_me + step, planes)
        pl.semaphore_signal(barrier, inc=1, device_id=(plane_peer(q), kv), device_id_type=MESH)
        return carry

    lax.fori_loop(1, planes, greet, 0)
    pl.semaphore_signal(barrier, inc=1, device_id=(ring_peer(z_right), kv), device_id_type=MESH)
    pl.semaphore_signal(barrier, inc=1, device_id=(ring_peer(z_left), kv), device_id_type=MESH)
    kv_count = lax.axis_size("kv")

    def greet_kv(step, carry):
        peer = lax.rem(kv + step, kv_count)
        pl.semaphore_signal(barrier, inc=1, device_id=(me, peer), device_id_type=MESH)
        return carry

    lax.fori_loop(1, kv_count, greet_kv, 0)
    pl.semaphore_wait(barrier, planes + 1 + kv_count - 1)

    local = pltpu.make_async_copy(src_ref, out_ref.at[z_me, q_me], local_sem)
    local.start()
    caches = ((kc_ref, kc_out), (vc_ref, vc_out))
    local_cache = []
    for which, (cache_src, cache_dst) in enumerate(caches):
        c = pltpu.make_async_copy(cache_src.at[kv], cache_dst.at[kv], kv_local.at[which])
        c.start()
        local_cache.append(c)


    def send(step, carry):
        q = lax.rem(q_me + step, planes)
        remote(src_ref, out_ref.at[z_me, q_me], s1_send.at[step - 1], s1_recv.at[step - 1],
               (plane_peer(q), kv)).start()
        return carry

    lax.fori_loop(1, planes, send, 0)

    def finish(step, carry):
        q = lax.rem(q_me + step, planes)
        source = lax.rem(q_me + planes - step, planes)
        remote(src_ref, out_ref.at[z_me, q_me], s1_send.at[step - 1], s1_recv.at[step - 1],
               (plane_peer(q), kv)).wait_send()
        remote(src_ref, out_ref.at[z_me, source], s1_send.at[step - 1], s1_recv.at[step - 1],
               (plane_peer(source), kv)).wait_recv()
        return carry

    lax.fori_loop(1, planes, finish, 0)
    local.wait()

    sent = []
    if right_hops > 0:
        c = remote(out_ref.at[z_me], out_ref.at[z_me], r_send.at[0], r_recv.at[0],
                   (ring_peer(z_right), kv))
        c.start()
        sent.append(c)
    if left_hops > 0:
        c = remote(out_ref.at[z_me], out_ref.at[z_me], l_send.at[0], l_recv.at[0],
                   (ring_peer(z_left), kv))
        c.start()
        sent.append(c)
    def send_kv(step, carry):
        peer = lax.rem(kv + step, kv_count)
        for which, (cache_src, cache_dst) in enumerate(caches):
            remote(cache_src.at[peer], cache_dst.at[kv], kv_send.at[which, step - 1],
                   kv_recv.at[which, step - 1], (me, peer)).start()
        return carry

    lax.fori_loop(1, kv_count, send_kv, 0)
    for k in range(1, max(right_hops, left_hops) + 1):
        if k <= right_hops:
            z_from = lax.rem(z_me + runs - k, runs)
            remote(out_ref.at[z_from], out_ref.at[z_from], r_send.at[k - 1], r_recv.at[k - 1],
                   (ring_peer(z_right), kv)).wait_recv()
            if k < right_hops:
                c = remote(out_ref.at[z_from], out_ref.at[z_from], r_send.at[k], r_recv.at[k],
                           (ring_peer(z_right), kv))
                c.start()
                sent.append(c)
        if k <= left_hops:
            z_from = lax.rem(z_me + k, runs)
            remote(out_ref.at[z_from], out_ref.at[z_from], l_send.at[k - 1], l_recv.at[k - 1],
                   (ring_peer(z_left), kv)).wait_recv()
            if k < left_hops:
                c = remote(out_ref.at[z_from], out_ref.at[z_from], l_send.at[k], l_recv.at[k],
                           (ring_peer(z_left), kv))
                c.start()
                sent.append(c)
    for c in sent:
        c.wait_send()

    def finish_kv(step, carry):
        peer = lax.rem(kv + step, kv_count)
        source = lax.rem(kv + kv_count - step, kv_count)
        for which, (cache_src, cache_dst) in enumerate(caches):
            remote(cache_src.at[peer], cache_dst.at[kv], kv_send.at[which, step - 1],
                   kv_recv.at[which, step - 1], (me, peer)).wait_send()
            remote(cache_src.at[kv], cache_dst.at[source], kv_send.at[which, step - 1],
                   kv_recv.at[which, step - 1], (me, source)).wait_recv()
        return carry

    lax.fori_loop(1, kv_count, finish_kv, 0)
    for c in local_cache:
        c.wait()


def gather_req(piece, keys_send, values_send):
    count = lax.axis_size("req")
    kv_count = lax.axis_size("kv")
    runs = min(Z_RUN, count // Y_RUN)
    planes = count // runs
    rows, width = piece.shape
    hops = max(runs - 1, 1)
    anywhere = pl.BlockSpec(memory_space=pl.ANY)
    gathered, keys_old, values_old = pl.pallas_call(
        functools.partial(plane_ring_kernel, planes, runs),
        out_shape=(
            jax.ShapeDtypeStruct((runs, planes, rows, width), piece.dtype),
            jax.ShapeDtypeStruct(keys_send.shape, keys_send.dtype),
            jax.ShapeDtypeStruct(values_send.shape, values_send.dtype),
        ),
        in_specs=[anywhere, anywhere, anywhere],
        out_specs=(anywhere, anywhere, anywhere),
        scratch_shapes=[
            pltpu.SemaphoreType.DMA((planes - 1,)),
            pltpu.SemaphoreType.DMA((planes - 1,)),
            pltpu.SemaphoreType.DMA((hops,)),
            pltpu.SemaphoreType.DMA((hops,)),
            pltpu.SemaphoreType.DMA((hops,)),
            pltpu.SemaphoreType.DMA((hops,)),
            pltpu.SemaphoreType.DMA,
            pltpu.SemaphoreType.DMA((2, kv_count - 1)),
            pltpu.SemaphoreType.DMA((2, kv_count - 1)),
            pltpu.SemaphoreType.DMA((2,)),
        ],
        compiler_params=pltpu.CompilerParams(collective_id=0, has_side_effects=True),
    )(piece, keys_send, values_send)
    x_count = planes // Y_RUN
    ordered = jnp.transpose(
        gathered.reshape(runs, x_count, Y_RUN, rows, width), (1, 0, 2, 3, 4)
    )
    return ordered.reshape(count * rows, width), keys_old, values_old


BLOCK_Q = 512
BLOCK_K = 512


def flash_kernel(tokens, scale, len_ref, q_ref, kc_ref, vc_ref, kn_ref, vn_ref, o_ref):
    block_q = q_ref.shape[1]
    block_k = kc_ref.shape[2]
    width = q_ref.shape[2]
    i = pl.program_id(1)
    length = len_ref[0]
    first = lax.rem(i * block_q, tokens)
    q = q_ref[0]
    query_index = first + lax.broadcasted_iota(jnp.int32, (block_q, block_k), 0)
    key_offset = lax.broadcasted_iota(jnp.int32, (block_q, block_k), 1)

    def step(keys, values, visible, carry):
        peak, total, acc = carry
        score = lax.dot_general(
            q, keys, (((1,), (1,)), ((), ())), preferred_element_type=jnp.float32
        ) * scale
        score = jnp.where(visible, score, masked_score)
        new_peak = jnp.maximum(peak, jnp.max(score, axis=1, keepdims=True))
        alpha = jnp.exp(peak - new_peak)
        weights = jnp.where(visible, jnp.exp(score - new_peak), 0.0)
        total = alpha * total + jnp.sum(weights, axis=1, keepdims=True)
        acc = alpha * acc + jnp.dot(
            weights.astype(jnp.bfloat16), values, preferred_element_type=jnp.float32
        )
        return new_peak, total, acc

    def cache_step(block, carry):
        start = pl.multiple_of(block * block_k, block_k)
        keys = kc_ref[block, 0]
        values = vc_ref[block, 0]
        visible = start + key_offset < length
        return step(keys, values, visible, carry)

    def new_step(block, carry):
        start = pl.multiple_of(block * block_k, block_k)
        keys = kn_ref[0, pl.ds(start, block_k), :]
        values = vn_ref[0, pl.ds(start, block_k), :]
        visible = start + key_offset <= query_index
        return step(keys, values, visible, carry)

    carry = (
        jnp.full((block_q, 1), -jnp.inf, jnp.float32),
        jnp.zeros((block_q, 1), jnp.float32),
        jnp.zeros((block_q, width), jnp.float32),
    )
    live_blocks = (length + block_k - 1) // block_k
    carry = lax.fori_loop(0, live_blocks, cache_step, carry)
    new_blocks = (first + block_q - 1) // block_k + 1
    peak, total, acc = lax.fori_loop(0, new_blocks, new_step, carry)
    o_ref[0] = (acc / total).astype(o_ref.dtype)


def flash_attention(lengths, queries, keys_old, values_old, keys_new, values_new, tokens, scale):
    heads, rows, width = queries.shape
    blocks, _, block_k, _ = keys_old.shape
    slots = blocks * block_k
    block_q = min(BLOCK_Q, tokens)
    grid = (heads, rows // block_q)
    whole_cache = pl.BlockSpec((blocks, 1, block_k, width), lambda c, i, n: (0, c, 0, 0))
    whole_new = pl.BlockSpec((1, tokens, width), lambda c, i, n: (c, 0, 0))
    return pl.pallas_call(
        functools.partial(flash_kernel, tokens, scale),
        out_shape=jax.ShapeDtypeStruct((heads, rows, width), jnp.bfloat16),
        grid_spec=pltpu.PrefetchScalarGridSpec(
            num_scalar_prefetch=1,
            grid=grid,
            in_specs=[
                pl.BlockSpec((1, block_q, width), lambda c, i, n: (c, i, 0)),
                whole_cache, whole_cache, whole_new, whole_new,
            ],
            out_specs=pl.BlockSpec((1, block_q, width), lambda c, i, n: (c, i, 0)),
        ),
        cost_estimate=pl.CostEstimate(
            flops=4 * heads * rows * (slots + tokens) * width,
            transcendentals=heads * rows * (slots + tokens),
            bytes_accessed=2 * width * heads * (2 * rows + 2 * slots + 2 * tokens),
        ),
    )(lengths, queries, keys_old, values_old, keys_new, values_new)


def body(hidden, lengths, key_cache, value_cache, norm_gain, w_query, w_key, w_value, w_out):
    rows_here = hidden.shape[1]
    kv_count = lax.axis_size("kv")
    appended = rows_here * kv_count
    slots = key_cache.shape[1]
    groups = H // KVH
    scale = HD ** (-0.5)
    length = lengths[0]
    q_cols = w_query.shape[1]
    k_cols = w_key.shape[1]
    v_cols = w_value.shape[1]
    heads_here = q_cols // HD
    kv_heads_here = k_cols // HD

    normed = rms_norm(hidden[0].astype(jnp.float32), norm_gain)
    normed_all = lax.all_gather(normed, "kv", axis=0, tiled=True)

    pieces = jnp.concatenate([w_query, w_key, w_value, w_out], axis=1)
    def to_peers(cache):
        return jnp.transpose(
            cache.reshape(slots, kv_count, kv_heads_here, HD), (1, 2, 0, 3)
        )

    cols, keys_old, values_old = gather_req(
        pieces, to_peers(key_cache[0]), to_peers(value_cache[0])
    )
    wq = cols[:, :q_cols]
    wk = cols[:, q_cols:q_cols + k_cols]
    wv = cols[:, q_cols + k_cols:q_cols + k_cols + v_cols]
    wo = cols[:, q_cols + k_cols + v_cols:]

    wo_full = lax.all_gather(wo, "kv", axis=1, tiled=True)

    positions = (length + jnp.arange(appended, dtype=jnp.int32)).astype(jnp.float32)
    half = HD // 2
    frequency = rope_base ** (-(jnp.arange(half, dtype=jnp.float32) * 2.0 / HD))
    angle = positions[:, None] * frequency[None, :]
    cosine = jnp.cos(angle)
    sine = jnp.sin(angle)

    def turn(values):
        first = values[..., :half]
        second = values[..., half:]
        return jnp.concatenate(
            [first * cosine - second * sine, second * cosine + first * sine], axis=-1
        )

    width = normed_all.shape[1]
    proj_q = jnp.einsum(
        "td,dcgh->cgth", normed_all, wq.reshape(width, kv_heads_here, groups, HD),
        preferred_element_type=jnp.float32,
    )
    proj_k = jnp.einsum(
        "td,dch->cth", normed_all, wk.reshape(width, kv_heads_here, HD),
        preferred_element_type=jnp.float32,
    )
    proj_v = jnp.einsum(
        "td,dch->cth", normed_all, wv.reshape(width, kv_heads_here, HD),
        preferred_element_type=jnp.float32,
    )
    query_heads = turn(proj_q).astype(jnp.bfloat16).reshape(kv_heads_here, groups * appended, HD)
    keys_new = turn(proj_k).astype(jnp.bfloat16)
    values_new = proj_v.astype(jnp.bfloat16)

    def to_tokens(values):
        parts = values.reshape(kv_heads_here, kv_count, rows_here, HD)
        got = lax.all_to_all(parts, "kv", split_axis=1, concat_axis=1, tiled=True)
        return jnp.transpose(got, (2, 1, 0, 3)).reshape(rows_here, kv_count * kv_heads_here * HD)

    new_keys = to_tokens(keys_new)
    new_values = to_tokens(values_new)

    contexts = flash_attention(
        lengths, query_heads, keys_old, values_old, keys_new, values_new, appended, scale,
    )
    parts = contexts.reshape(kv_heads_here, groups, kv_count, rows_here, HD)
    got = lax.all_to_all(parts, "kv", split_axis=2, concat_axis=2, tiled=True)
    attended = jnp.einsum(
        "cgsth,scghn->tn", got,
        wo_full.reshape(kv_count, kv_heads_here, groups, HD, wo_full.shape[1]),
        preferred_element_type=jnp.float32,
    ).astype(jnp.bfloat16)
    return (attended[None], new_keys[None], new_values[None])


def solution(mesh):
    return jax.shard_map(
        body,
        mesh=mesh,
        in_specs=(
            P("req", "kv", None),
            P("req"),
            P("req", "kv", None),
            P("req", "kv", None),
            P(),
            P("req", "kv"),
            P("req", "kv"),
            P("req", "kv"),
            P("req", "kv"),
        ),
        out_specs=(P("req", "kv", None), P("req", "kv", None), P("req", "kv", None)),
        check_vma=False,
    )
```

```python
import functools

import jax
import jax.numpy as jnp
from jax import lax
from jax.sharding import PartitionSpec as P
from jax.experimental import pallas as pl
from jax.experimental.pallas import tpu as pltpu

H = 16
KVH = 8
HD = 96


rope_base = 100000.0
masked_score = -1e30


def rms_norm(states, gain):
    mean_square = jnp.mean(states * states, axis=-1, keepdims=True)
    scaled = states * lax.rsqrt(mean_square + 1e-05) * gain.astype(jnp.float32)
    return scaled.astype(jnp.bfloat16)


def rotate(values, positions):
    count = values.shape[0]
    heads = values.shape[1] // HD
    half = HD // 2
    frequency = rope_base ** (-(jnp.arange(half, dtype=jnp.float32) * 2.0 / HD))
    angle = positions[:, None] * frequency[None, :]
    cosine = jnp.cos(angle)[:, None, :]
    sine = jnp.sin(angle)[:, None, :]
    shaped = values.reshape(count, heads, HD)
    first = shaped[..., :half]
    second = shaped[..., half:]
    turned = jnp.concatenate(
        [first * cosine - second * sine, second * cosine + first * sine], axis=-1
    )
    return turned.reshape(count, heads * HD)


Z_RUN = 8
Y_RUN = 2
MESH = pl.DeviceIdType.MESH


def remote(src, dst, send, recv, device):
    return pltpu.make_async_remote_copy(
        src_ref=src, dst_ref=dst, send_sem=send, recv_sem=recv,
        device_id=device, device_id_type=MESH,
    )


def plane_ring_kernel(planes, runs, src_ref, kc_ref, vc_ref, out_ref, kc_out, vc_out, s1_send,
                      s1_recv, r_send, r_recv, l_send, l_recv, local_sem, kv_send, kv_recv, kv_local):
    me = lax.axis_index("req")
    kv = lax.axis_index("kv")
    y_me = lax.rem(me, Y_RUN)
    z_me = lax.rem(me // Y_RUN, runs)
    x_me = me // (Y_RUN * runs)
    q_me = x_me * Y_RUN + y_me
    right_hops = runs // 2
    left_hops = runs - 1 - right_hops

    def plane_peer(q):
        return ((q // Y_RUN) * runs + z_me) * Y_RUN + lax.rem(q, Y_RUN)

    def ring_peer(z):
        return (x_me * runs + z) * Y_RUN + y_me

    z_right = lax.rem(z_me + 1, runs)
    z_left = lax.rem(z_me + runs - 1, runs)

    barrier = pltpu.get_barrier_semaphore()

    def greet(step, carry):
        q = lax.rem(q_me + step, planes)
        pl.semaphore_signal(barrier, inc=1, device_id=(plane_peer(q), kv), device_id_type=MESH)
        return carry

    lax.fori_loop(1, planes, greet, 0)
    pl.semaphore_signal(barrier, inc=1, device_id=(ring_peer(z_right), kv), device_id_type=MESH)
    pl.semaphore_signal(barrier, inc=1, device_id=(ring_peer(z_left), kv), device_id_type=MESH)
    kv_count = lax.axis_size("kv")

    def greet_kv(step, carry):
        peer = lax.rem(kv + step, kv_count)
        pl.semaphore_signal(barrier, inc=1, device_id=(me, peer), device_id_type=MESH)
        return carry

    lax.fori_loop(1, kv_count, greet_kv, 0)
    pl.semaphore_wait(barrier, planes + 1 + kv_count - 1)

    local = pltpu.make_async_copy(src_ref, out_ref.at[z_me, q_me], local_sem)
    local.start()
    caches = ((kc_ref, kc_out), (vc_ref, vc_out))
    local_cache = []
    for which, (cache_src, cache_dst) in enumerate(caches):
        c = pltpu.make_async_copy(cache_src.at[kv], cache_dst.at[kv], kv_local.at[which])
        c.start()
        local_cache.append(c)


    def send(step, carry):
        q = lax.rem(q_me + step, planes)
        remote(src_ref, out_ref.at[z_me, q_me], s1_send.at[step - 1], s1_recv.at[step - 1],
               (plane_peer(q), kv)).start()
        return carry

    lax.fori_loop(1, planes, send, 0)

    def finish(step, carry):
        q = lax.rem(q_me + step, planes)
        source = lax.rem(q_me + planes - step, planes)
        remote(src_ref, out_ref.at[z_me, q_me], s1_send.at[step - 1], s1_recv.at[step - 1],
               (plane_peer(q), kv)).wait_send()
        remote(src_ref, out_ref.at[z_me, source], s1_send.at[step - 1], s1_recv.at[step - 1],
               (plane_peer(source), kv)).wait_recv()
        return carry

    lax.fori_loop(1, planes, finish, 0)
    local.wait()

    split = 2 if planes % 2 == 0 else 1
    share = planes // split

    def ring_copy(z_block, h, send, recv, k, z_to):
        part = out_ref.at[z_block, pl.ds(h * share, share)]
        return remote(part, part, send.at[k, h], recv.at[k, h], (ring_peer(z_to), kv))

    sent = []
    for h in range(split):
        if right_hops > 0:
            c = ring_copy(z_me, h, r_send, r_recv, 0, z_right)
            c.start()
            sent.append(c)
        if left_hops > 0:
            c = ring_copy(z_me, h, l_send, l_recv, 0, z_left)
            c.start()
            sent.append(c)

    def send_kv(step, carry):
        peer = lax.rem(kv + step, kv_count)
        for which, (cache_src, cache_dst) in enumerate(caches):
            remote(cache_src.at[peer], cache_dst.at[kv], kv_send.at[which, step - 1],
                   kv_recv.at[which, step - 1], (me, peer)).start()
        return carry

    lax.fori_loop(1, kv_count, send_kv, 0)
    for k in range(1, max(right_hops, left_hops) + 1):
        for h in range(split):
            if k <= right_hops:
                z_from = lax.rem(z_me + runs - k, runs)
                ring_copy(z_from, h, r_send, r_recv, k - 1, z_right).wait_recv()
                if k < right_hops:
                    c = ring_copy(z_from, h, r_send, r_recv, k, z_right)
                    c.start()
                    sent.append(c)
            if k <= left_hops:
                z_from = lax.rem(z_me + k, runs)
                ring_copy(z_from, h, l_send, l_recv, k - 1, z_left).wait_recv()
                if k < left_hops:
                    c = ring_copy(z_from, h, l_send, l_recv, k, z_left)
                    c.start()
                    sent.append(c)
    for c in sent:
        c.wait_send()

    def finish_kv(step, carry):
        peer = lax.rem(kv + step, kv_count)
        source = lax.rem(kv + kv_count - step, kv_count)
        for which, (cache_src, cache_dst) in enumerate(caches):
            remote(cache_src.at[peer], cache_dst.at[kv], kv_send.at[which, step - 1],
                   kv_recv.at[which, step - 1], (me, peer)).wait_send()
            remote(cache_src.at[kv], cache_dst.at[source], kv_send.at[which, step - 1],
                   kv_recv.at[which, step - 1], (me, source)).wait_recv()
        return carry

    lax.fori_loop(1, kv_count, finish_kv, 0)
    for c in local_cache:
        c.wait()


def gather_req(piece, keys_send, values_send):
    count = lax.axis_size("req")
    kv_count = lax.axis_size("kv")
    runs = min(Z_RUN, count // Y_RUN)
    planes = count // runs
    rows, width = piece.shape
    hops = max(runs - 1, 1)
    anywhere = pl.BlockSpec(memory_space=pl.ANY)
    gathered, keys_old, values_old = pl.pallas_call(
        functools.partial(plane_ring_kernel, planes, runs),
        out_shape=(
            jax.ShapeDtypeStruct((runs, planes, rows, width), piece.dtype),
            jax.ShapeDtypeStruct(keys_send.shape, keys_send.dtype),
            jax.ShapeDtypeStruct(values_send.shape, values_send.dtype),
        ),
        in_specs=[anywhere, anywhere, anywhere],
        out_specs=(anywhere, anywhere, anywhere),
        scratch_shapes=[
            pltpu.SemaphoreType.DMA((planes - 1,)),
            pltpu.SemaphoreType.DMA((planes - 1,)),
            pltpu.SemaphoreType.DMA((hops, 2)),
            pltpu.SemaphoreType.DMA((hops, 2)),
            pltpu.SemaphoreType.DMA((hops, 2)),
            pltpu.SemaphoreType.DMA((hops, 2)),
            pltpu.SemaphoreType.DMA,
            pltpu.SemaphoreType.DMA((2, kv_count - 1)),
            pltpu.SemaphoreType.DMA((2, kv_count - 1)),
            pltpu.SemaphoreType.DMA((2,)),
        ],
        compiler_params=pltpu.CompilerParams(collective_id=0, has_side_effects=True),
    )(piece, keys_send, values_send)
    x_count = planes // Y_RUN
    ordered = jnp.transpose(
        gathered.reshape(runs, x_count, Y_RUN, rows, width), (1, 0, 2, 3, 4)
    )
    return ordered.reshape(count * rows, width), keys_old, values_old


BLOCK_Q = 512
BLOCK_K = 512


def flash_kernel(tokens, scale, len_ref, q_ref, kc_ref, vc_ref, kn_ref, vn_ref, o_ref):
    block_q = q_ref.shape[1]
    block_k = kc_ref.shape[2]
    width = q_ref.shape[2]
    i = pl.program_id(1)
    length = len_ref[0]
    first = lax.rem(i * block_q, tokens)
    q = q_ref[0]
    query_index = first + lax.broadcasted_iota(jnp.int32, (block_q, block_k), 0)
    key_offset = lax.broadcasted_iota(jnp.int32, (block_q, block_k), 1)

    def step(keys, values, visible, carry):
        peak, total, acc = carry
        score = lax.dot_general(
            q, keys, (((1,), (1,)), ((), ())), preferred_element_type=jnp.float32
        ) * scale
        score = jnp.where(visible, score, masked_score)
        new_peak = jnp.maximum(peak, jnp.max(score, axis=1, keepdims=True))
        alpha = jnp.exp(peak - new_peak)
        weights = jnp.where(visible, jnp.exp(score - new_peak), 0.0)
        total = alpha * total + jnp.sum(weights, axis=1, keepdims=True)
        acc = alpha * acc + jnp.dot(
            weights.astype(jnp.bfloat16), values, preferred_element_type=jnp.float32
        )
        return new_peak, total, acc

    def cache_step(block, carry):
        start = pl.multiple_of(block * block_k, block_k)
        keys = kc_ref[block, 0]
        values = vc_ref[block, 0]
        visible = start + key_offset < length
        return step(keys, values, visible, carry)

    def new_step(block, carry):
        start = pl.multiple_of(block * block_k, block_k)
        keys = kn_ref[0, pl.ds(start, block_k), :]
        values = vn_ref[0, pl.ds(start, block_k), :]
        visible = start + key_offset <= query_index
        return step(keys, values, visible, carry)

    carry = (
        jnp.full((block_q, 1), -jnp.inf, jnp.float32),
        jnp.zeros((block_q, 1), jnp.float32),
        jnp.zeros((block_q, width), jnp.float32),
    )
    live_blocks = (length + block_k - 1) // block_k
    carry = lax.fori_loop(0, live_blocks, cache_step, carry)
    new_blocks = (first + block_q - 1) // block_k + 1
    peak, total, acc = lax.fori_loop(0, new_blocks, new_step, carry)
    o_ref[0] = (acc / total).astype(o_ref.dtype)


def flash_attention(lengths, queries, keys_old, values_old, keys_new, values_new, tokens, scale):
    heads, rows, width = queries.shape
    blocks, _, block_k, _ = keys_old.shape
    slots = blocks * block_k
    block_q = min(BLOCK_Q, tokens)
    grid = (heads, rows // block_q)
    whole_cache = pl.BlockSpec((blocks, 1, block_k, width), lambda c, i, n: (0, c, 0, 0))
    whole_new = pl.BlockSpec((1, tokens, width), lambda c, i, n: (c, 0, 0))
    return pl.pallas_call(
        functools.partial(flash_kernel, tokens, scale),
        out_shape=jax.ShapeDtypeStruct((heads, rows, width), jnp.bfloat16),
        grid_spec=pltpu.PrefetchScalarGridSpec(
            num_scalar_prefetch=1,
            grid=grid,
            in_specs=[
                pl.BlockSpec((1, block_q, width), lambda c, i, n: (c, i, 0)),
                whole_cache, whole_cache, whole_new, whole_new,
            ],
            out_specs=pl.BlockSpec((1, block_q, width), lambda c, i, n: (c, i, 0)),
        ),
        cost_estimate=pl.CostEstimate(
            flops=4 * heads * rows * (slots + tokens) * width,
            transcendentals=heads * rows * (slots + tokens),
            bytes_accessed=2 * width * heads * (2 * rows + 2 * slots + 2 * tokens),
        ),
    )(lengths, queries, keys_old, values_old, keys_new, values_new)


def body(hidden, lengths, key_cache, value_cache, norm_gain, w_query, w_key, w_value, w_out):
    rows_here = hidden.shape[1]
    kv_count = lax.axis_size("kv")
    appended = rows_here * kv_count
    slots = key_cache.shape[1]
    groups = H // KVH
    scale = HD ** (-0.5)
    length = lengths[0]
    q_cols = w_query.shape[1]
    k_cols = w_key.shape[1]
    v_cols = w_value.shape[1]
    heads_here = q_cols // HD
    kv_heads_here = k_cols // HD

    normed = rms_norm(hidden[0].astype(jnp.float32), norm_gain)
    normed_all = lax.all_gather(normed, "kv", axis=0, tiled=True)

    pieces = jnp.concatenate([w_query, w_key, w_value, w_out], axis=1)
    def to_peers(cache):
        return jnp.transpose(
            cache.reshape(slots, kv_count, kv_heads_here, HD), (1, 2, 0, 3)
        )

    cols, keys_old, values_old = gather_req(
        pieces, to_peers(key_cache[0]), to_peers(value_cache[0])
    )
    wq = cols[:, :q_cols]
    wk = cols[:, q_cols:q_cols + k_cols]
    wv = cols[:, q_cols + k_cols:q_cols + k_cols + v_cols]
    wo = cols[:, q_cols + k_cols + v_cols:]

    wo_full = lax.all_gather(wo, "kv", axis=1, tiled=True)

    positions = (length + jnp.arange(appended, dtype=jnp.int32)).astype(jnp.float32)
    half = HD // 2
    frequency = rope_base ** (-(jnp.arange(half, dtype=jnp.float32) * 2.0 / HD))
    angle = positions[:, None] * frequency[None, :]
    cosine = jnp.cos(angle)
    sine = jnp.sin(angle)

    def turn(values):
        first = values[..., :half]
        second = values[..., half:]
        return jnp.concatenate(
            [first * cosine - second * sine, second * cosine + first * sine], axis=-1
        )

    width = normed_all.shape[1]
    proj_q = jnp.einsum(
        "td,dcgh->cgth", normed_all, wq.reshape(width, kv_heads_here, groups, HD),
        preferred_element_type=jnp.float32,
    )
    proj_k = jnp.einsum(
        "td,dch->cth", normed_all, wk.reshape(width, kv_heads_here, HD),
        preferred_element_type=jnp.float32,
    )
    proj_v = jnp.einsum(
        "td,dch->cth", normed_all, wv.reshape(width, kv_heads_here, HD),
        preferred_element_type=jnp.float32,
    )
    query_heads = turn(proj_q).astype(jnp.bfloat16).reshape(kv_heads_here, groups * appended, HD)
    keys_new = turn(proj_k).astype(jnp.bfloat16)
    values_new = proj_v.astype(jnp.bfloat16)

    def to_tokens(values):
        parts = values.reshape(kv_heads_here, kv_count, rows_here, HD)
        got = lax.all_to_all(parts, "kv", split_axis=1, concat_axis=1, tiled=True)
        return jnp.transpose(got, (2, 1, 0, 3)).reshape(rows_here, kv_count * kv_heads_here * HD)

    new_keys = to_tokens(keys_new)
    new_values = to_tokens(values_new)

    contexts = flash_attention(
        lengths, query_heads, keys_old, values_old, keys_new, values_new, appended, scale,
    )
    parts = contexts.reshape(kv_heads_here, groups, kv_count, rows_here, HD)
    got = lax.all_to_all(parts, "kv", split_axis=2, concat_axis=2, tiled=True)
    attended = jnp.einsum(
        "cgsth,scghn->tn", got,
        wo_full.reshape(kv_count, kv_heads_here, groups, HD, wo_full.shape[1]),
        preferred_element_type=jnp.float32,
    ).astype(jnp.bfloat16)
    return (attended[None], new_keys[None], new_values[None])


def solution(mesh):
    return jax.shard_map(
        body,
        mesh=mesh,
        in_specs=(
            P("req", "kv", None),
            P("req"),
            P("req", "kv", None),
            P("req", "kv", None),
            P(),
            P("req", "kv"),
            P("req", "kv"),
            P("req", "kv"),
            P("req", "kv"),
        ),
        out_specs=(P("req", "kv", None), P("req", "kv", None), P("req", "kv", None)),
        check_vma=False,
    )
```

```python
import functools

import jax
import jax.numpy as jnp
from jax import lax
from jax.sharding import PartitionSpec as P
from jax.experimental import pallas as pl
from jax.experimental.pallas import tpu as pltpu

H = 16
KVH = 8
HD = 96


rope_base = 100000.0
masked_score = -1e30


def rms_norm(states, gain):
    mean_square = jnp.mean(states * states, axis=-1, keepdims=True)
    scaled = states * lax.rsqrt(mean_square + 1e-05) * gain.astype(jnp.float32)
    return scaled.astype(jnp.bfloat16)


def rotate(values, positions):
    count = values.shape[0]
    heads = values.shape[1] // HD
    half = HD // 2
    frequency = rope_base ** (-(jnp.arange(half, dtype=jnp.float32) * 2.0 / HD))
    angle = positions[:, None] * frequency[None, :]
    cosine = jnp.cos(angle)[:, None, :]
    sine = jnp.sin(angle)[:, None, :]
    shaped = values.reshape(count, heads, HD)
    first = shaped[..., :half]
    second = shaped[..., half:]
    turned = jnp.concatenate(
        [first * cosine - second * sine, second * cosine + first * sine], axis=-1
    )
    return turned.reshape(count, heads * HD)


Z_RUN = 8
Y_RUN = 2
MESH = pl.DeviceIdType.MESH


def remote(src, dst, send, recv, device):
    return pltpu.make_async_remote_copy(
        src_ref=src, dst_ref=dst, send_sem=send, recv_sem=recv,
        device_id=device, device_id_type=MESH,
    )


def plane_ring_kernel(planes, runs, src_ref, kc_ref, vc_ref, out_ref, kc_out, vc_out, s1_send,
                      s1_recv, r_send, r_recv, l_send, l_recv, local_sem, kv_send, kv_recv, kv_local):
    me = lax.axis_index("req")
    kv = lax.axis_index("kv")
    y_me = lax.rem(me, Y_RUN)
    z_me = lax.rem(me // Y_RUN, runs)
    x_me = me // (Y_RUN * runs)
    q_me = x_me * Y_RUN + y_me
    right_hops = runs // 2
    left_hops = runs - 1 - right_hops

    def plane_peer(q):
        return ((q // Y_RUN) * runs + z_me) * Y_RUN + lax.rem(q, Y_RUN)

    def ring_peer(z):
        return (x_me * runs + z) * Y_RUN + y_me

    z_right = lax.rem(z_me + 1, runs)
    z_left = lax.rem(z_me + runs - 1, runs)

    barrier = pltpu.get_barrier_semaphore()

    def greet(step, carry):
        q = lax.rem(q_me + step, planes)
        pl.semaphore_signal(barrier, inc=1, device_id=(plane_peer(q), kv), device_id_type=MESH)
        return carry

    lax.fori_loop(1, planes, greet, 0)
    pl.semaphore_signal(barrier, inc=1, device_id=(ring_peer(z_right), kv), device_id_type=MESH)
    pl.semaphore_signal(barrier, inc=1, device_id=(ring_peer(z_left), kv), device_id_type=MESH)
    kv_count = lax.axis_size("kv")

    def greet_kv(step, carry):
        peer = lax.rem(kv + step, kv_count)
        pl.semaphore_signal(barrier, inc=1, device_id=(me, peer), device_id_type=MESH)
        return carry

    lax.fori_loop(1, kv_count, greet_kv, 0)
    pl.semaphore_wait(barrier, planes + 1 + kv_count - 1)

    local = pltpu.make_async_copy(src_ref, out_ref.at[z_me, q_me], local_sem)
    local.start()
    caches = ((kc_ref, kc_out), (vc_ref, vc_out))
    local_cache = []
    for which, (cache_src, cache_dst) in enumerate(caches):
        c = pltpu.make_async_copy(cache_src.at[kv], cache_dst.at[kv], kv_local.at[which])
        c.start()
        local_cache.append(c)


    def send(step, carry):
        q = lax.rem(q_me + step, planes)
        remote(src_ref, out_ref.at[z_me, q_me], s1_send.at[step - 1], s1_recv.at[step - 1],
               (plane_peer(q), kv)).start()
        return carry

    lax.fori_loop(1, planes, send, 0)

    def finish(step, carry):
        q = lax.rem(q_me + step, planes)
        source = lax.rem(q_me + planes - step, planes)
        remote(src_ref, out_ref.at[z_me, q_me], s1_send.at[step - 1], s1_recv.at[step - 1],
               (plane_peer(q), kv)).wait_send()
        remote(src_ref, out_ref.at[z_me, source], s1_send.at[step - 1], s1_recv.at[step - 1],
               (plane_peer(source), kv)).wait_recv()
        return carry

    lax.fori_loop(1, planes, finish, 0)
    local.wait()

    split = 2 if planes % 2 == 0 else 1
    share = planes // split

    def ring_copy(z_block, h, send, recv, k, z_to):
        part = out_ref.at[z_block, pl.ds(h * share, share)]
        return remote(part, part, send.at[k, h], recv.at[k, h], (ring_peer(z_to), kv))

    sent = []
    for h in range(split):
        if right_hops > 0:
            c = ring_copy(z_me, h, r_send, r_recv, 0, z_right)
            c.start()
            sent.append(c)
        if left_hops > 0:
            c = ring_copy(z_me, h, l_send, l_recv, 0, z_left)
            c.start()
            sent.append(c)

    def send_kv(step, carry):
        peer = lax.rem(kv + step, kv_count)
        for which, (cache_src, cache_dst) in enumerate(caches):
            remote(cache_src.at[peer], cache_dst.at[kv], kv_send.at[which, step - 1],
                   kv_recv.at[which, step - 1], (me, peer)).start()
        return carry

    lax.fori_loop(1, kv_count, send_kv, 0)
    for k in range(1, max(right_hops, left_hops) + 1):
        for h in range(split):
            if k <= right_hops:
                z_from = lax.rem(z_me + runs - k, runs)
                ring_copy(z_from, h, r_send, r_recv, k - 1, z_right).wait_recv()
                if k < right_hops:
                    c = ring_copy(z_from, h, r_send, r_recv, k, z_right)
                    c.start()
                    sent.append(c)
            if k <= left_hops:
                z_from = lax.rem(z_me + k, runs)
                ring_copy(z_from, h, l_send, l_recv, k - 1, z_left).wait_recv()
                if k < left_hops:
                    c = ring_copy(z_from, h, l_send, l_recv, k, z_left)
                    c.start()
                    sent.append(c)
    for c in sent:
        c.wait_send()

    def finish_kv(step, carry):
        peer = lax.rem(kv + step, kv_count)
        source = lax.rem(kv + kv_count - step, kv_count)
        for which, (cache_src, cache_dst) in enumerate(caches):
            remote(cache_src.at[peer], cache_dst.at[kv], kv_send.at[which, step - 1],
                   kv_recv.at[which, step - 1], (me, peer)).wait_send()
            remote(cache_src.at[kv], cache_dst.at[source], kv_send.at[which, step - 1],
                   kv_recv.at[which, step - 1], (me, source)).wait_recv()
        return carry

    lax.fori_loop(1, kv_count, finish_kv, 0)
    for c in local_cache:
        c.wait()


def gather_req(piece, keys_send, values_send):
    count = lax.axis_size("req")
    kv_count = lax.axis_size("kv")
    runs = min(Z_RUN, count // Y_RUN)
    planes = count // runs
    rows, width = piece.shape
    hops = max(runs - 1, 1)
    anywhere = pl.BlockSpec(memory_space=pl.ANY)
    gathered, keys_old, values_old = pl.pallas_call(
        functools.partial(plane_ring_kernel, planes, runs),
        out_shape=(
            jax.ShapeDtypeStruct((runs, planes, rows, width), piece.dtype),
            jax.ShapeDtypeStruct(keys_send.shape, keys_send.dtype),
            jax.ShapeDtypeStruct(values_send.shape, values_send.dtype),
        ),
        in_specs=[anywhere, anywhere, anywhere],
        out_specs=(anywhere, anywhere, anywhere),
        scratch_shapes=[
            pltpu.SemaphoreType.DMA((planes - 1,)),
            pltpu.SemaphoreType.DMA((planes - 1,)),
            pltpu.SemaphoreType.DMA((hops, 2)),
            pltpu.SemaphoreType.DMA((hops, 2)),
            pltpu.SemaphoreType.DMA((hops, 2)),
            pltpu.SemaphoreType.DMA((hops, 2)),
            pltpu.SemaphoreType.DMA,
            pltpu.SemaphoreType.DMA((2, kv_count - 1)),
            pltpu.SemaphoreType.DMA((2, kv_count - 1)),
            pltpu.SemaphoreType.DMA((2,)),
        ],
        compiler_params=pltpu.CompilerParams(collective_id=0, has_side_effects=True),
    )(piece, keys_send, values_send)
    x_count = planes // Y_RUN
    ordered = jnp.transpose(
        gathered.reshape(runs, x_count, Y_RUN, rows, width), (1, 0, 2, 3, 4)
    )
    return ordered.reshape(count * rows, width), keys_old, values_old


BLOCK_Q = 512
BLOCK_K = 512


def flash_kernel(tokens, scale, len_ref, q_ref, kc_ref, vc_ref, kn_ref, vn_ref, o_ref):
    block_q = q_ref.shape[1]
    block_k = kc_ref.shape[2]
    width = q_ref.shape[2]
    i = pl.program_id(0)
    length = len_ref[0]
    first = lax.rem(i * block_q, tokens)
    q = q_ref[0]
    query_index = first + lax.broadcasted_iota(jnp.int32, (block_q, block_k), 0)
    key_offset = lax.broadcasted_iota(jnp.int32, (block_q, block_k), 1)

    def step(keys, values, visible, carry):
        peak, total, acc = carry
        score = lax.dot_general(
            q, keys, (((1,), (1,)), ((), ())), preferred_element_type=jnp.float32
        ) * scale
        if visible is not None:
            score = jnp.where(visible, score, masked_score)
        new_peak = jnp.maximum(peak, jnp.max(score, axis=1, keepdims=True))
        alpha = jnp.exp(peak - new_peak)
        weights = jnp.exp(score - new_peak)
        if visible is not None:
            weights = jnp.where(visible, weights, 0.0)
        total = alpha * total + jnp.sum(weights, axis=1, keepdims=True)
        acc = alpha * acc + jnp.dot(
            weights.astype(jnp.bfloat16), values, preferred_element_type=jnp.float32
        )
        return new_peak, total, acc

    def cache_full(block, carry):
        return step(kc_ref[block, 0], vc_ref[block, 0], None, carry)

    def cache_part(block, carry):
        start = block * block_k
        visible = start + key_offset < length
        return step(kc_ref[block, 0], vc_ref[block, 0], visible, carry)

    def new_full(block, carry):
        start = pl.multiple_of(block * block_k, block_k)
        keys = kn_ref[0, pl.ds(start, block_k), :]
        values = vn_ref[0, pl.ds(start, block_k), :]
        return step(keys, values, None, carry)

    def new_part(block, carry):
        start = pl.multiple_of(block * block_k, block_k)
        keys = kn_ref[0, pl.ds(start, block_k), :]
        values = vn_ref[0, pl.ds(start, block_k), :]
        visible = start + key_offset <= query_index
        return step(keys, values, visible, carry)

    carry = (
        jnp.full((block_q, 1), -jnp.inf, jnp.float32),
        jnp.zeros((block_q, 1), jnp.float32),
        jnp.zeros((block_q, width), jnp.float32),
    )
    full_blocks = length // block_k
    live_blocks = (length + block_k - 1) // block_k
    carry = lax.fori_loop(0, full_blocks, cache_full, carry)
    carry = lax.fori_loop(full_blocks, live_blocks, cache_part, carry)
    clear_blocks = first // block_k
    new_blocks = (first + block_q - 1) // block_k + 1
    carry = lax.fori_loop(0, clear_blocks, new_full, carry)
    peak, total, acc = lax.fori_loop(clear_blocks, new_blocks, new_part, carry)
    o_ref[...] = (acc / total).astype(o_ref.dtype)


def flash_attention(lengths, queries, keys_old, values_old, keys_new, values_new, tokens, scale,
                    head):
    heads, rows, width = queries.shape
    blocks, _, block_k, _ = keys_old.shape
    slots = blocks * block_k
    block_q = min(BLOCK_Q, tokens)
    grid = (rows // block_q,)
    whole_cache = pl.BlockSpec((blocks, 1, block_k, width), lambda i, n: (0, head, 0, 0))
    whole_new = pl.BlockSpec((1, tokens, width), lambda i, n: (head, 0, 0))
    return pl.pallas_call(
        functools.partial(flash_kernel, tokens, scale),
        out_shape=jax.ShapeDtypeStruct((rows, width), jnp.bfloat16),
        grid_spec=pltpu.PrefetchScalarGridSpec(
            num_scalar_prefetch=1,
            grid=grid,
            in_specs=[
                pl.BlockSpec((1, block_q, width), lambda i, n: (head, i, 0)),
                whole_cache, whole_cache, whole_new, whole_new,
            ],
            out_specs=pl.BlockSpec((block_q, width), lambda i, n: (i, 0)),
        ),
        cost_estimate=pl.CostEstimate(
            flops=4 * rows * (slots + tokens) * width,
            transcendentals=rows * (slots + tokens),
            bytes_accessed=2 * width * (2 * rows + 2 * slots + 2 * tokens),
        ),
    )(lengths, queries, keys_old, values_old, keys_new, values_new)


def body(hidden, lengths, key_cache, value_cache, norm_gain, w_query, w_key, w_value, w_out):
    rows_here = hidden.shape[1]
    kv_count = lax.axis_size("kv")
    appended = rows_here * kv_count
    slots = key_cache.shape[1]
    groups = H // KVH
    scale = HD ** (-0.5)
    length = lengths[0]
    q_cols = w_query.shape[1]
    k_cols = w_key.shape[1]
    v_cols = w_value.shape[1]
    heads_here = q_cols // HD
    kv_heads_here = k_cols // HD

    normed = rms_norm(hidden[0].astype(jnp.float32), norm_gain)
    normed_all = lax.all_gather(normed, "kv", axis=0, tiled=True)

    pieces = jnp.concatenate([w_query, w_key, w_value, w_out], axis=1)
    def to_peers(cache):
        return jnp.transpose(
            cache.reshape(slots, kv_count, kv_heads_here, HD), (1, 2, 0, 3)
        )

    cols, keys_old, values_old = gather_req(
        pieces, to_peers(key_cache[0]), to_peers(value_cache[0])
    )
    wq = cols[:, :q_cols]
    wk = cols[:, q_cols:q_cols + k_cols]
    wv = cols[:, q_cols + k_cols:q_cols + k_cols + v_cols]
    wo = cols[:, q_cols + k_cols + v_cols:]

    wo_full = lax.all_gather(wo, "kv", axis=1, tiled=True)

    positions = (length + jnp.arange(appended, dtype=jnp.int32)).astype(jnp.float32)
    half = HD // 2
    frequency = rope_base ** (-(jnp.arange(half, dtype=jnp.float32) * 2.0 / HD))
    angle = positions[:, None] * frequency[None, :]
    cosine = jnp.cos(angle)
    sine = jnp.sin(angle)

    def turn(values):
        first = values[..., :half]
        second = values[..., half:]
        return jnp.concatenate(
            [first * cosine - second * sine, second * cosine + first * sine], axis=-1
        )

    width = normed_all.shape[1]
    proj_q = jnp.einsum(
        "td,dcgh->cgth", normed_all, wq.reshape(width, kv_heads_here, groups, HD),
        preferred_element_type=jnp.float32,
    )
    proj_k = jnp.einsum(
        "td,dch->cth", normed_all, wk.reshape(width, kv_heads_here, HD),
        preferred_element_type=jnp.float32,
    )
    proj_v = jnp.einsum(
        "td,dch->cth", normed_all, wv.reshape(width, kv_heads_here, HD),
        preferred_element_type=jnp.float32,
    )
    query_heads = turn(proj_q).astype(jnp.bfloat16).reshape(kv_heads_here, groups * appended, HD)
    keys_new = turn(proj_k).astype(jnp.bfloat16)
    values_new = proj_v.astype(jnp.bfloat16)

    def to_tokens(values):
        parts = values.reshape(kv_heads_here, kv_count, rows_here, HD)
        got = lax.all_to_all(parts, "kv", split_axis=1, concat_axis=1, tiled=True)
        return jnp.transpose(got, (2, 1, 0, 3)).reshape(rows_here, kv_count * kv_heads_here * HD)

    new_keys = to_tokens(keys_new)
    new_values = to_tokens(values_new)

    wo_heads = wo_full.reshape(kv_count, kv_heads_here, groups, HD, wo_full.shape[1])
    attended = None
    for head in range(kv_heads_here):
        context = flash_attention(
            lengths, query_heads, keys_old, values_old, keys_new, values_new, appended, scale,
            head,
        )
        parts = context.reshape(groups, kv_count, rows_here, HD)
        got = lax.all_to_all(parts, "kv", split_axis=1, concat_axis=1, tiled=True)
        partial = jnp.einsum(
            "gsth,sghn->tn", got, wo_heads[:, head], preferred_element_type=jnp.float32
        )
        attended = partial if attended is None else attended + partial
    attended = attended.astype(jnp.bfloat16)
    return (attended[None], new_keys[None], new_values[None])


def solution(mesh):
    return jax.shard_map(
        body,
        mesh=mesh,
        in_specs=(
            P("req", "kv", None),
            P("req"),
            P("req", "kv", None),
            P("req", "kv", None),
            P(),
            P("req", "kv"),
            P("req", "kv"),
            P("req", "kv"),
            P("req", "kv"),
        ),
        out_specs=(P("req", "kv", None), P("req", "kv", None), P("req", "kv", None)),
        check_vma=False,
    )
```

```python
import functools

import jax
import jax.numpy as jnp
from jax import lax
from jax.sharding import PartitionSpec as P
from jax.experimental import pallas as pl
from jax.experimental.pallas import tpu as pltpu

H = 16
KVH = 8
HD = 96


rope_base = 100000.0
masked_score = -1e30


def rms_norm(states, gain):
    mean_square = jnp.mean(states * states, axis=-1, keepdims=True)
    scaled = states * lax.rsqrt(mean_square + 1e-05) * gain.astype(jnp.float32)
    return scaled.astype(jnp.bfloat16)


def rotate(values, positions):
    count = values.shape[0]
    heads = values.shape[1] // HD
    half = HD // 2
    frequency = rope_base ** (-(jnp.arange(half, dtype=jnp.float32) * 2.0 / HD))
    angle = positions[:, None] * frequency[None, :]
    cosine = jnp.cos(angle)[:, None, :]
    sine = jnp.sin(angle)[:, None, :]
    shaped = values.reshape(count, heads, HD)
    first = shaped[..., :half]
    second = shaped[..., half:]
    turned = jnp.concatenate(
        [first * cosine - second * sine, second * cosine + first * sine], axis=-1
    )
    return turned.reshape(count, heads * HD)


Z_RUN = 8
Y_RUN = 2
MESH = pl.DeviceIdType.MESH


def remote(src, dst, send, recv, device):
    return pltpu.make_async_remote_copy(
        src_ref=src, dst_ref=dst, send_sem=send, recv_sem=recv,
        device_id=device, device_id_type=MESH,
    )


def plane_ring_kernel(planes, runs, src_ref, kc_ref, vc_ref, out_ref, kc_out, vc_out, s1_send,
                      s1_recv, r_send, r_recv, l_send, l_recv, local_sem, kv_send, kv_recv, kv_local):
    me = lax.axis_index("req")
    kv = lax.axis_index("kv")
    y_me = lax.rem(me, Y_RUN)
    z_me = lax.rem(me // Y_RUN, runs)
    x_me = me // (Y_RUN * runs)
    q_me = x_me * Y_RUN + y_me
    right_hops = runs // 2
    left_hops = runs - 1 - right_hops

    def plane_peer(q):
        return ((q // Y_RUN) * runs + z_me) * Y_RUN + lax.rem(q, Y_RUN)

    def ring_peer(z):
        return (x_me * runs + z) * Y_RUN + y_me

    z_right = lax.rem(z_me + 1, runs)
    z_left = lax.rem(z_me + runs - 1, runs)

    barrier = pltpu.get_barrier_semaphore()

    def greet(step, carry):
        q = lax.rem(q_me + step, planes)
        pl.semaphore_signal(barrier, inc=1, device_id=(plane_peer(q), kv), device_id_type=MESH)
        return carry

    lax.fori_loop(1, planes, greet, 0)
    pl.semaphore_signal(barrier, inc=1, device_id=(ring_peer(z_right), kv), device_id_type=MESH)
    pl.semaphore_signal(barrier, inc=1, device_id=(ring_peer(z_left), kv), device_id_type=MESH)
    kv_count = lax.axis_size("kv")

    def greet_kv(step, carry):
        peer = lax.rem(kv + step, kv_count)
        pl.semaphore_signal(barrier, inc=1, device_id=(me, peer), device_id_type=MESH)
        return carry

    lax.fori_loop(1, kv_count, greet_kv, 0)
    pl.semaphore_wait(barrier, planes + 1 + kv_count - 1)

    local = pltpu.make_async_copy(src_ref, out_ref.at[z_me, q_me], local_sem)
    local.start()
    caches = ((kc_ref, kc_out), (vc_ref, vc_out))
    local_cache = []
    for which, (cache_src, cache_dst) in enumerate(caches):
        c = pltpu.make_async_copy(cache_src.at[kv], cache_dst.at[kv], kv_local.at[which])
        c.start()
        local_cache.append(c)


    def send(step, carry):
        q = lax.rem(q_me + step, planes)
        remote(src_ref, out_ref.at[z_me, q_me], s1_send.at[step - 1], s1_recv.at[step - 1],
               (plane_peer(q), kv)).start()
        return carry

    lax.fori_loop(1, planes, send, 0)

    def finish(step, carry):
        q = lax.rem(q_me + step, planes)
        source = lax.rem(q_me + planes - step, planes)
        remote(src_ref, out_ref.at[z_me, q_me], s1_send.at[step - 1], s1_recv.at[step - 1],
               (plane_peer(q), kv)).wait_send()
        remote(src_ref, out_ref.at[z_me, source], s1_send.at[step - 1], s1_recv.at[step - 1],
               (plane_peer(source), kv)).wait_recv()
        return carry

    lax.fori_loop(1, planes, finish, 0)
    local.wait()

    split = 2 if planes % 2 == 0 else 1
    share = planes // split

    def ring_copy(z_block, h, send, recv, k, z_to):
        part = out_ref.at[z_block, pl.ds(h * share, share)]
        return remote(part, part, send.at[k, h], recv.at[k, h], (ring_peer(z_to), kv))

    sent = []
    for h in range(split):
        if right_hops > 0:
            c = ring_copy(z_me, h, r_send, r_recv, 0, z_right)
            c.start()
            sent.append(c)
        if left_hops > 0:
            c = ring_copy(z_me, h, l_send, l_recv, 0, z_left)
            c.start()
            sent.append(c)

    def send_kv(step, carry):
        peer = lax.rem(kv + step, kv_count)
        for which, (cache_src, cache_dst) in enumerate(caches):
            remote(cache_src.at[peer], cache_dst.at[kv], kv_send.at[which, step - 1],
                   kv_recv.at[which, step - 1], (me, peer)).start()
        return carry

    lax.fori_loop(1, kv_count, send_kv, 0)
    for k in range(1, max(right_hops, left_hops) + 1):
        for h in range(split):
            if k <= right_hops:
                z_from = lax.rem(z_me + runs - k, runs)
                ring_copy(z_from, h, r_send, r_recv, k - 1, z_right).wait_recv()
                if k < right_hops:
                    c = ring_copy(z_from, h, r_send, r_recv, k, z_right)
                    c.start()
                    sent.append(c)
            if k <= left_hops:
                z_from = lax.rem(z_me + k, runs)
                ring_copy(z_from, h, l_send, l_recv, k - 1, z_left).wait_recv()
                if k < left_hops:
                    c = ring_copy(z_from, h, l_send, l_recv, k, z_left)
                    c.start()
                    sent.append(c)
    for c in sent:
        c.wait_send()

    def finish_kv(step, carry):
        peer = lax.rem(kv + step, kv_count)
        source = lax.rem(kv + kv_count - step, kv_count)
        for which, (cache_src, cache_dst) in enumerate(caches):
            remote(cache_src.at[peer], cache_dst.at[kv], kv_send.at[which, step - 1],
                   kv_recv.at[which, step - 1], (me, peer)).wait_send()
            remote(cache_src.at[kv], cache_dst.at[source], kv_send.at[which, step - 1],
                   kv_recv.at[which, step - 1], (me, source)).wait_recv()
        return carry

    lax.fori_loop(1, kv_count, finish_kv, 0)
    for c in local_cache:
        c.wait()


def gather_req(piece, keys_send, values_send):
    count = lax.axis_size("req")
    kv_count = lax.axis_size("kv")
    runs = min(Z_RUN, count // Y_RUN)
    planes = count // runs
    rows, width = piece.shape
    hops = max(runs - 1, 1)
    anywhere = pl.BlockSpec(memory_space=pl.ANY)
    gathered, keys_old, values_old = pl.pallas_call(
        functools.partial(plane_ring_kernel, planes, runs),
        out_shape=(
            jax.ShapeDtypeStruct((runs, planes, rows, width), piece.dtype),
            jax.ShapeDtypeStruct(keys_send.shape, keys_send.dtype),
            jax.ShapeDtypeStruct(values_send.shape, values_send.dtype),
        ),
        in_specs=[anywhere, anywhere, anywhere],
        out_specs=(anywhere, anywhere, anywhere),
        scratch_shapes=[
            pltpu.SemaphoreType.DMA((planes - 1,)),
            pltpu.SemaphoreType.DMA((planes - 1,)),
            pltpu.SemaphoreType.DMA((hops, 2)),
            pltpu.SemaphoreType.DMA((hops, 2)),
            pltpu.SemaphoreType.DMA((hops, 2)),
            pltpu.SemaphoreType.DMA((hops, 2)),
            pltpu.SemaphoreType.DMA,
            pltpu.SemaphoreType.DMA((2, kv_count - 1)),
            pltpu.SemaphoreType.DMA((2, kv_count - 1)),
            pltpu.SemaphoreType.DMA((2,)),
        ],
        compiler_params=pltpu.CompilerParams(collective_id=0, has_side_effects=True),
    )(piece, keys_send, values_send)
    x_count = planes // Y_RUN
    ordered = jnp.transpose(
        gathered.reshape(runs, x_count, Y_RUN, rows, width), (1, 0, 2, 3, 4)
    )
    return ordered.reshape(count * rows, width), keys_old, values_old


BLOCK_Q = 512
BLOCK_K = 512


def flash_kernel(tokens, scale, len_ref, q_ref, kc_ref, vc_ref, kn_ref, vn_ref, o_ref):
    block_q = q_ref.shape[1]
    block_k = kc_ref.shape[2]
    width = q_ref.shape[2]
    i = pl.program_id(1)
    length = len_ref[0]
    first = lax.rem(i * block_q, tokens)
    q = q_ref[0]
    query_index = first + lax.broadcasted_iota(jnp.int32, (block_q, block_k), 0)
    key_offset = lax.broadcasted_iota(jnp.int32, (block_q, block_k), 1)

    def step(keys, values, visible, carry):
        peak, total, acc = carry
        score = lax.dot_general(
            q, keys, (((1,), (1,)), ((), ())), preferred_element_type=jnp.float32
        ) * scale
        score = jnp.where(visible, score, masked_score)
        new_peak = jnp.maximum(peak, jnp.max(score, axis=1, keepdims=True))
        alpha = jnp.exp(peak - new_peak)
        weights = jnp.where(visible, jnp.exp(score - new_peak), 0.0)
        total = alpha * total + jnp.sum(weights, axis=1, keepdims=True)
        acc = alpha * acc + jnp.dot(
            weights.astype(jnp.bfloat16), values, preferred_element_type=jnp.float32
        )
        return new_peak, total, acc

    def cache_step(block, carry):
        start = pl.multiple_of(block * block_k, block_k)
        keys = kc_ref[block, 0]
        values = vc_ref[block, 0]
        visible = start + key_offset < length
        return step(keys, values, visible, carry)

    block_n = kn_ref.shape[2]
    query_new = first + lax.broadcasted_iota(jnp.int32, (block_q, block_n), 0)
    offset_new = lax.broadcasted_iota(jnp.int32, (block_q, block_n), 1)

    def new_step(block, carry):
        visible = block * block_n + offset_new <= query_new
        return step(kn_ref[block, 0], vn_ref[block, 0], visible, carry)

    carry = (
        jnp.full((block_q, 1), -jnp.inf, jnp.float32),
        jnp.zeros((block_q, 1), jnp.float32),
        jnp.zeros((block_q, width), jnp.float32),
    )
    live_blocks = (length + block_k - 1) // block_k
    carry = lax.fori_loop(0, live_blocks, cache_step, carry)
    new_blocks = (first + block_q - 1) // block_n + 1
    peak, total, acc = lax.fori_loop(0, new_blocks, new_step, carry)
    o_ref[...] = (acc / total).astype(o_ref.dtype).reshape(o_ref.shape)


def flash_attention(lengths, queries, keys_old, values_old, keys_new, values_new, tokens, scale):
    heads, rows, width = queries.shape
    blocks, _, block_k, _ = keys_old.shape
    slots = blocks * block_k
    block_q = min(BLOCK_Q, tokens)
    grid = (heads, rows // block_q)
    whole_cache = pl.BlockSpec((blocks, 1, block_k, width), lambda c, i, n: (0, c, 0, 0))
    peers, _, block_n, _ = keys_new.shape
    whole_new = pl.BlockSpec((peers, 1, block_n, width), lambda c, i, n: (0, c, 0, 0))
    per_q = block_q // block_n
    halves = tokens // block_q
    groups = rows // tokens
    return pl.pallas_call(
        functools.partial(flash_kernel, tokens, scale),
        out_shape=jax.ShapeDtypeStruct((peers, heads, groups, block_n, width), jnp.bfloat16),
        grid_spec=pltpu.PrefetchScalarGridSpec(
            num_scalar_prefetch=1,
            grid=grid,
            in_specs=[
                pl.BlockSpec((1, block_q, width), lambda c, i, n: (c, i, 0)),
                whole_cache, whole_cache, whole_new, whole_new,
            ],
            out_specs=pl.BlockSpec(
                (per_q, 1, 1, block_n, width),
                lambda c, i, n: (lax.rem(i, halves), c, i // halves, 0, 0),
            ),
        ),
        cost_estimate=pl.CostEstimate(
            flops=4 * heads * rows * (slots + tokens) * width,
            transcendentals=heads * rows * (slots + tokens),
            bytes_accessed=2 * width * heads * (2 * rows + 2 * slots + 2 * tokens),
        ),
    )(lengths, queries, keys_old, values_old, keys_new, values_new)


def exchange_kernel(k_ref, v_ref, c_ref, k_out, v_out, c_out, send_sem, recv_sem, local_sem):
    me = lax.axis_index("kv")
    req = lax.axis_index("req")
    count = lax.axis_size("kv")
    arrays = ((k_ref, k_out), (v_ref, v_out), (c_ref, c_out))
    barrier = pltpu.get_barrier_semaphore()

    def greet(step, carry):
        peer = lax.rem(me + step, count)
        pl.semaphore_signal(barrier, inc=1, device_id=(req, peer), device_id_type=MESH)
        return carry

    lax.fori_loop(1, count, greet, 0)
    pl.semaphore_wait(barrier, count - 1)
    local = []
    for which, (src, dst) in enumerate(arrays):
        c = pltpu.make_async_copy(src.at[me], dst.at[me], local_sem.at[which])
        c.start()
        local.append(c)

    def send(step, carry):
        peer = lax.rem(me + step, count)
        for which, (src, dst) in enumerate(arrays):
            remote(src.at[peer], dst.at[me], send_sem.at[which, step - 1],
                   recv_sem.at[which, step - 1], (req, peer)).start()
        return carry

    lax.fori_loop(1, count, send, 0)

    def finish(step, carry):
        peer = lax.rem(me + step, count)
        source = lax.rem(me + count - step, count)
        for which, (src, dst) in enumerate(arrays):
            remote(src.at[peer], dst.at[me], send_sem.at[which, step - 1],
                   recv_sem.at[which, step - 1], (req, peer)).wait_send()
            remote(src.at[me], dst.at[source], send_sem.at[which, step - 1],
                   recv_sem.at[which, step - 1], (req, source)).wait_recv()
        return carry

    lax.fori_loop(1, count, finish, 0)
    for c in local:
        c.wait()


def exchange_kv(keys, values, context):
    count = lax.axis_size("kv")
    anywhere = pl.BlockSpec(memory_space=pl.ANY)
    return pl.pallas_call(
        exchange_kernel,
        out_shape=tuple(jax.ShapeDtypeStruct(a.shape, a.dtype) for a in (keys, values, context)),
        in_specs=[anywhere, anywhere, anywhere],
        out_specs=(anywhere, anywhere, anywhere),
        scratch_shapes=[
            pltpu.SemaphoreType.DMA((3, count - 1)),
            pltpu.SemaphoreType.DMA((3, count - 1)),
            pltpu.SemaphoreType.DMA((3,)),
        ],
        compiler_params=pltpu.CompilerParams(collective_id=1, has_side_effects=True),
    )(keys, values, context)


def body(hidden, lengths, key_cache, value_cache, norm_gain, w_query, w_key, w_value, w_out):
    rows_here = hidden.shape[1]
    kv_count = lax.axis_size("kv")
    appended = rows_here * kv_count
    slots = key_cache.shape[1]
    groups = H // KVH
    scale = HD ** (-0.5)
    length = lengths[0]
    q_cols = w_query.shape[1]
    k_cols = w_key.shape[1]
    v_cols = w_value.shape[1]
    heads_here = q_cols // HD
    kv_heads_here = k_cols // HD

    normed = rms_norm(hidden[0].astype(jnp.float32), norm_gain)
    normed_all = lax.all_gather(normed, "kv", axis=0, tiled=True)

    pieces = jnp.concatenate([w_query, w_key, w_value, w_out], axis=1)
    def to_peers(cache):
        return jnp.transpose(
            cache.reshape(slots, kv_count, kv_heads_here, HD), (1, 2, 0, 3)
        )

    cols, keys_old, values_old = gather_req(
        pieces, to_peers(key_cache[0]), to_peers(value_cache[0])
    )
    wq = cols[:, :q_cols]
    wk = cols[:, q_cols:q_cols + k_cols]
    wv = cols[:, q_cols + k_cols:q_cols + k_cols + v_cols]
    wo = cols[:, q_cols + k_cols + v_cols:]

    wo_full = lax.all_gather(wo, "kv", axis=1, tiled=True)

    positions = (length + jnp.arange(appended, dtype=jnp.int32)).astype(jnp.float32)
    half = HD // 2
    frequency = rope_base ** (-(jnp.arange(half, dtype=jnp.float32) * 2.0 / HD))
    angle = positions[:, None] * frequency[None, :]
    cosine = jnp.cos(angle)
    sine = jnp.sin(angle)

    def turn(values):
        first = values[..., :half]
        second = values[..., half:]
        return jnp.concatenate(
            [first * cosine - second * sine, second * cosine + first * sine], axis=-1
        )

    width = normed_all.shape[1]
    proj_q = jnp.einsum(
        "td,dcgh->cgth", normed_all, wq.reshape(width, kv_heads_here, groups, HD),
        preferred_element_type=jnp.float32,
    )
    normed_blocks = normed_all.reshape(kv_count, rows_here, width)
    proj_k = jnp.einsum(
        "std,dch->scth", normed_blocks, wk.reshape(width, kv_heads_here, HD),
        preferred_element_type=jnp.float32,
    )
    proj_v = jnp.einsum(
        "std,dch->scth", normed_blocks, wv.reshape(width, kv_heads_here, HD),
        preferred_element_type=jnp.float32,
    )
    cosine_blocks = cosine.reshape(kv_count, 1, rows_here, half)
    sine_blocks = sine.reshape(kv_count, 1, rows_here, half)
    query_heads = turn(proj_q).astype(jnp.bfloat16).reshape(kv_heads_here, groups * appended, HD)
    first_k = proj_k[..., :half]
    second_k = proj_k[..., half:]
    keys_new = jnp.concatenate(
        [first_k * cosine_blocks - second_k * sine_blocks,
         second_k * cosine_blocks + first_k * sine_blocks], axis=-1,
    ).astype(jnp.bfloat16)
    values_new = proj_v.astype(jnp.bfloat16)

    contexts = flash_attention(
        lengths, query_heads, keys_old, values_old, keys_new, values_new, appended, scale,
    )
    keys_got, values_got, got = exchange_kv(keys_new, values_new, contexts)

    def to_tokens(values):
        return jnp.transpose(values, (2, 0, 1, 3)).reshape(rows_here, kv_count * kv_heads_here * HD)

    new_keys = to_tokens(keys_got)
    new_values = to_tokens(values_got)
    attended = jnp.einsum(
        "scgth,scghn->tn", got,
        wo_full.reshape(kv_count, kv_heads_here, groups, HD, wo_full.shape[1]),
        preferred_element_type=jnp.float32,
    ).astype(jnp.bfloat16)
    return (attended[None], new_keys[None], new_values[None])


def solution(mesh):
    return jax.shard_map(
        body,
        mesh=mesh,
        in_specs=(
            P("req", "kv", None),
            P("req"),
            P("req", "kv", None),
            P("req", "kv", None),
            P(),
            P("req", "kv"),
            P("req", "kv"),
            P("req", "kv"),
            P("req", "kv"),
        ),
        out_specs=(P("req", "kv", None), P("req", "kv", None), P("req", "kv", None)),
        check_vma=False,
    )
```

```python
import functools

import jax
import jax.numpy as jnp
from jax import lax
from jax.sharding import PartitionSpec as P
from jax.experimental import pallas as pl
from jax.experimental.pallas import tpu as pltpu

H = 16
KVH = 8
HD = 96


rope_base = 100000.0
masked_score = -1e30


def rms_norm(states, gain):
    mean_square = jnp.mean(states * states, axis=-1, keepdims=True)
    scaled = states * lax.rsqrt(mean_square + 1e-05) * gain.astype(jnp.float32)
    return scaled.astype(jnp.bfloat16)


def rotate(values, positions):
    count = values.shape[0]
    heads = values.shape[1] // HD
    half = HD // 2
    frequency = rope_base ** (-(jnp.arange(half, dtype=jnp.float32) * 2.0 / HD))
    angle = positions[:, None] * frequency[None, :]
    cosine = jnp.cos(angle)[:, None, :]
    sine = jnp.sin(angle)[:, None, :]
    shaped = values.reshape(count, heads, HD)
    first = shaped[..., :half]
    second = shaped[..., half:]
    turned = jnp.concatenate(
        [first * cosine - second * sine, second * cosine + first * sine], axis=-1
    )
    return turned.reshape(count, heads * HD)


Z_RUN = 8
Y_RUN = 2
MESH = pl.DeviceIdType.MESH


def remote(src, dst, send, recv, device):
    return pltpu.make_async_remote_copy(
        src_ref=src, dst_ref=dst, send_sem=send, recv_sem=recv,
        device_id=device, device_id_type=MESH,
    )


def plane_ring_kernel(planes, runs, src_ref, kc_ref, vc_ref, out_ref, kc_out, vc_out, s1_send,
                      s1_recv, r_send, r_recv, l_send, l_recv, local_sem, kv_send, kv_recv, kv_local):
    me = lax.axis_index("req")
    kv = lax.axis_index("kv")
    y_me = lax.rem(me, Y_RUN)
    z_me = lax.rem(me // Y_RUN, runs)
    x_me = me // (Y_RUN * runs)
    q_me = x_me * Y_RUN + y_me
    right_hops = runs // 2
    left_hops = runs - 1 - right_hops

    def plane_peer(q):
        return ((q // Y_RUN) * runs + z_me) * Y_RUN + lax.rem(q, Y_RUN)

    def ring_peer(z):
        return (x_me * runs + z) * Y_RUN + y_me

    z_right = lax.rem(z_me + 1, runs)
    z_left = lax.rem(z_me + runs - 1, runs)

    barrier = pltpu.get_barrier_semaphore()

    def greet(step, carry):
        q = lax.rem(q_me + step, planes)
        pl.semaphore_signal(barrier, inc=1, device_id=(plane_peer(q), kv), device_id_type=MESH)
        return carry

    lax.fori_loop(1, planes, greet, 0)
    pl.semaphore_signal(barrier, inc=1, device_id=(ring_peer(z_right), kv), device_id_type=MESH)
    pl.semaphore_signal(barrier, inc=1, device_id=(ring_peer(z_left), kv), device_id_type=MESH)
    kv_count = lax.axis_size("kv")

    def greet_kv(step, carry):
        peer = lax.rem(kv + step, kv_count)
        pl.semaphore_signal(barrier, inc=1, device_id=(me, peer), device_id_type=MESH)
        return carry

    lax.fori_loop(1, kv_count, greet_kv, 0)
    pl.semaphore_wait(barrier, planes + 1 + kv_count - 1)

    local = pltpu.make_async_copy(src_ref, out_ref.at[z_me, q_me], local_sem)
    local.start()
    caches = ((kc_ref, kc_out), (vc_ref, vc_out))
    local_cache = []
    for which, (cache_src, cache_dst) in enumerate(caches):
        c = pltpu.make_async_copy(cache_src.at[kv], cache_dst.at[kv], kv_local.at[which])
        c.start()
        local_cache.append(c)


    def send(step, carry):
        q = lax.rem(q_me + step, planes)
        remote(src_ref, out_ref.at[z_me, q_me], s1_send.at[step - 1], s1_recv.at[step - 1],
               (plane_peer(q), kv)).start()
        return carry

    lax.fori_loop(1, planes, send, 0)

    def finish(step, carry):
        q = lax.rem(q_me + step, planes)
        source = lax.rem(q_me + planes - step, planes)
        remote(src_ref, out_ref.at[z_me, q_me], s1_send.at[step - 1], s1_recv.at[step - 1],
               (plane_peer(q), kv)).wait_send()
        remote(src_ref, out_ref.at[z_me, source], s1_send.at[step - 1], s1_recv.at[step - 1],
               (plane_peer(source), kv)).wait_recv()
        return carry

    lax.fori_loop(1, planes, finish, 0)
    local.wait()

    split = 2 if planes % 2 == 0 else 1
    share = planes // split

    def ring_copy(z_block, h, send, recv, k, z_to):
        part = out_ref.at[z_block, pl.ds(h * share, share)]
        return remote(part, part, send.at[k, h], recv.at[k, h], (ring_peer(z_to), kv))

    sent = []
    for h in range(split):
        if right_hops > 0:
            c = ring_copy(z_me, h, r_send, r_recv, 0, z_right)
            c.start()
            sent.append(c)
        if left_hops > 0:
            c = ring_copy(z_me, h, l_send, l_recv, 0, z_left)
            c.start()
            sent.append(c)

    def send_kv(step, carry):
        peer = lax.rem(kv + step, kv_count)
        for which, (cache_src, cache_dst) in enumerate(caches):
            remote(cache_src.at[peer], cache_dst.at[kv], kv_send.at[which, step - 1],
                   kv_recv.at[which, step - 1], (me, peer)).start()
        return carry

    lax.fori_loop(1, kv_count, send_kv, 0)
    for k in range(1, max(right_hops, left_hops) + 1):
        for h in range(split):
            if k <= right_hops:
                z_from = lax.rem(z_me + runs - k, runs)
                ring_copy(z_from, h, r_send, r_recv, k - 1, z_right).wait_recv()
                if k < right_hops:
                    c = ring_copy(z_from, h, r_send, r_recv, k, z_right)
                    c.start()
                    sent.append(c)
            if k <= left_hops:
                z_from = lax.rem(z_me + k, runs)
                ring_copy(z_from, h, l_send, l_recv, k - 1, z_left).wait_recv()
                if k < left_hops:
                    c = ring_copy(z_from, h, l_send, l_recv, k, z_left)
                    c.start()
                    sent.append(c)
    for c in sent:
        c.wait_send()

    def finish_kv(step, carry):
        peer = lax.rem(kv + step, kv_count)
        source = lax.rem(kv + kv_count - step, kv_count)
        for which, (cache_src, cache_dst) in enumerate(caches):
            remote(cache_src.at[peer], cache_dst.at[kv], kv_send.at[which, step - 1],
                   kv_recv.at[which, step - 1], (me, peer)).wait_send()
            remote(cache_src.at[kv], cache_dst.at[source], kv_send.at[which, step - 1],
                   kv_recv.at[which, step - 1], (me, source)).wait_recv()
        return carry

    lax.fori_loop(1, kv_count, finish_kv, 0)
    for c in local_cache:
        c.wait()


def gather_req(piece, keys_send, values_send):
    count = lax.axis_size("req")
    kv_count = lax.axis_size("kv")
    runs = min(Z_RUN, count // Y_RUN)
    planes = count // runs
    rows, width = piece.shape
    hops = max(runs - 1, 1)
    anywhere = pl.BlockSpec(memory_space=pl.ANY)
    gathered, keys_old, values_old = pl.pallas_call(
        functools.partial(plane_ring_kernel, planes, runs),
        out_shape=(
            jax.ShapeDtypeStruct((runs, planes, rows, width), piece.dtype),
            jax.ShapeDtypeStruct(keys_send.shape, keys_send.dtype),
            jax.ShapeDtypeStruct(values_send.shape, values_send.dtype),
        ),
        in_specs=[anywhere, anywhere, anywhere],
        out_specs=(anywhere, anywhere, anywhere),
        scratch_shapes=[
            pltpu.SemaphoreType.DMA((planes - 1,)),
            pltpu.SemaphoreType.DMA((planes - 1,)),
            pltpu.SemaphoreType.DMA((hops, 2)),
            pltpu.SemaphoreType.DMA((hops, 2)),
            pltpu.SemaphoreType.DMA((hops, 2)),
            pltpu.SemaphoreType.DMA((hops, 2)),
            pltpu.SemaphoreType.DMA,
            pltpu.SemaphoreType.DMA((2, kv_count - 1)),
            pltpu.SemaphoreType.DMA((2, kv_count - 1)),
            pltpu.SemaphoreType.DMA((2,)),
        ],
        compiler_params=pltpu.CompilerParams(collective_id=0, has_side_effects=True),
    )(piece, keys_send, values_send)
    x_count = planes // Y_RUN
    ordered = jnp.transpose(
        gathered.reshape(runs, x_count, Y_RUN, rows, width), (1, 0, 2, 3, 4)
    )
    return ordered.reshape(count * rows, width), keys_old, values_old


BLOCK_Q = 512
BLOCK_K = 512


def flash_kernel(tokens, scale, len_ref, q_ref, kc_ref, vc_ref, kn_ref, vn_ref, o_ref):
    block_q = q_ref.shape[1]
    block_k = kc_ref.shape[2]
    width = q_ref.shape[2]
    i = pl.program_id(1)
    length = len_ref[0]
    first = lax.rem(i * block_q, tokens)
    q = q_ref[0]
    query_index = first + lax.broadcasted_iota(jnp.int32, (block_q, block_k), 0)
    key_offset = lax.broadcasted_iota(jnp.int32, (block_q, block_k), 1)

    def step(keys, values, visible, carry):
        peak, total, acc = carry
        score = lax.dot_general(
            q, keys, (((1,), (1,)), ((), ())), preferred_element_type=jnp.float32
        ) * scale
        if visible is not None:
            score = jnp.where(visible, score, masked_score)
        new_peak = jnp.maximum(peak, jnp.max(score, axis=1, keepdims=True))
        alpha = jnp.exp(peak - new_peak)
        weights = jnp.exp(score - new_peak)
        if visible is not None:
            weights = jnp.where(visible, weights, 0.0)
        total = alpha * total + jnp.sum(weights, axis=1, keepdims=True)
        acc = alpha * acc + jnp.dot(
            weights.astype(jnp.bfloat16), values, preferred_element_type=jnp.float32
        )
        return new_peak, total, acc

    def cache_full(block, carry):
        return step(kc_ref[block, 0], vc_ref[block, 0], None, carry)

    def cache_part(block, carry):
        visible = block * block_k + key_offset < length
        return step(kc_ref[block, 0], vc_ref[block, 0], visible, carry)

    def new_full(block, carry):
        start = pl.multiple_of(block * block_k, block_k)
        keys = kn_ref[0, pl.ds(start, block_k), :]
        values = vn_ref[0, pl.ds(start, block_k), :]
        return step(keys, values, None, carry)

    def new_part(block, carry):
        start = pl.multiple_of(block * block_k, block_k)
        keys = kn_ref[0, pl.ds(start, block_k), :]
        values = vn_ref[0, pl.ds(start, block_k), :]
        visible = start + key_offset <= query_index
        return step(keys, values, visible, carry)

    carry = (
        jnp.full((block_q, 1), -jnp.inf, jnp.float32),
        jnp.zeros((block_q, 1), jnp.float32),
        jnp.zeros((block_q, width), jnp.float32),
    )
    full_blocks = length // block_k
    live_blocks = (length + block_k - 1) // block_k
    carry = lax.fori_loop(0, full_blocks, cache_full, carry)
    carry = lax.fori_loop(full_blocks, live_blocks, cache_part, carry)
    clear_blocks = first // block_k
    new_blocks = (first + block_q - 1) // block_k + 1
    carry = lax.fori_loop(0, clear_blocks, new_full, carry)
    peak, total, acc = lax.fori_loop(clear_blocks, new_blocks, new_part, carry)
    o_ref[0] = (acc / total).astype(o_ref.dtype)


def flash_attention(lengths, queries, keys_old, values_old, keys_new, values_new, tokens, scale):
    heads, rows, width = queries.shape
    blocks, _, block_k, _ = keys_old.shape
    slots = blocks * block_k
    block_q = min(BLOCK_Q, tokens)
    grid = (heads, rows // block_q)
    whole_cache = pl.BlockSpec((blocks, 1, block_k, width), lambda c, i, n: (0, c, 0, 0))
    whole_new = pl.BlockSpec((1, tokens, width), lambda c, i, n: (c, 0, 0))
    return pl.pallas_call(
        functools.partial(flash_kernel, tokens, scale),
        out_shape=jax.ShapeDtypeStruct((heads, rows, width), jnp.bfloat16),
        grid_spec=pltpu.PrefetchScalarGridSpec(
            num_scalar_prefetch=1,
            grid=grid,
            in_specs=[
                pl.BlockSpec((1, block_q, width), lambda c, i, n: (c, i, 0)),
                whole_cache, whole_cache, whole_new, whole_new,
            ],
            out_specs=pl.BlockSpec((1, block_q, width), lambda c, i, n: (c, i, 0)),
        ),
        cost_estimate=pl.CostEstimate(
            flops=4 * heads * rows * (slots + tokens) * width,
            transcendentals=heads * rows * (slots + tokens),
            bytes_accessed=2 * width * heads * (2 * rows + 2 * slots + 2 * tokens),
        ),
    )(lengths, queries, keys_old, values_old, keys_new, values_new)


def body(hidden, lengths, key_cache, value_cache, norm_gain, w_query, w_key, w_value, w_out):
    rows_here = hidden.shape[1]
    kv_count = lax.axis_size("kv")
    appended = rows_here * kv_count
    slots = key_cache.shape[1]
    groups = H // KVH
    scale = HD ** (-0.5)
    length = lengths[0]
    q_cols = w_query.shape[1]
    k_cols = w_key.shape[1]
    v_cols = w_value.shape[1]
    heads_here = q_cols // HD
    kv_heads_here = k_cols // HD

    normed = rms_norm(hidden[0].astype(jnp.float32), norm_gain)
    normed_all = lax.all_gather(normed, "kv", axis=0, tiled=True)

    pieces = jnp.concatenate([w_query, w_key, w_value, w_out], axis=1)
    def to_peers(cache):
        return jnp.transpose(
            cache.reshape(slots, kv_count, kv_heads_here, HD), (1, 2, 0, 3)
        )

    cols, keys_old, values_old = gather_req(
        pieces, to_peers(key_cache[0]), to_peers(value_cache[0])
    )
    wq = cols[:, :q_cols]
    wk = cols[:, q_cols:q_cols + k_cols]
    wv = cols[:, q_cols + k_cols:q_cols + k_cols + v_cols]
    wo = cols[:, q_cols + k_cols + v_cols:]

    wo_full = lax.all_gather(wo, "kv", axis=1, tiled=True)

    positions = (length + jnp.arange(appended, dtype=jnp.int32)).astype(jnp.float32)
    half = HD // 2
    frequency = rope_base ** (-(jnp.arange(half, dtype=jnp.float32) * 2.0 / HD))
    angle = positions[:, None] * frequency[None, :]
    cosine = jnp.cos(angle)
    sine = jnp.sin(angle)

    def turn(values):
        first = values[..., :half]
        second = values[..., half:]
        return jnp.concatenate(
            [first * cosine - second * sine, second * cosine + first * sine], axis=-1
        )

    width = normed_all.shape[1]
    proj_q = jnp.einsum(
        "td,dcgh->cgth", normed_all, wq.reshape(width, kv_heads_here, groups, HD),
        preferred_element_type=jnp.float32,
    )
    proj_k = jnp.einsum(
        "td,dch->cth", normed_all, wk.reshape(width, kv_heads_here, HD),
        preferred_element_type=jnp.float32,
    )
    proj_v = jnp.einsum(
        "td,dch->cth", normed_all, wv.reshape(width, kv_heads_here, HD),
        preferred_element_type=jnp.float32,
    )
    query_heads = turn(proj_q).astype(jnp.bfloat16).reshape(kv_heads_here, groups * appended, HD)
    keys_new = turn(proj_k).astype(jnp.bfloat16)
    values_new = proj_v.astype(jnp.bfloat16)

    def to_tokens(values):
        parts = values.reshape(kv_heads_here, kv_count, rows_here, HD)
        got = lax.all_to_all(parts, "kv", split_axis=1, concat_axis=1, tiled=True)
        return jnp.transpose(got, (2, 1, 0, 3)).reshape(rows_here, kv_count * kv_heads_here * HD)

    new_keys = to_tokens(keys_new)
    new_values = to_tokens(values_new)

    contexts = flash_attention(
        lengths, query_heads, keys_old, values_old, keys_new, values_new, appended, scale,
    )
    parts = contexts.reshape(kv_heads_here, groups, kv_count, rows_here, HD)
    got = lax.all_to_all(parts, "kv", split_axis=2, concat_axis=2, tiled=True)
    attended = jnp.einsum(
        "cgsth,scghn->tn", got,
        wo_full.reshape(kv_count, kv_heads_here, groups, HD, wo_full.shape[1]),
        preferred_element_type=jnp.float32,
    ).astype(jnp.bfloat16)
    return (attended[None], new_keys[None], new_values[None])


def solution(mesh):
    return jax.shard_map(
        body,
        mesh=mesh,
        in_specs=(
            P("req", "kv", None),
            P("req"),
            P("req", "kv", None),
            P("req", "kv", None),
            P(),
            P("req", "kv"),
            P("req", "kv"),
            P("req", "kv"),
            P("req", "kv"),
        ),
        out_specs=(P("req", "kv", None), P("req", "kv", None), P("req", "kv", None)),
        check_vma=False,
    )
```

```python
import functools

import jax
import jax.numpy as jnp
from jax import lax
from jax.sharding import PartitionSpec as P
from jax.experimental import pallas as pl
from jax.experimental.pallas import tpu as pltpu

H = 16
KVH = 8
HD = 96


rope_base = 100000.0
masked_score = -1e30


def rms_norm(states, gain):
    mean_square = jnp.mean(states * states, axis=-1, keepdims=True)
    scaled = states * lax.rsqrt(mean_square + 1e-05) * gain.astype(jnp.float32)
    return scaled.astype(jnp.bfloat16)


def rotate(values, positions):
    count = values.shape[0]
    heads = values.shape[1] // HD
    half = HD // 2
    frequency = rope_base ** (-(jnp.arange(half, dtype=jnp.float32) * 2.0 / HD))
    angle = positions[:, None] * frequency[None, :]
    cosine = jnp.cos(angle)[:, None, :]
    sine = jnp.sin(angle)[:, None, :]
    shaped = values.reshape(count, heads, HD)
    first = shaped[..., :half]
    second = shaped[..., half:]
    turned = jnp.concatenate(
        [first * cosine - second * sine, second * cosine + first * sine], axis=-1
    )
    return turned.reshape(count, heads * HD)


Z_RUN = 8
Y_RUN = 2
MESH = pl.DeviceIdType.MESH


def remote(src, dst, send, recv, device):
    return pltpu.make_async_remote_copy(
        src_ref=src, dst_ref=dst, send_sem=send, recv_sem=recv,
        device_id=device, device_id_type=MESH,
    )


def plane_ring_kernel(planes, runs, src_ref, kc_ref, vc_ref, out_ref, kc_out, vc_out, s1_send,
                      s1_recv, r_send, r_recv, l_send, l_recv, local_sem, kv_send, kv_recv, kv_local):
    me = lax.axis_index("req")
    kv = lax.axis_index("kv")
    y_me = lax.rem(me, Y_RUN)
    z_me = lax.rem(me // Y_RUN, runs)
    x_me = me // (Y_RUN * runs)
    q_me = x_me * Y_RUN + y_me
    right_hops = runs // 2
    left_hops = runs - 1 - right_hops

    def plane_peer(q):
        return ((q // Y_RUN) * runs + z_me) * Y_RUN + lax.rem(q, Y_RUN)

    def ring_peer(z):
        return (x_me * runs + z) * Y_RUN + y_me

    z_right = lax.rem(z_me + 1, runs)
    z_left = lax.rem(z_me + runs - 1, runs)

    barrier = pltpu.get_barrier_semaphore()

    def greet(step, carry):
        q = lax.rem(q_me + step, planes)
        pl.semaphore_signal(barrier, inc=1, device_id=(plane_peer(q), kv), device_id_type=MESH)
        return carry

    lax.fori_loop(1, planes, greet, 0)
    pl.semaphore_signal(barrier, inc=1, device_id=(ring_peer(z_right), kv), device_id_type=MESH)
    pl.semaphore_signal(barrier, inc=1, device_id=(ring_peer(z_left), kv), device_id_type=MESH)
    kv_count = lax.axis_size("kv")

    def greet_kv(step, carry):
        peer = lax.rem(kv + step, kv_count)
        pl.semaphore_signal(barrier, inc=1, device_id=(me, peer), device_id_type=MESH)
        return carry

    lax.fori_loop(1, kv_count, greet_kv, 0)
    pl.semaphore_wait(barrier, planes + 1 + kv_count - 1)

    local = pltpu.make_async_copy(src_ref, out_ref.at[z_me, q_me], local_sem)
    local.start()
    caches = ((kc_ref, kc_out), (vc_ref, vc_out))
    local_cache = []
    for which, (cache_src, cache_dst) in enumerate(caches):
        c = pltpu.make_async_copy(cache_src.at[kv], cache_dst.at[kv], kv_local.at[which])
        c.start()
        local_cache.append(c)


    def send(step, carry):
        q = lax.rem(q_me + step, planes)
        remote(src_ref, out_ref.at[z_me, q_me], s1_send.at[step - 1], s1_recv.at[step - 1],
               (plane_peer(q), kv)).start()
        return carry

    lax.fori_loop(1, planes, send, 0)

    def finish(step, carry):
        q = lax.rem(q_me + step, planes)
        source = lax.rem(q_me + planes - step, planes)
        remote(src_ref, out_ref.at[z_me, q_me], s1_send.at[step - 1], s1_recv.at[step - 1],
               (plane_peer(q), kv)).wait_send()
        remote(src_ref, out_ref.at[z_me, source], s1_send.at[step - 1], s1_recv.at[step - 1],
               (plane_peer(source), kv)).wait_recv()
        return carry

    lax.fori_loop(1, planes, finish, 0)
    local.wait()

    split = 2 if planes % 2 == 0 else 1
    share = planes // split

    def ring_copy(z_block, h, send, recv, k, z_to):
        part = out_ref.at[z_block, pl.ds(h * share, share)]
        return remote(part, part, send.at[k, h], recv.at[k, h], (ring_peer(z_to), kv))

    sent = []
    for h in range(split):
        if right_hops > 0:
            c = ring_copy(z_me, h, r_send, r_recv, 0, z_right)
            c.start()
            sent.append(c)
        if left_hops > 0:
            c = ring_copy(z_me, h, l_send, l_recv, 0, z_left)
            c.start()
            sent.append(c)

    def send_kv(step, carry):
        peer = lax.rem(kv + step, kv_count)
        for which, (cache_src, cache_dst) in enumerate(caches):
            remote(cache_src.at[peer], cache_dst.at[kv], kv_send.at[which, step - 1],
                   kv_recv.at[which, step - 1], (me, peer)).start()
        return carry

    lax.fori_loop(1, kv_count, send_kv, 0)
    for k in range(1, max(right_hops, left_hops) + 1):
        for h in range(split):
            if k <= right_hops:
                z_from = lax.rem(z_me + runs - k, runs)
                ring_copy(z_from, h, r_send, r_recv, k - 1, z_right).wait_recv()
                if k < right_hops:
                    c = ring_copy(z_from, h, r_send, r_recv, k, z_right)
                    c.start()
                    sent.append(c)
            if k <= left_hops:
                z_from = lax.rem(z_me + k, runs)
                ring_copy(z_from, h, l_send, l_recv, k - 1, z_left).wait_recv()
                if k < left_hops:
                    c = ring_copy(z_from, h, l_send, l_recv, k, z_left)
                    c.start()
                    sent.append(c)
    for c in sent:
        c.wait_send()

    def finish_kv(step, carry):
        peer = lax.rem(kv + step, kv_count)
        source = lax.rem(kv + kv_count - step, kv_count)
        for which, (cache_src, cache_dst) in enumerate(caches):
            remote(cache_src.at[peer], cache_dst.at[kv], kv_send.at[which, step - 1],
                   kv_recv.at[which, step - 1], (me, peer)).wait_send()
            remote(cache_src.at[kv], cache_dst.at[source], kv_send.at[which, step - 1],
                   kv_recv.at[which, step - 1], (me, source)).wait_recv()
        return carry

    lax.fori_loop(1, kv_count, finish_kv, 0)
    for c in local_cache:
        c.wait()


def gather_req(piece, keys_send, values_send):
    count = lax.axis_size("req")
    kv_count = lax.axis_size("kv")
    runs = min(Z_RUN, count // Y_RUN)
    planes = count // runs
    rows, width = piece.shape
    hops = max(runs - 1, 1)
    anywhere = pl.BlockSpec(memory_space=pl.ANY)
    gathered, keys_old, values_old = pl.pallas_call(
        functools.partial(plane_ring_kernel, planes, runs),
        out_shape=(
            jax.ShapeDtypeStruct((runs, planes, rows, width), piece.dtype),
            jax.ShapeDtypeStruct(keys_send.shape, keys_send.dtype),
            jax.ShapeDtypeStruct(values_send.shape, values_send.dtype),
        ),
        in_specs=[anywhere, anywhere, anywhere],
        out_specs=(anywhere, anywhere, anywhere),
        scratch_shapes=[
            pltpu.SemaphoreType.DMA((planes - 1,)),
            pltpu.SemaphoreType.DMA((planes - 1,)),
            pltpu.SemaphoreType.DMA((hops, 2)),
            pltpu.SemaphoreType.DMA((hops, 2)),
            pltpu.SemaphoreType.DMA((hops, 2)),
            pltpu.SemaphoreType.DMA((hops, 2)),
            pltpu.SemaphoreType.DMA,
            pltpu.SemaphoreType.DMA((2, kv_count - 1)),
            pltpu.SemaphoreType.DMA((2, kv_count - 1)),
            pltpu.SemaphoreType.DMA((2,)),
        ],
        compiler_params=pltpu.CompilerParams(collective_id=0, has_side_effects=True),
    )(piece, keys_send, values_send)
    return gathered.reshape(count * rows, width), keys_old, values_old


def req_order(block, count, piece_rows):
    runs = min(Z_RUN, count // Y_RUN)
    x_count = count // (runs * Y_RUN)
    shaped = block.reshape(runs, x_count, Y_RUN, piece_rows, block.shape[1])
    return jnp.transpose(shaped, (1, 0, 2, 3, 4)).reshape(block.shape)


def gathered_order(normed, count, piece_rows):
    runs = min(Z_RUN, count // Y_RUN)
    x_count = count // (runs * Y_RUN)
    rows = normed.shape[0]
    shaped = normed.reshape(rows, x_count, runs, Y_RUN, piece_rows)
    return jnp.transpose(shaped, (0, 2, 1, 3, 4)).reshape(rows, -1)


BLOCK_Q = 512
BLOCK_K = 512


def flash_kernel(tokens, scale, len_ref, q_ref, kc_ref, vc_ref, kn_ref, vn_ref, o_ref):
    block_q = q_ref.shape[1]
    block_k = kc_ref.shape[2]
    width = q_ref.shape[2]
    i = pl.program_id(1)
    length = len_ref[0]
    first = lax.rem(i * block_q, tokens)
    q = q_ref[0]
    query_index = first + lax.broadcasted_iota(jnp.int32, (block_q, block_k), 0)
    key_offset = lax.broadcasted_iota(jnp.int32, (block_q, block_k), 1)

    def step(keys, values, visible, carry):
        peak, total, acc = carry
        score = lax.dot_general(
            q, keys, (((1,), (1,)), ((), ())), preferred_element_type=jnp.float32
        ) * scale
        score = jnp.where(visible, score, masked_score)
        new_peak = jnp.maximum(peak, jnp.max(score, axis=1, keepdims=True))
        alpha = jnp.exp(peak - new_peak)
        weights = jnp.where(visible, jnp.exp(score - new_peak), 0.0)
        total = alpha * total + jnp.sum(weights, axis=1, keepdims=True)
        acc = alpha * acc + jnp.dot(
            weights.astype(jnp.bfloat16), values, preferred_element_type=jnp.float32
        )
        return new_peak, total, acc

    def cache_step(block, carry):
        start = pl.multiple_of(block * block_k, block_k)
        keys = kc_ref[block, 0]
        values = vc_ref[block, 0]
        visible = start + key_offset < length
        return step(keys, values, visible, carry)

    def new_step(block, carry):
        start = pl.multiple_of(block * block_k, block_k)
        keys = kn_ref[0, pl.ds(start, block_k), :]
        values = vn_ref[0, pl.ds(start, block_k), :]
        visible = start + key_offset <= query_index
        return step(keys, values, visible, carry)

    carry = (
        jnp.full((block_q, 1), -jnp.inf, jnp.float32),
        jnp.zeros((block_q, 1), jnp.float32),
        jnp.zeros((block_q, width), jnp.float32),
    )
    live_blocks = (length + block_k - 1) // block_k
    carry = lax.fori_loop(0, live_blocks, cache_step, carry)
    new_blocks = (first + block_q - 1) // block_k + 1
    peak, total, acc = lax.fori_loop(0, new_blocks, new_step, carry)
    o_ref[0] = (acc / total).astype(o_ref.dtype)


def flash_attention(lengths, queries, keys_old, values_old, keys_new, values_new, tokens, scale):
    heads, rows, width = queries.shape
    blocks, _, block_k, _ = keys_old.shape
    slots = blocks * block_k
    block_q = min(BLOCK_Q, tokens)
    grid = (heads, rows // block_q)
    whole_cache = pl.BlockSpec((blocks, 1, block_k, width), lambda c, i, n: (0, c, 0, 0))
    whole_new = pl.BlockSpec((1, tokens, width), lambda c, i, n: (c, 0, 0))
    return pl.pallas_call(
        functools.partial(flash_kernel, tokens, scale),
        out_shape=jax.ShapeDtypeStruct((heads, rows, width), jnp.bfloat16),
        grid_spec=pltpu.PrefetchScalarGridSpec(
            num_scalar_prefetch=1,
            grid=grid,
            in_specs=[
                pl.BlockSpec((1, block_q, width), lambda c, i, n: (c, i, 0)),
                whole_cache, whole_cache, whole_new, whole_new,
            ],
            out_specs=pl.BlockSpec((1, block_q, width), lambda c, i, n: (c, i, 0)),
        ),
        cost_estimate=pl.CostEstimate(
            flops=4 * heads * rows * (slots + tokens) * width,
            transcendentals=heads * rows * (slots + tokens),
            bytes_accessed=2 * width * heads * (2 * rows + 2 * slots + 2 * tokens),
        ),
    )(lengths, queries, keys_old, values_old, keys_new, values_new)


def body(hidden, lengths, key_cache, value_cache, norm_gain, w_query, w_key, w_value, w_out):
    rows_here = hidden.shape[1]
    kv_count = lax.axis_size("kv")
    appended = rows_here * kv_count
    slots = key_cache.shape[1]
    groups = H // KVH
    scale = HD ** (-0.5)
    length = lengths[0]
    q_cols = w_query.shape[1]
    k_cols = w_key.shape[1]
    v_cols = w_value.shape[1]
    heads_here = q_cols // HD
    kv_heads_here = k_cols // HD

    normed = rms_norm(hidden[0].astype(jnp.float32), norm_gain)
    normed = gathered_order(normed, lax.axis_size("req"), w_query.shape[0])
    normed_all = lax.all_gather(normed, "kv", axis=0, tiled=True)

    pieces = jnp.concatenate([w_query, w_key, w_value, w_out], axis=1)
    def to_peers(cache):
        return jnp.transpose(
            cache.reshape(slots, kv_count, kv_heads_here, HD), (1, 2, 0, 3)
        )

    cols, keys_old, values_old = gather_req(
        pieces, to_peers(key_cache[0]), to_peers(value_cache[0])
    )
    wq = cols[:, :q_cols]
    wk = cols[:, q_cols:q_cols + k_cols]
    wv = cols[:, q_cols + k_cols:q_cols + k_cols + v_cols]
    wo = req_order(cols[:, q_cols + k_cols + v_cols:], lax.axis_size("req"), w_query.shape[0])

    wo_full = lax.all_gather(wo, "kv", axis=1, tiled=True)

    positions = (length + jnp.arange(appended, dtype=jnp.int32)).astype(jnp.float32)
    half = HD // 2
    frequency = rope_base ** (-(jnp.arange(half, dtype=jnp.float32) * 2.0 / HD))
    angle = positions[:, None] * frequency[None, :]
    cosine = jnp.cos(angle)
    sine = jnp.sin(angle)

    def turn(values):
        first = values[..., :half]
        second = values[..., half:]
        return jnp.concatenate(
            [first * cosine - second * sine, second * cosine + first * sine], axis=-1
        )

    width = normed_all.shape[1]
    proj_q = jnp.einsum(
        "td,dcgh->cgth", normed_all, wq.reshape(width, kv_heads_here, groups, HD),
        preferred_element_type=jnp.float32,
    )
    proj_k = jnp.einsum(
        "td,dch->cth", normed_all, wk.reshape(width, kv_heads_here, HD),
        preferred_element_type=jnp.float32,
    )
    proj_v = jnp.einsum(
        "td,dch->cth", normed_all, wv.reshape(width, kv_heads_here, HD),
        preferred_element_type=jnp.float32,
    )
    query_heads = turn(proj_q).astype(jnp.bfloat16).reshape(kv_heads_here, groups * appended, HD)
    keys_new = turn(proj_k).astype(jnp.bfloat16)
    values_new = proj_v.astype(jnp.bfloat16)

    def to_tokens(values):
        parts = values.reshape(kv_heads_here, kv_count, rows_here, HD)
        got = lax.all_to_all(parts, "kv", split_axis=1, concat_axis=1, tiled=True)
        return jnp.transpose(got, (2, 1, 0, 3)).reshape(rows_here, kv_count * kv_heads_here * HD)

    new_keys = to_tokens(keys_new)
    new_values = to_tokens(values_new)

    contexts = flash_attention(
        lengths, query_heads, keys_old, values_old, keys_new, values_new, appended, scale,
    )
    parts = contexts.reshape(kv_heads_here, groups, kv_count, rows_here, HD)
    got = lax.all_to_all(parts, "kv", split_axis=2, concat_axis=2, tiled=True)
    attended = jnp.einsum(
        "cgsth,scghn->tn", got,
        wo_full.reshape(kv_count, kv_heads_here, groups, HD, wo_full.shape[1]),
        preferred_element_type=jnp.float32,
    ).astype(jnp.bfloat16)
    return (attended[None], new_keys[None], new_values[None])


def solution(mesh):
    return jax.shard_map(
        body,
        mesh=mesh,
        in_specs=(
            P("req", "kv", None),
            P("req"),
            P("req", "kv", None),
            P("req", "kv", None),
            P(),
            P("req", "kv"),
            P("req", "kv"),
            P("req", "kv"),
            P("req", "kv"),
        ),
        out_specs=(P("req", "kv", None), P("req", "kv", None), P("req", "kv", None)),
        check_vma=False,
    )
```

```python
import functools

import jax
import jax.numpy as jnp
from jax import lax
from jax.sharding import PartitionSpec as P
from jax.experimental import pallas as pl
from jax.experimental.pallas import tpu as pltpu

H = 16
KVH = 8
HD = 96


rope_base = 100000.0
masked_score = -1e30


def rms_norm(states, gain):
    mean_square = jnp.mean(states * states, axis=-1, keepdims=True)
    scaled = states * lax.rsqrt(mean_square + 1e-05) * gain.astype(jnp.float32)
    return scaled.astype(jnp.bfloat16)


def rotate(values, positions):
    count = values.shape[0]
    heads = values.shape[1] // HD
    half = HD // 2
    frequency = rope_base ** (-(jnp.arange(half, dtype=jnp.float32) * 2.0 / HD))
    angle = positions[:, None] * frequency[None, :]
    cosine = jnp.cos(angle)[:, None, :]
    sine = jnp.sin(angle)[:, None, :]
    shaped = values.reshape(count, heads, HD)
    first = shaped[..., :half]
    second = shaped[..., half:]
    turned = jnp.concatenate(
        [first * cosine - second * sine, second * cosine + first * sine], axis=-1
    )
    return turned.reshape(count, heads * HD)


Z_RUN = 8
Y_RUN = 2
MESH = pl.DeviceIdType.MESH


def remote(src, dst, send, recv, device):
    return pltpu.make_async_remote_copy(
        src_ref=src, dst_ref=dst, send_sem=send, recv_sem=recv,
        device_id=device, device_id_type=MESH,
    )


def plane_ring_kernel(planes, runs, src_ref, kc_ref, vc_ref, out_ref, kc_out, vc_out, s1_send,
                      s1_recv, r_send, r_recv, l_send, l_recv, local_sem, kv_send, kv_recv, kv_local):
    me = lax.axis_index("req")
    kv = lax.axis_index("kv")
    y_me = lax.rem(me, Y_RUN)
    z_me = lax.rem(me // Y_RUN, runs)
    x_me = me // (Y_RUN * runs)
    q_me = x_me * Y_RUN + y_me
    right_hops = runs // 2
    left_hops = runs - 1 - right_hops

    def plane_peer(q):
        return ((q // Y_RUN) * runs + z_me) * Y_RUN + lax.rem(q, Y_RUN)

    def ring_peer(z):
        return (x_me * runs + z) * Y_RUN + y_me

    z_right = lax.rem(z_me + 1, runs)
    z_left = lax.rem(z_me + runs - 1, runs)

    barrier = pltpu.get_barrier_semaphore()

    def greet(step, carry):
        q = lax.rem(q_me + step, planes)
        pl.semaphore_signal(barrier, inc=1, device_id=(plane_peer(q), kv), device_id_type=MESH)
        return carry

    lax.fori_loop(1, planes, greet, 0)
    pl.semaphore_signal(barrier, inc=1, device_id=(ring_peer(z_right), kv), device_id_type=MESH)
    pl.semaphore_signal(barrier, inc=1, device_id=(ring_peer(z_left), kv), device_id_type=MESH)
    kv_count = lax.axis_size("kv")

    def greet_kv(step, carry):
        peer = lax.rem(kv + step, kv_count)
        pl.semaphore_signal(barrier, inc=1, device_id=(me, peer), device_id_type=MESH)
        return carry

    lax.fori_loop(1, kv_count, greet_kv, 0)
    pl.semaphore_wait(barrier, planes + 1 + kv_count - 1)

    local = pltpu.make_async_copy(src_ref, out_ref.at[z_me, q_me], local_sem)
    local.start()
    caches = ((kc_ref, kc_out), (vc_ref, vc_out))
    local_cache = []
    for which, (cache_src, cache_dst) in enumerate(caches):
        c = pltpu.make_async_copy(cache_src.at[kv], cache_dst.at[kv], kv_local.at[which])
        c.start()
        local_cache.append(c)


    def send(step, carry):
        q = lax.rem(q_me + step, planes)
        remote(src_ref, out_ref.at[z_me, q_me], s1_send.at[step - 1], s1_recv.at[step - 1],
               (plane_peer(q), kv)).start()
        return carry

    lax.fori_loop(1, planes, send, 0)

    def finish(step, carry):
        q = lax.rem(q_me + step, planes)
        source = lax.rem(q_me + planes - step, planes)
        remote(src_ref, out_ref.at[z_me, q_me], s1_send.at[step - 1], s1_recv.at[step - 1],
               (plane_peer(q), kv)).wait_send()
        remote(src_ref, out_ref.at[z_me, source], s1_send.at[step - 1], s1_recv.at[step - 1],
               (plane_peer(source), kv)).wait_recv()
        return carry

    lax.fori_loop(1, planes, finish, 0)
    local.wait()

    split = 2 if planes % 2 == 0 else 1
    share = planes // split

    def ring_copy(z_block, h, send, recv, k, z_to):
        part = out_ref.at[z_block, pl.ds(h * share, share)]
        return remote(part, part, send.at[k, h], recv.at[k, h], (ring_peer(z_to), kv))

    if split == 2:
        right_of = (right_hops, left_hops)
        left_of = (left_hops, right_hops)
    else:
        right_of = (right_hops,)
        left_of = (left_hops,)
    sent = []
    for h in range(split):
        if right_of[h] > 0:
            c = ring_copy(z_me, h, r_send, r_recv, 0, z_right)
            c.start()
            sent.append(c)
        if left_of[h] > 0:
            c = ring_copy(z_me, h, l_send, l_recv, 0, z_left)
            c.start()
            sent.append(c)

    def send_kv(step, carry):
        peer = lax.rem(kv + step, kv_count)
        for which, (cache_src, cache_dst) in enumerate(caches):
            remote(cache_src.at[peer], cache_dst.at[kv], kv_send.at[which, step - 1],
                   kv_recv.at[which, step - 1], (me, peer)).start()
        return carry

    lax.fori_loop(1, kv_count, send_kv, 0)
    for k in range(1, max(right_of + left_of) + 1):
        for h in range(split):
            if k <= right_of[h]:
                z_from = lax.rem(z_me + runs - k, runs)
                ring_copy(z_from, h, r_send, r_recv, k - 1, z_right).wait_recv()
                if k < right_of[h]:
                    c = ring_copy(z_from, h, r_send, r_recv, k, z_right)
                    c.start()
                    sent.append(c)
            if k <= left_of[h]:
                z_from = lax.rem(z_me + k, runs)
                ring_copy(z_from, h, l_send, l_recv, k - 1, z_left).wait_recv()
                if k < left_of[h]:
                    c = ring_copy(z_from, h, l_send, l_recv, k, z_left)
                    c.start()
                    sent.append(c)
    for c in sent:
        c.wait_send()

    def finish_kv(step, carry):
        peer = lax.rem(kv + step, kv_count)
        source = lax.rem(kv + kv_count - step, kv_count)
        for which, (cache_src, cache_dst) in enumerate(caches):
            remote(cache_src.at[peer], cache_dst.at[kv], kv_send.at[which, step - 1],
                   kv_recv.at[which, step - 1], (me, peer)).wait_send()
            remote(cache_src.at[kv], cache_dst.at[source], kv_send.at[which, step - 1],
                   kv_recv.at[which, step - 1], (me, source)).wait_recv()
        return carry

    lax.fori_loop(1, kv_count, finish_kv, 0)
    for c in local_cache:
        c.wait()


def gather_req(piece, keys_send, values_send):
    count = lax.axis_size("req")
    kv_count = lax.axis_size("kv")
    runs = min(Z_RUN, count // Y_RUN)
    planes = count // runs
    rows, width = piece.shape
    hops = max(runs - 1, 1)
    anywhere = pl.BlockSpec(memory_space=pl.ANY)
    gathered, keys_old, values_old = pl.pallas_call(
        functools.partial(plane_ring_kernel, planes, runs),
        out_shape=(
            jax.ShapeDtypeStruct((runs, planes, rows, width), piece.dtype),
            jax.ShapeDtypeStruct(keys_send.shape, keys_send.dtype),
            jax.ShapeDtypeStruct(values_send.shape, values_send.dtype),
        ),
        in_specs=[anywhere, anywhere, anywhere],
        out_specs=(anywhere, anywhere, anywhere),
        scratch_shapes=[
            pltpu.SemaphoreType.DMA((planes - 1,)),
            pltpu.SemaphoreType.DMA((planes - 1,)),
            pltpu.SemaphoreType.DMA((hops, 2)),
            pltpu.SemaphoreType.DMA((hops, 2)),
            pltpu.SemaphoreType.DMA((hops, 2)),
            pltpu.SemaphoreType.DMA((hops, 2)),
            pltpu.SemaphoreType.DMA,
            pltpu.SemaphoreType.DMA((2, kv_count - 1)),
            pltpu.SemaphoreType.DMA((2, kv_count - 1)),
            pltpu.SemaphoreType.DMA((2,)),
        ],
        compiler_params=pltpu.CompilerParams(collective_id=0, has_side_effects=True),
    )(piece, keys_send, values_send)
    return gathered.reshape(count * rows, width), keys_old, values_old


def req_order(block, count, piece_rows):
    runs = min(Z_RUN, count // Y_RUN)
    x_count = count // (runs * Y_RUN)
    shaped = block.reshape(runs, x_count, Y_RUN, piece_rows, block.shape[1])
    return jnp.transpose(shaped, (1, 0, 2, 3, 4)).reshape(block.shape)


def gathered_order(normed, count, piece_rows):
    runs = min(Z_RUN, count // Y_RUN)
    x_count = count // (runs * Y_RUN)
    rows = normed.shape[0]
    shaped = normed.reshape(rows, x_count, runs, Y_RUN, piece_rows)
    return jnp.transpose(shaped, (0, 2, 1, 3, 4)).reshape(rows, -1)


BLOCK_Q = 512
BLOCK_K = 512


def flash_kernel(tokens, scale, len_ref, q_ref, kc_ref, vc_ref, kn_ref, vn_ref, o_ref):
    block_q = q_ref.shape[1]
    block_k = kc_ref.shape[2]
    width = q_ref.shape[2]
    i = pl.program_id(1)
    length = len_ref[0]
    first = lax.rem(i * block_q, tokens)
    q = q_ref[0]
    query_index = first + lax.broadcasted_iota(jnp.int32, (block_q, block_k), 0)
    key_offset = lax.broadcasted_iota(jnp.int32, (block_q, block_k), 1)

    def step(keys, values, visible, carry):
        peak, total, acc = carry
        score = lax.dot_general(
            q, keys, (((1,), (1,)), ((), ())), preferred_element_type=jnp.float32
        ) * scale
        score = jnp.where(visible, score, masked_score)
        new_peak = jnp.maximum(peak, jnp.max(score, axis=1, keepdims=True))
        alpha = jnp.exp(peak - new_peak)
        weights = jnp.where(visible, jnp.exp(score - new_peak), 0.0)
        total = alpha * total + jnp.sum(weights, axis=1, keepdims=True)
        acc = alpha * acc + jnp.dot(
            weights.astype(jnp.bfloat16), values, preferred_element_type=jnp.float32
        )
        return new_peak, total, acc

    def cache_step(block, carry):
        start = pl.multiple_of(block * block_k, block_k)
        keys = kc_ref[block, 0]
        values = vc_ref[block, 0]
        visible = start + key_offset < length
        return step(keys, values, visible, carry)

    def new_step(block, carry):
        start = pl.multiple_of(block * block_k, block_k)
        keys = kn_ref[0, pl.ds(start, block_k), :]
        values = vn_ref[0, pl.ds(start, block_k), :]
        visible = start + key_offset <= query_index
        return step(keys, values, visible, carry)

    carry = (
        jnp.full((block_q, 1), -jnp.inf, jnp.float32),
        jnp.zeros((block_q, 1), jnp.float32),
        jnp.zeros((block_q, width), jnp.float32),
    )
    live_blocks = (length + block_k - 1) // block_k
    carry = lax.fori_loop(0, live_blocks, cache_step, carry)
    new_blocks = (first + block_q - 1) // block_k + 1
    peak, total, acc = lax.fori_loop(0, new_blocks, new_step, carry)
    o_ref[0] = (acc / total).astype(o_ref.dtype)


def flash_attention(lengths, queries, keys_old, values_old, keys_new, values_new, tokens, scale):
    heads, rows, width = queries.shape
    blocks, _, block_k, _ = keys_old.shape
    slots = blocks * block_k
    block_q = min(BLOCK_Q, tokens)
    grid = (heads, rows // block_q)
    whole_cache = pl.BlockSpec((blocks, 1, block_k, width), lambda c, i, n: (0, c, 0, 0))
    whole_new = pl.BlockSpec((1, tokens, width), lambda c, i, n: (c, 0, 0))
    return pl.pallas_call(
        functools.partial(flash_kernel, tokens, scale),
        out_shape=jax.ShapeDtypeStruct((heads, rows, width), jnp.bfloat16),
        grid_spec=pltpu.PrefetchScalarGridSpec(
            num_scalar_prefetch=1,
            grid=grid,
            in_specs=[
                pl.BlockSpec((1, block_q, width), lambda c, i, n: (c, i, 0)),
                whole_cache, whole_cache, whole_new, whole_new,
            ],
            out_specs=pl.BlockSpec((1, block_q, width), lambda c, i, n: (c, i, 0)),
        ),
        cost_estimate=pl.CostEstimate(
            flops=4 * heads * rows * (slots + tokens) * width,
            transcendentals=heads * rows * (slots + tokens),
            bytes_accessed=2 * width * heads * (2 * rows + 2 * slots + 2 * tokens),
        ),
    )(lengths, queries, keys_old, values_old, keys_new, values_new)


def body(hidden, lengths, key_cache, value_cache, norm_gain, w_query, w_key, w_value, w_out):
    rows_here = hidden.shape[1]
    kv_count = lax.axis_size("kv")
    appended = rows_here * kv_count
    slots = key_cache.shape[1]
    groups = H // KVH
    scale = HD ** (-0.5)
    length = lengths[0]
    q_cols = w_query.shape[1]
    k_cols = w_key.shape[1]
    v_cols = w_value.shape[1]
    heads_here = q_cols // HD
    kv_heads_here = k_cols // HD

    normed = rms_norm(hidden[0].astype(jnp.float32), norm_gain)
    normed = gathered_order(normed, lax.axis_size("req"), w_query.shape[0])
    normed_all = lax.all_gather(normed, "kv", axis=0, tiled=True)

    pieces = jnp.concatenate([w_query, w_key, w_value, w_out], axis=1)
    def to_peers(cache):
        return jnp.transpose(
            cache.reshape(slots, kv_count, kv_heads_here, HD), (1, 2, 0, 3)
        )

    cols, keys_old, values_old = gather_req(
        pieces, to_peers(key_cache[0]), to_peers(value_cache[0])
    )
    wq = cols[:, :q_cols]
    wk = cols[:, q_cols:q_cols + k_cols]
    wv = cols[:, q_cols + k_cols:q_cols + k_cols + v_cols]
    wo = req_order(cols[:, q_cols + k_cols + v_cols:], lax.axis_size("req"), w_query.shape[0])

    wo_full = lax.all_gather(wo, "kv", axis=1, tiled=True)

    positions = (length + jnp.arange(appended, dtype=jnp.int32)).astype(jnp.float32)
    half = HD // 2
    frequency = rope_base ** (-(jnp.arange(half, dtype=jnp.float32) * 2.0 / HD))
    angle = positions[:, None] * frequency[None, :]
    cosine = jnp.cos(angle)
    sine = jnp.sin(angle)

    def turn(values):
        first = values[..., :half]
        second = values[..., half:]
        return jnp.concatenate(
            [first * cosine - second * sine, second * cosine + first * sine], axis=-1
        )

    width = normed_all.shape[1]
    proj_q = jnp.einsum(
        "td,dcgh->cgth", normed_all, wq.reshape(width, kv_heads_here, groups, HD),
        preferred_element_type=jnp.float32,
    )
    proj_k = jnp.einsum(
        "td,dch->cth", normed_all, wk.reshape(width, kv_heads_here, HD),
        preferred_element_type=jnp.float32,
    )
    proj_v = jnp.einsum(
        "td,dch->cth", normed_all, wv.reshape(width, kv_heads_here, HD),
        preferred_element_type=jnp.float32,
    )
    query_heads = turn(proj_q).astype(jnp.bfloat16).reshape(kv_heads_here, groups * appended, HD)
    keys_new = turn(proj_k).astype(jnp.bfloat16)
    values_new = proj_v.astype(jnp.bfloat16)

    def to_tokens(values):
        parts = values.reshape(kv_heads_here, kv_count, rows_here, HD)
        got = lax.all_to_all(parts, "kv", split_axis=1, concat_axis=1, tiled=True)
        return jnp.transpose(got, (2, 1, 0, 3)).reshape(rows_here, kv_count * kv_heads_here * HD)

    new_keys = to_tokens(keys_new)
    new_values = to_tokens(values_new)

    contexts = flash_attention(
        lengths, query_heads, keys_old, values_old, keys_new, values_new, appended, scale,
    )
    parts = contexts.reshape(kv_heads_here, groups, kv_count, rows_here, HD)
    got = lax.all_to_all(parts, "kv", split_axis=2, concat_axis=2, tiled=True)
    attended = jnp.einsum(
        "cgsth,scghn->tn", got,
        wo_full.reshape(kv_count, kv_heads_here, groups, HD, wo_full.shape[1]),
        preferred_element_type=jnp.float32,
    ).astype(jnp.bfloat16)
    return (attended[None], new_keys[None], new_values[None])


def solution(mesh):
    return jax.shard_map(
        body,
        mesh=mesh,
        in_specs=(
            P("req", "kv", None),
            P("req"),
            P("req", "kv", None),
            P("req", "kv", None),
            P(),
            P("req", "kv"),
            P("req", "kv"),
            P("req", "kv"),
            P("req", "kv"),
        ),
        out_specs=(P("req", "kv", None), P("req", "kv", None), P("req", "kv", None)),
        check_vma=False,
    )
```

```python
import functools

import jax
import jax.numpy as jnp
from jax import lax
from jax.sharding import PartitionSpec as P
from jax.experimental import pallas as pl
from jax.experimental.pallas import tpu as pltpu

H = 16
KVH = 8
HD = 96


rope_base = 100000.0
masked_score = -1e30


def rms_norm(states, gain):
    mean_square = jnp.mean(states * states, axis=-1, keepdims=True)
    scaled = states * lax.rsqrt(mean_square + 1e-05) * gain.astype(jnp.float32)
    return scaled.astype(jnp.bfloat16)


def rotate(values, positions):
    count = values.shape[0]
    heads = values.shape[1] // HD
    half = HD // 2
    frequency = rope_base ** (-(jnp.arange(half, dtype=jnp.float32) * 2.0 / HD))
    angle = positions[:, None] * frequency[None, :]
    cosine = jnp.cos(angle)[:, None, :]
    sine = jnp.sin(angle)[:, None, :]
    shaped = values.reshape(count, heads, HD)
    first = shaped[..., :half]
    second = shaped[..., half:]
    turned = jnp.concatenate(
        [first * cosine - second * sine, second * cosine + first * sine], axis=-1
    )
    return turned.reshape(count, heads * HD)


Z_RUN = 8
Y_RUN = 2
MESH = pl.DeviceIdType.MESH


def remote(src, dst, send, recv, device):
    return pltpu.make_async_remote_copy(
        src_ref=src, dst_ref=dst, send_sem=send, recv_sem=recv,
        device_id=device, device_id_type=MESH,
    )


def plane_ring_kernel(planes, runs, src_ref, kc_ref, vc_ref, out_ref, kc_out, vc_out, s1_send,
                      s1_recv, r_send, r_recv, l_send, l_recv, local_sem, kv_send, kv_recv, kv_local):
    me = lax.axis_index("req")
    kv = lax.axis_index("kv")
    y_me = lax.rem(me, Y_RUN)
    z_me = lax.rem(me // Y_RUN, runs)
    x_me = me // (Y_RUN * runs)
    q_me = x_me * Y_RUN + y_me
    right_hops = runs // 2
    left_hops = runs - 1 - right_hops

    def plane_peer(q):
        return ((q // Y_RUN) * runs + z_me) * Y_RUN + lax.rem(q, Y_RUN)

    def ring_peer(z):
        return (x_me * runs + z) * Y_RUN + y_me

    z_right = lax.rem(z_me + 1, runs)
    z_left = lax.rem(z_me + runs - 1, runs)

    barrier = pltpu.get_barrier_semaphore()

    def greet(step, carry):
        q = lax.rem(q_me + step, planes)
        pl.semaphore_signal(barrier, inc=1, device_id=(plane_peer(q), kv), device_id_type=MESH)
        return carry

    lax.fori_loop(1, planes, greet, 0)
    pl.semaphore_signal(barrier, inc=1, device_id=(ring_peer(z_right), kv), device_id_type=MESH)
    pl.semaphore_signal(barrier, inc=1, device_id=(ring_peer(z_left), kv), device_id_type=MESH)
    kv_count = lax.axis_size("kv")

    def greet_kv(step, carry):
        peer = lax.rem(kv + step, kv_count)
        pl.semaphore_signal(barrier, inc=1, device_id=(me, peer), device_id_type=MESH)
        return carry

    lax.fori_loop(1, kv_count, greet_kv, 0)
    pl.semaphore_wait(barrier, planes + 1 + kv_count - 1)

    local = pltpu.make_async_copy(src_ref, out_ref.at[z_me, q_me], local_sem)
    local.start()
    caches = ((kc_ref, kc_out), (vc_ref, vc_out))
    local_cache = []
    for which, (cache_src, cache_dst) in enumerate(caches):
        c = pltpu.make_async_copy(cache_src.at[kv], cache_dst.at[kv], kv_local.at[which])
        c.start()
        local_cache.append(c)


    def send(step, carry):
        q = lax.rem(q_me + step, planes)
        remote(src_ref, out_ref.at[z_me, q_me], s1_send.at[step - 1], s1_recv.at[step - 1],
               (plane_peer(q), kv)).start()
        return carry

    lax.fori_loop(1, planes, send, 0)

    def finish(step, carry):
        q = lax.rem(q_me + step, planes)
        source = lax.rem(q_me + planes - step, planes)
        remote(src_ref, out_ref.at[z_me, q_me], s1_send.at[step - 1], s1_recv.at[step - 1],
               (plane_peer(q), kv)).wait_send()
        remote(src_ref, out_ref.at[z_me, source], s1_send.at[step - 1], s1_recv.at[step - 1],
               (plane_peer(source), kv)).wait_recv()
        return carry

    lax.fori_loop(1, planes, finish, 0)
    local.wait()

    split = 2 if planes % 2 == 0 else 1
    share = planes // split

    def ring_copy(z_block, h, send, recv, k, z_to):
        part = out_ref.at[z_block, pl.ds(h * share, share)]
        return remote(part, part, send.at[k, h], recv.at[k, h], (ring_peer(z_to), kv))

    if split == 2:
        right_of = (right_hops, left_hops)
        left_of = (left_hops, right_hops)
    else:
        right_of = (right_hops,)
        left_of = (left_hops,)
    sent = []
    for h in range(split):
        if right_of[h] > 0:
            c = ring_copy(z_me, h, r_send, r_recv, 0, z_right)
            c.start()
            sent.append(c)
        if left_of[h] > 0:
            c = ring_copy(z_me, h, l_send, l_recv, 0, z_left)
            c.start()
            sent.append(c)

    def send_kv(step, carry):
        peer = lax.rem(kv + step, kv_count)
        for which, (cache_src, cache_dst) in enumerate(caches):
            remote(cache_src.at[peer], cache_dst.at[kv], kv_send.at[which, step - 1],
                   kv_recv.at[which, step - 1], (me, peer)).start()
        return carry

    lax.fori_loop(1, kv_count, send_kv, 0)
    for k in range(1, max(right_of + left_of) + 1):
        for h in range(split):
            if k <= right_of[h]:
                z_from = lax.rem(z_me + runs - k, runs)
                ring_copy(z_from, h, r_send, r_recv, k - 1, z_right).wait_recv()
                if k < right_of[h]:
                    c = ring_copy(z_from, h, r_send, r_recv, k, z_right)
                    c.start()
                    sent.append(c)
            if k <= left_of[h]:
                z_from = lax.rem(z_me + k, runs)
                ring_copy(z_from, h, l_send, l_recv, k - 1, z_left).wait_recv()
                if k < left_of[h]:
                    c = ring_copy(z_from, h, l_send, l_recv, k, z_left)
                    c.start()
                    sent.append(c)
    for c in sent:
        c.wait_send()

    def finish_kv(step, carry):
        peer = lax.rem(kv + step, kv_count)
        source = lax.rem(kv + kv_count - step, kv_count)
        for which, (cache_src, cache_dst) in enumerate(caches):
            remote(cache_src.at[peer], cache_dst.at[kv], kv_send.at[which, step - 1],
                   kv_recv.at[which, step - 1], (me, peer)).wait_send()
            remote(cache_src.at[kv], cache_dst.at[source], kv_send.at[which, step - 1],
                   kv_recv.at[which, step - 1], (me, source)).wait_recv()
        return carry

    lax.fori_loop(1, kv_count, finish_kv, 0)
    for c in local_cache:
        c.wait()


def gather_req(piece, keys_send, values_send):
    count = lax.axis_size("req")
    kv_count = lax.axis_size("kv")
    runs = min(Z_RUN, count // Y_RUN)
    planes = count // runs
    rows, width = piece.shape
    hops = max(runs - 1, 1)
    anywhere = pl.BlockSpec(memory_space=pl.ANY)
    gathered, keys_old, values_old = pl.pallas_call(
        functools.partial(plane_ring_kernel, planes, runs),
        out_shape=(
            jax.ShapeDtypeStruct((runs, planes, rows, width), piece.dtype),
            jax.ShapeDtypeStruct(keys_send.shape, keys_send.dtype),
            jax.ShapeDtypeStruct(values_send.shape, values_send.dtype),
        ),
        in_specs=[anywhere, anywhere, anywhere],
        out_specs=(anywhere, anywhere, anywhere),
        scratch_shapes=[
            pltpu.SemaphoreType.DMA((planes - 1,)),
            pltpu.SemaphoreType.DMA((planes - 1,)),
            pltpu.SemaphoreType.DMA((hops, 2)),
            pltpu.SemaphoreType.DMA((hops, 2)),
            pltpu.SemaphoreType.DMA((hops, 2)),
            pltpu.SemaphoreType.DMA((hops, 2)),
            pltpu.SemaphoreType.DMA,
            pltpu.SemaphoreType.DMA((2, kv_count - 1)),
            pltpu.SemaphoreType.DMA((2, kv_count - 1)),
            pltpu.SemaphoreType.DMA((2,)),
        ],
        compiler_params=pltpu.CompilerParams(collective_id=0, has_side_effects=True),
    )(piece, keys_send, values_send)
    return gathered.reshape(count * rows, width), keys_old, values_old


def req_order(block, count, piece_rows):
    runs = min(Z_RUN, count // Y_RUN)
    x_count = count // (runs * Y_RUN)
    shaped = block.reshape(runs, x_count, Y_RUN, piece_rows, block.shape[1])
    return jnp.transpose(shaped, (1, 0, 2, 3, 4)).reshape(block.shape)


def gathered_order(normed, count, piece_rows):
    runs = min(Z_RUN, count // Y_RUN)
    x_count = count // (runs * Y_RUN)
    rows = normed.shape[0]
    shaped = normed.reshape(rows, x_count, runs, Y_RUN, piece_rows)
    return jnp.transpose(shaped, (0, 2, 1, 3, 4)).reshape(rows, -1)


BLOCK_Q = 512
BLOCK_K = 512


def flash_kernel(tokens, scale, len_ref, q_ref, kc_ref, vc_ref, kn_ref, vn_ref, o_ref):
    block_q = q_ref.shape[1]
    block_k = kc_ref.shape[2]
    width = q_ref.shape[2]
    i = pl.program_id(1)
    length = len_ref[0]
    first = lax.rem(i * block_q, tokens)
    q = q_ref[0]
    query_index = first + lax.broadcasted_iota(jnp.int32, (block_q, block_k), 0)
    key_offset = lax.broadcasted_iota(jnp.int32, (block_q, block_k), 1)

    def step(keys, values, visible, carry):
        peak, total, acc = carry
        score = lax.dot_general(
            q, keys, (((1,), (1,)), ((), ())), preferred_element_type=jnp.float32
        ) * scale
        score = jnp.where(visible, score, masked_score)
        new_peak = jnp.maximum(peak, jnp.max(score, axis=1, keepdims=True))
        alpha = jnp.exp(peak - new_peak)
        weights = jnp.where(visible, jnp.exp(score - new_peak), 0.0)
        total = alpha * total + jnp.sum(weights, axis=1, keepdims=True)
        acc = alpha * acc + jnp.dot(
            weights.astype(jnp.bfloat16), values, preferred_element_type=jnp.float32
        )
        return new_peak, total, acc

    def cache_step(block, carry):
        start = pl.multiple_of(block * block_k, block_k)
        keys = kc_ref[block, 0]
        values = vc_ref[block, 0]
        visible = start + key_offset < length
        return step(keys, values, visible, carry)

    block_n = kn_ref.shape[2]
    query_new = first + lax.broadcasted_iota(jnp.int32, (block_q, block_n), 0)
    offset_new = lax.broadcasted_iota(jnp.int32, (block_q, block_n), 1)

    def new_step(block, carry):
        visible = block * block_n + offset_new <= query_new
        return step(kn_ref[block, 0], vn_ref[block, 0], visible, carry)

    carry = (
        jnp.full((block_q, 1), -jnp.inf, jnp.float32),
        jnp.zeros((block_q, 1), jnp.float32),
        jnp.zeros((block_q, width), jnp.float32),
    )
    live_blocks = (length + block_k - 1) // block_k
    carry = lax.fori_loop(0, live_blocks, cache_step, carry)
    new_blocks = (first + block_q - 1) // block_n + 1
    peak, total, acc = lax.fori_loop(0, new_blocks, new_step, carry)
    o_ref[0] = (acc / total).astype(o_ref.dtype)


def flash_attention(lengths, queries, keys_old, values_old, keys_new, values_new, tokens, scale):
    heads, rows, width = queries.shape
    blocks, _, block_k, _ = keys_old.shape
    slots = blocks * block_k
    block_q = min(BLOCK_Q, tokens)
    grid = (heads, rows // block_q)
    whole_cache = pl.BlockSpec((blocks, 1, block_k, width), lambda c, i, n: (0, c, 0, 0))
    peers, _, block_n, _ = keys_new.shape
    whole_new = pl.BlockSpec((peers, 1, block_n, width), lambda c, i, n: (0, c, 0, 0))
    return pl.pallas_call(
        functools.partial(flash_kernel, tokens, scale),
        out_shape=jax.ShapeDtypeStruct((heads, rows, width), jnp.bfloat16),
        grid_spec=pltpu.PrefetchScalarGridSpec(
            num_scalar_prefetch=1,
            grid=grid,
            in_specs=[
                pl.BlockSpec((1, block_q, width), lambda c, i, n: (c, i, 0)),
                whole_cache, whole_cache, whole_new, whole_new,
            ],
            out_specs=pl.BlockSpec((1, block_q, width), lambda c, i, n: (c, i, 0)),
        ),
        cost_estimate=pl.CostEstimate(
            flops=4 * heads * rows * (slots + tokens) * width,
            transcendentals=heads * rows * (slots + tokens),
            bytes_accessed=2 * width * heads * (2 * rows + 2 * slots + 2 * tokens),
        ),
    )(lengths, queries, keys_old, values_old, keys_new, values_new)


def exchange_kernel(k_ref, v_ref, k_out, v_out, send_sem, recv_sem, local_sem):
    me = lax.axis_index("kv")
    req = lax.axis_index("req")
    count = lax.axis_size("kv")
    arrays = ((k_ref, k_out), (v_ref, v_out))
    barrier = pltpu.get_barrier_semaphore()

    def greet(step, carry):
        peer = lax.rem(me + step, count)
        pl.semaphore_signal(barrier, inc=1, device_id=(req, peer), device_id_type=MESH)
        return carry

    lax.fori_loop(1, count, greet, 0)
    pl.semaphore_wait(barrier, count - 1)
    local = []
    for which, (src, dst) in enumerate(arrays):
        c = pltpu.make_async_copy(src.at[me], dst.at[me], local_sem.at[which])
        c.start()
        local.append(c)

    def send(step, carry):
        peer = lax.rem(me + step, count)
        for which, (src, dst) in enumerate(arrays):
            remote(src.at[peer], dst.at[me], send_sem.at[which, step - 1],
                   recv_sem.at[which, step - 1], (req, peer)).start()
        return carry

    lax.fori_loop(1, count, send, 0)

    def finish(step, carry):
        peer = lax.rem(me + step, count)
        source = lax.rem(me + count - step, count)
        for which, (src, dst) in enumerate(arrays):
            remote(src.at[peer], dst.at[me], send_sem.at[which, step - 1],
                   recv_sem.at[which, step - 1], (req, peer)).wait_send()
            remote(src.at[me], dst.at[source], send_sem.at[which, step - 1],
                   recv_sem.at[which, step - 1], (req, source)).wait_recv()
        return carry

    lax.fori_loop(1, count, finish, 0)
    for c in local:
        c.wait()


def exchange_kv(keys, values):
    count = lax.axis_size("kv")
    anywhere = pl.BlockSpec(memory_space=pl.ANY)
    return pl.pallas_call(
        exchange_kernel,
        out_shape=tuple(jax.ShapeDtypeStruct(a.shape, a.dtype) for a in (keys, values)),
        in_specs=[anywhere, anywhere],
        out_specs=(anywhere, anywhere),
        scratch_shapes=[
            pltpu.SemaphoreType.DMA((2, count - 1)),
            pltpu.SemaphoreType.DMA((2, count - 1)),
            pltpu.SemaphoreType.DMA((2,)),
        ],
        compiler_params=pltpu.CompilerParams(collective_id=1, has_side_effects=True),
    )(keys, values)


def body(hidden, lengths, key_cache, value_cache, norm_gain, w_query, w_key, w_value, w_out):
    rows_here = hidden.shape[1]
    kv_count = lax.axis_size("kv")
    appended = rows_here * kv_count
    slots = key_cache.shape[1]
    groups = H // KVH
    scale = HD ** (-0.5)
    length = lengths[0]
    q_cols = w_query.shape[1]
    k_cols = w_key.shape[1]
    v_cols = w_value.shape[1]
    heads_here = q_cols // HD
    kv_heads_here = k_cols // HD

    normed = rms_norm(hidden[0].astype(jnp.float32), norm_gain)
    normed = gathered_order(normed, lax.axis_size("req"), w_query.shape[0])
    normed_all = lax.all_gather(normed, "kv", axis=0, tiled=True)

    pieces = jnp.concatenate([w_query, w_key, w_value, w_out], axis=1)
    def to_peers(cache):
        return jnp.transpose(
            cache.reshape(slots, kv_count, kv_heads_here, HD), (1, 2, 0, 3)
        )

    cols, keys_old, values_old = gather_req(
        pieces, to_peers(key_cache[0]), to_peers(value_cache[0])
    )
    wq = cols[:, :q_cols]
    wk = cols[:, q_cols:q_cols + k_cols]
    wv = cols[:, q_cols + k_cols:q_cols + k_cols + v_cols]
    wo = req_order(cols[:, q_cols + k_cols + v_cols:], lax.axis_size("req"), w_query.shape[0])

    wo_full = lax.all_gather(wo, "kv", axis=1, tiled=True)

    positions = (length + jnp.arange(appended, dtype=jnp.int32)).astype(jnp.float32)
    half = HD // 2
    frequency = rope_base ** (-(jnp.arange(half, dtype=jnp.float32) * 2.0 / HD))
    angle = positions[:, None] * frequency[None, :]
    cosine = jnp.cos(angle)
    sine = jnp.sin(angle)

    def turn(values):
        first = values[..., :half]
        second = values[..., half:]
        return jnp.concatenate(
            [first * cosine - second * sine, second * cosine + first * sine], axis=-1
        )

    width = normed_all.shape[1]
    proj_q = jnp.einsum(
        "td,dcgh->cgth", normed_all, wq.reshape(width, kv_heads_here, groups, HD),
        preferred_element_type=jnp.float32,
    )
    normed_blocks = normed_all.reshape(kv_count, rows_here, width)
    proj_k = jnp.einsum(
        "std,dch->scth", normed_blocks, wk.reshape(width, kv_heads_here, HD),
        preferred_element_type=jnp.float32,
    )
    proj_v = jnp.einsum(
        "std,dch->scth", normed_blocks, wv.reshape(width, kv_heads_here, HD),
        preferred_element_type=jnp.float32,
    )
    cosine_blocks = cosine.reshape(kv_count, 1, rows_here, half)
    sine_blocks = sine.reshape(kv_count, 1, rows_here, half)
    query_heads = turn(proj_q).astype(jnp.bfloat16).reshape(kv_heads_here, groups * appended, HD)
    first_k = proj_k[..., :half]
    second_k = proj_k[..., half:]
    keys_new = jnp.concatenate(
        [first_k * cosine_blocks - second_k * sine_blocks,
         second_k * cosine_blocks + first_k * sine_blocks], axis=-1,
    ).astype(jnp.bfloat16)
    values_new = proj_v.astype(jnp.bfloat16)

    keys_got, values_got = exchange_kv(keys_new, values_new)

    def to_tokens(values):
        return jnp.transpose(values, (2, 0, 1, 3)).reshape(rows_here, kv_count * kv_heads_here * HD)

    new_keys = to_tokens(keys_got)
    new_values = to_tokens(values_got)

    contexts = flash_attention(
        lengths, query_heads, keys_old, values_old, keys_new, values_new, appended, scale,
    )
    parts = contexts.reshape(kv_heads_here, groups, kv_count, rows_here, HD)
    got = lax.all_to_all(parts, "kv", split_axis=2, concat_axis=2, tiled=True)
    attended = jnp.einsum(
        "cgsth,scghn->tn", got,
        wo_full.reshape(kv_count, kv_heads_here, groups, HD, wo_full.shape[1]),
        preferred_element_type=jnp.float32,
    ).astype(jnp.bfloat16)
    return (attended[None], new_keys[None], new_values[None])


def solution(mesh):
    return jax.shard_map(
        body,
        mesh=mesh,
        in_specs=(
            P("req", "kv", None),
            P("req"),
            P("req", "kv", None),
            P("req", "kv", None),
            P(),
            P("req", "kv"),
            P("req", "kv"),
            P("req", "kv"),
            P("req", "kv"),
        ),
        out_specs=(P("req", "kv", None), P("req", "kv", None), P("req", "kv", None)),
        check_vma=False,
    )
```

```python
import functools

import jax
import jax.numpy as jnp
from jax import lax
from jax.sharding import PartitionSpec as P
from jax.experimental import pallas as pl
from jax.experimental.pallas import tpu as pltpu

H = 16
KVH = 8
HD = 96


rope_base = 100000.0
masked_score = -1e30


def rms_norm(states, gain):
    mean_square = jnp.mean(states * states, axis=-1, keepdims=True)
    scaled = states * lax.rsqrt(mean_square + 1e-05) * gain.astype(jnp.float32)
    return scaled.astype(jnp.bfloat16)


def rotate(values, positions):
    count = values.shape[0]
    heads = values.shape[1] // HD
    half = HD // 2
    frequency = rope_base ** (-(jnp.arange(half, dtype=jnp.float32) * 2.0 / HD))
    angle = positions[:, None] * frequency[None, :]
    cosine = jnp.cos(angle)[:, None, :]
    sine = jnp.sin(angle)[:, None, :]
    shaped = values.reshape(count, heads, HD)
    first = shaped[..., :half]
    second = shaped[..., half:]
    turned = jnp.concatenate(
        [first * cosine - second * sine, second * cosine + first * sine], axis=-1
    )
    return turned.reshape(count, heads * HD)


Z_RUN = 8
Y_RUN = 2
MESH = pl.DeviceIdType.MESH


def remote(src, dst, send, recv, device):
    return pltpu.make_async_remote_copy(
        src_ref=src, dst_ref=dst, send_sem=send, recv_sem=recv,
        device_id=device, device_id_type=MESH,
    )


def plane_ring_kernel(planes, runs, src_ref, kc_ref, vc_ref, out_ref, kc_out, vc_out, s1_send,
                      s1_recv, r_send, r_recv, l_send, l_recv, local_sem, kv_send, kv_recv, kv_local):
    me = lax.axis_index("req")
    kv = lax.axis_index("kv")
    y_me = lax.rem(me, Y_RUN)
    z_me = lax.rem(me // Y_RUN, runs)
    x_me = me // (Y_RUN * runs)
    q_me = x_me * Y_RUN + y_me
    right_hops = runs // 2
    left_hops = runs - 1 - right_hops

    def plane_peer(q):
        return ((q // Y_RUN) * runs + z_me) * Y_RUN + lax.rem(q, Y_RUN)

    def ring_peer(z):
        return (x_me * runs + z) * Y_RUN + y_me

    z_right = lax.rem(z_me + 1, runs)
    z_left = lax.rem(z_me + runs - 1, runs)

    barrier = pltpu.get_barrier_semaphore()

    def greet(step, carry):
        q = lax.rem(q_me + step, planes)
        pl.semaphore_signal(barrier, inc=1, device_id=(plane_peer(q), kv), device_id_type=MESH)
        return carry

    lax.fori_loop(1, planes, greet, 0)
    pl.semaphore_signal(barrier, inc=1, device_id=(ring_peer(z_right), kv), device_id_type=MESH)
    pl.semaphore_signal(barrier, inc=1, device_id=(ring_peer(z_left), kv), device_id_type=MESH)
    kv_count = lax.axis_size("kv")

    def greet_kv(step, carry):
        peer = lax.rem(kv + step, kv_count)
        pl.semaphore_signal(barrier, inc=1, device_id=(me, peer), device_id_type=MESH)
        return carry

    lax.fori_loop(1, kv_count, greet_kv, 0)
    pl.semaphore_wait(barrier, planes + 1 + kv_count - 1)

    local = pltpu.make_async_copy(src_ref, out_ref.at[z_me, q_me], local_sem)
    local.start()
    caches = ((kc_ref, kc_out), (vc_ref, vc_out))
    local_cache = []
    for which, (cache_src, cache_dst) in enumerate(caches):
        c = pltpu.make_async_copy(cache_src.at[kv], cache_dst.at[kv], kv_local.at[which])
        c.start()
        local_cache.append(c)


    def send(step, carry):
        q = lax.rem(q_me + step, planes)
        remote(src_ref, out_ref.at[z_me, q_me], s1_send.at[step - 1], s1_recv.at[step - 1],
               (plane_peer(q), kv)).start()
        return carry

    lax.fori_loop(1, planes, send, 0)

    def finish(step, carry):
        q = lax.rem(q_me + step, planes)
        source = lax.rem(q_me + planes - step, planes)
        remote(src_ref, out_ref.at[z_me, q_me], s1_send.at[step - 1], s1_recv.at[step - 1],
               (plane_peer(q), kv)).wait_send()
        remote(src_ref, out_ref.at[z_me, source], s1_send.at[step - 1], s1_recv.at[step - 1],
               (plane_peer(source), kv)).wait_recv()
        return carry

    lax.fori_loop(1, planes, finish, 0)
    local.wait()

    split = 2 if planes % 2 == 0 else 1
    share = planes // split

    def ring_copy(z_block, h, send, recv, k, z_to):
        part = out_ref.at[z_block, pl.ds(h * share, share)]
        return remote(part, part, send.at[k, h], recv.at[k, h], (ring_peer(z_to), kv))

    if split == 2:
        right_of = (right_hops, left_hops)
        left_of = (left_hops, right_hops)
    else:
        right_of = (right_hops,)
        left_of = (left_hops,)
    sent = []
    for h in range(split):
        if right_of[h] > 0:
            c = ring_copy(z_me, h, r_send, r_recv, 0, z_right)
            c.start()
            sent.append(c)
        if left_of[h] > 0:
            c = ring_copy(z_me, h, l_send, l_recv, 0, z_left)
            c.start()
            sent.append(c)

    def send_kv(step, carry):
        peer = lax.rem(kv + step, kv_count)
        for which, (cache_src, cache_dst) in enumerate(caches):
            remote(cache_src.at[peer], cache_dst.at[kv], kv_send.at[which, step - 1],
                   kv_recv.at[which, step - 1], (me, peer)).start()
        return carry

    lax.fori_loop(1, kv_count, send_kv, 0)
    for k in range(1, max(right_of + left_of) + 1):
        for h in range(split):
            if k <= right_of[h]:
                z_from = lax.rem(z_me + runs - k, runs)
                ring_copy(z_from, h, r_send, r_recv, k - 1, z_right).wait_recv()
                if k < right_of[h]:
                    c = ring_copy(z_from, h, r_send, r_recv, k, z_right)
                    c.start()
                    sent.append(c)
            if k <= left_of[h]:
                z_from = lax.rem(z_me + k, runs)
                ring_copy(z_from, h, l_send, l_recv, k - 1, z_left).wait_recv()
                if k < left_of[h]:
                    c = ring_copy(z_from, h, l_send, l_recv, k, z_left)
                    c.start()
                    sent.append(c)
    for c in sent:
        c.wait_send()

    def finish_kv(step, carry):
        peer = lax.rem(kv + step, kv_count)
        source = lax.rem(kv + kv_count - step, kv_count)
        for which, (cache_src, cache_dst) in enumerate(caches):
            remote(cache_src.at[peer], cache_dst.at[kv], kv_send.at[which, step - 1],
                   kv_recv.at[which, step - 1], (me, peer)).wait_send()
            remote(cache_src.at[kv], cache_dst.at[source], kv_send.at[which, step - 1],
                   kv_recv.at[which, step - 1], (me, source)).wait_recv()
        return carry

    lax.fori_loop(1, kv_count, finish_kv, 0)
    for c in local_cache:
        c.wait()


def gather_req(piece, keys_send, values_send):
    count = lax.axis_size("req")
    kv_count = lax.axis_size("kv")
    runs = min(Z_RUN, count // Y_RUN)
    planes = count // runs
    rows, width = piece.shape
    hops = max(runs - 1, 1)
    anywhere = pl.BlockSpec(memory_space=pl.ANY)
    gathered, keys_old, values_old = pl.pallas_call(
        functools.partial(plane_ring_kernel, planes, runs),
        out_shape=(
            jax.ShapeDtypeStruct((runs, planes, rows, width), piece.dtype),
            jax.ShapeDtypeStruct(keys_send.shape, keys_send.dtype),
            jax.ShapeDtypeStruct(values_send.shape, values_send.dtype),
        ),
        in_specs=[anywhere, anywhere, anywhere],
        out_specs=(anywhere, anywhere, anywhere),
        scratch_shapes=[
            pltpu.SemaphoreType.DMA((planes - 1,)),
            pltpu.SemaphoreType.DMA((planes - 1,)),
            pltpu.SemaphoreType.DMA((hops, 2)),
            pltpu.SemaphoreType.DMA((hops, 2)),
            pltpu.SemaphoreType.DMA((hops, 2)),
            pltpu.SemaphoreType.DMA((hops, 2)),
            pltpu.SemaphoreType.DMA,
            pltpu.SemaphoreType.DMA((2, kv_count - 1)),
            pltpu.SemaphoreType.DMA((2, kv_count - 1)),
            pltpu.SemaphoreType.DMA((2,)),
        ],
        compiler_params=pltpu.CompilerParams(collective_id=0, has_side_effects=True),
    )(piece, keys_send, values_send)
    return gathered.reshape(count * rows, width), keys_old, values_old


def req_order(block, count, piece_rows):
    runs = min(Z_RUN, count // Y_RUN)
    x_count = count // (runs * Y_RUN)
    shaped = block.reshape(runs, x_count, Y_RUN, piece_rows, block.shape[1])
    return jnp.transpose(shaped, (1, 0, 2, 3, 4)).reshape(block.shape)


def gathered_order(normed, count, piece_rows):
    runs = min(Z_RUN, count // Y_RUN)
    x_count = count // (runs * Y_RUN)
    rows = normed.shape[0]
    shaped = normed.reshape(rows, x_count, runs, Y_RUN, piece_rows)
    return jnp.transpose(shaped, (0, 2, 1, 3, 4)).reshape(rows, -1)


BLOCK_Q = 1024
BLOCK_K = 512


def flash_kernel(tokens, scale, len_ref, q_ref, kc_ref, vc_ref, kn_ref, vn_ref, o_ref):
    block_q = q_ref.shape[1]
    block_k = kc_ref.shape[2]
    width = q_ref.shape[2]
    i = pl.program_id(1)
    length = len_ref[0]
    first = lax.rem(i * block_q, tokens)
    q = q_ref[0]
    query_index = first + lax.broadcasted_iota(jnp.int32, (block_q, block_k), 0)
    key_offset = lax.broadcasted_iota(jnp.int32, (block_q, block_k), 1)

    def step(keys, values, visible, carry):
        peak, total, acc = carry
        score = lax.dot_general(
            q, keys, (((1,), (1,)), ((), ())), preferred_element_type=jnp.float32
        ) * scale
        score = jnp.where(visible, score, masked_score)
        new_peak = jnp.maximum(peak, jnp.max(score, axis=1, keepdims=True))
        alpha = jnp.exp(peak - new_peak)
        weights = jnp.where(visible, jnp.exp(score - new_peak), 0.0)
        total = alpha * total + jnp.sum(weights, axis=1, keepdims=True)
        acc = alpha * acc + jnp.dot(
            weights.astype(jnp.bfloat16), values, preferred_element_type=jnp.float32
        )
        return new_peak, total, acc

    def cache_step(block, carry):
        start = pl.multiple_of(block * block_k, block_k)
        keys = kc_ref[block, 0]
        values = vc_ref[block, 0]
        visible = start + key_offset < length
        return step(keys, values, visible, carry)

    def new_step(block, carry):
        start = pl.multiple_of(block * block_k, block_k)
        keys = kn_ref[0, pl.ds(start, block_k), :]
        values = vn_ref[0, pl.ds(start, block_k), :]
        visible = start + key_offset <= query_index
        return step(keys, values, visible, carry)

    carry = (
        jnp.full((block_q, 1), -jnp.inf, jnp.float32),
        jnp.zeros((block_q, 1), jnp.float32),
        jnp.zeros((block_q, width), jnp.float32),
    )
    live_blocks = (length + block_k - 1) // block_k
    carry = lax.fori_loop(0, live_blocks, cache_step, carry)
    new_blocks = (first + block_q - 1) // block_k + 1
    peak, total, acc = lax.fori_loop(0, new_blocks, new_step, carry)
    o_ref[0] = (acc / total).astype(o_ref.dtype)


def flash_attention(lengths, queries, keys_old, values_old, keys_new, values_new, tokens, scale):
    heads, rows, width = queries.shape
    blocks, _, block_k, _ = keys_old.shape
    slots = blocks * block_k
    block_q = min(BLOCK_Q, tokens)
    grid = (heads, rows // block_q)
    whole_cache = pl.BlockSpec((blocks, 1, block_k, width), lambda c, i, n: (0, c, 0, 0))
    whole_new = pl.BlockSpec((1, tokens, width), lambda c, i, n: (c, 0, 0))
    return pl.pallas_call(
        functools.partial(flash_kernel, tokens, scale),
        out_shape=jax.ShapeDtypeStruct((heads, rows, width), jnp.bfloat16),
        grid_spec=pltpu.PrefetchScalarGridSpec(
            num_scalar_prefetch=1,
            grid=grid,
            in_specs=[
                pl.BlockSpec((1, block_q, width), lambda c, i, n: (c, i, 0)),
                whole_cache, whole_cache, whole_new, whole_new,
            ],
            out_specs=pl.BlockSpec((1, block_q, width), lambda c, i, n: (c, i, 0)),
        ),
        cost_estimate=pl.CostEstimate(
            flops=4 * heads * rows * (slots + tokens) * width,
            transcendentals=heads * rows * (slots + tokens),
            bytes_accessed=2 * width * heads * (2 * rows + 2 * slots + 2 * tokens),
        ),
    )(lengths, queries, keys_old, values_old, keys_new, values_new)


def body(hidden, lengths, key_cache, value_cache, norm_gain, w_query, w_key, w_value, w_out):
    rows_here = hidden.shape[1]
    kv_count = lax.axis_size("kv")
    appended = rows_here * kv_count
    slots = key_cache.shape[1]
    groups = H // KVH
    scale = HD ** (-0.5)
    length = lengths[0]
    q_cols = w_query.shape[1]
    k_cols = w_key.shape[1]
    v_cols = w_value.shape[1]
    heads_here = q_cols // HD
    kv_heads_here = k_cols // HD

    normed = rms_norm(hidden[0].astype(jnp.float32), norm_gain)
    normed = gathered_order(normed, lax.axis_size("req"), w_query.shape[0])
    normed_all = lax.all_gather(normed, "kv", axis=0, tiled=True)

    pieces = jnp.concatenate([w_query, w_key, w_value, w_out], axis=1)
    def to_peers(cache):
        return jnp.transpose(
            cache.reshape(slots, kv_count, kv_heads_here, HD), (1, 2, 0, 3)
        )

    cols, keys_old, values_old = gather_req(
        pieces, to_peers(key_cache[0]), to_peers(value_cache[0])
    )
    wq = cols[:, :q_cols]
    wk = cols[:, q_cols:q_cols + k_cols]
    wv = cols[:, q_cols + k_cols:q_cols + k_cols + v_cols]
    wo = req_order(cols[:, q_cols + k_cols + v_cols:], lax.axis_size("req"), w_query.shape[0])

    wo_full = lax.all_gather(wo, "kv", axis=1, tiled=True)

    positions = (length + jnp.arange(appended, dtype=jnp.int32)).astype(jnp.float32)
    half = HD // 2
    frequency = rope_base ** (-(jnp.arange(half, dtype=jnp.float32) * 2.0 / HD))
    angle = positions[:, None] * frequency[None, :]
    cosine = jnp.cos(angle)
    sine = jnp.sin(angle)

    def turn(values):
        first = values[..., :half]
        second = values[..., half:]
        return jnp.concatenate(
            [first * cosine - second * sine, second * cosine + first * sine], axis=-1
        )

    width = normed_all.shape[1]
    proj_q = jnp.einsum(
        "td,dcgh->cgth", normed_all, wq.reshape(width, kv_heads_here, groups, HD),
        preferred_element_type=jnp.float32,
    )
    proj_k = jnp.einsum(
        "td,dch->cth", normed_all, wk.reshape(width, kv_heads_here, HD),
        preferred_element_type=jnp.float32,
    )
    proj_v = jnp.einsum(
        "td,dch->cth", normed_all, wv.reshape(width, kv_heads_here, HD),
        preferred_element_type=jnp.float32,
    )
    query_heads = turn(proj_q).astype(jnp.bfloat16).reshape(kv_heads_here, groups * appended, HD)
    keys_new = turn(proj_k).astype(jnp.bfloat16)
    values_new = proj_v.astype(jnp.bfloat16)

    def to_tokens(values):
        parts = values.reshape(kv_heads_here, kv_count, rows_here, HD)
        got = lax.all_to_all(parts, "kv", split_axis=1, concat_axis=1, tiled=True)
        return jnp.transpose(got, (2, 1, 0, 3)).reshape(rows_here, kv_count * kv_heads_here * HD)

    new_keys = to_tokens(keys_new)
    new_values = to_tokens(values_new)

    contexts = flash_attention(
        lengths, query_heads, keys_old, values_old, keys_new, values_new, appended, scale,
    )
    parts = contexts.reshape(kv_heads_here, groups, kv_count, rows_here, HD)
    got = lax.all_to_all(parts, "kv", split_axis=2, concat_axis=2, tiled=True)
    attended = jnp.einsum(
        "cgsth,scghn->tn", got,
        wo_full.reshape(kv_count, kv_heads_here, groups, HD, wo_full.shape[1]),
        preferred_element_type=jnp.float32,
    ).astype(jnp.bfloat16)
    return (attended[None], new_keys[None], new_values[None])


def solution(mesh):
    return jax.shard_map(
        body,
        mesh=mesh,
        in_specs=(
            P("req", "kv", None),
            P("req"),
            P("req", "kv", None),
            P("req", "kv", None),
            P(),
            P("req", "kv"),
            P("req", "kv"),
            P("req", "kv"),
            P("req", "kv"),
        ),
        out_specs=(P("req", "kv", None), P("req", "kv", None), P("req", "kv", None)),
        check_vma=False,
    )
```

```python
import functools

import jax
import jax.numpy as jnp
from jax import lax
from jax.sharding import PartitionSpec as P
from jax.experimental import pallas as pl
from jax.experimental.pallas import tpu as pltpu

H = 16
KVH = 8
HD = 96


rope_base = 100000.0
masked_score = -1e30


def rms_norm(states, gain):
    mean_square = jnp.mean(states * states, axis=-1, keepdims=True)
    scaled = states * lax.rsqrt(mean_square + 1e-05) * gain.astype(jnp.float32)
    return scaled.astype(jnp.bfloat16)


def rotate(values, positions):
    count = values.shape[0]
    heads = values.shape[1] // HD
    half = HD // 2
    frequency = rope_base ** (-(jnp.arange(half, dtype=jnp.float32) * 2.0 / HD))
    angle = positions[:, None] * frequency[None, :]
    cosine = jnp.cos(angle)[:, None, :]
    sine = jnp.sin(angle)[:, None, :]
    shaped = values.reshape(count, heads, HD)
    first = shaped[..., :half]
    second = shaped[..., half:]
    turned = jnp.concatenate(
        [first * cosine - second * sine, second * cosine + first * sine], axis=-1
    )
    return turned.reshape(count, heads * HD)


Z_RUN = 8
Y_RUN = 2
MESH = pl.DeviceIdType.MESH


def remote(src, dst, send, recv, device):
    return pltpu.make_async_remote_copy(
        src_ref=src, dst_ref=dst, send_sem=send, recv_sem=recv,
        device_id=device, device_id_type=MESH,
    )


def plane_ring_kernel(planes, runs, src_ref, kc_ref, vc_ref, out_ref, kc_out, vc_out, s1_send,
                      s1_recv, r_send, r_recv, l_send, l_recv, local_sem, kv_send, kv_recv, kv_local):
    me = lax.axis_index("req")
    kv = lax.axis_index("kv")
    y_me = lax.rem(me, Y_RUN)
    z_me = lax.rem(me // Y_RUN, runs)
    x_me = me // (Y_RUN * runs)
    q_me = x_me * Y_RUN + y_me
    right_hops = runs // 2
    left_hops = runs - 1 - right_hops

    def plane_peer(q):
        return ((q // Y_RUN) * runs + z_me) * Y_RUN + lax.rem(q, Y_RUN)

    def ring_peer(z):
        return (x_me * runs + z) * Y_RUN + y_me

    z_right = lax.rem(z_me + 1, runs)
    z_left = lax.rem(z_me + runs - 1, runs)

    barrier = pltpu.get_barrier_semaphore()

    def greet(step, carry):
        q = lax.rem(q_me + step, planes)
        pl.semaphore_signal(barrier, inc=1, device_id=(plane_peer(q), kv), device_id_type=MESH)
        return carry

    lax.fori_loop(1, planes, greet, 0)
    pl.semaphore_signal(barrier, inc=1, device_id=(ring_peer(z_right), kv), device_id_type=MESH)
    pl.semaphore_signal(barrier, inc=1, device_id=(ring_peer(z_left), kv), device_id_type=MESH)
    kv_count = lax.axis_size("kv")

    def greet_kv(step, carry):
        peer = lax.rem(kv + step, kv_count)
        pl.semaphore_signal(barrier, inc=1, device_id=(me, peer), device_id_type=MESH)
        return carry

    lax.fori_loop(1, kv_count, greet_kv, 0)
    pl.semaphore_wait(barrier, planes + 1 + kv_count - 1)

    local = pltpu.make_async_copy(src_ref, out_ref.at[z_me, q_me], local_sem)
    local.start()
    caches = ((kc_ref, kc_out), (vc_ref, vc_out))
    local_cache = []
    for which, (cache_src, cache_dst) in enumerate(caches):
        c = pltpu.make_async_copy(cache_src.at[kv], cache_dst.at[kv], kv_local.at[which])
        c.start()
        local_cache.append(c)


    def send(step, carry):
        q = lax.rem(q_me + step, planes)
        remote(src_ref, out_ref.at[z_me, q_me], s1_send.at[step - 1], s1_recv.at[step - 1],
               (plane_peer(q), kv)).start()
        return carry

    lax.fori_loop(1, planes, send, 0)

    def finish(step, carry):
        q = lax.rem(q_me + step, planes)
        source = lax.rem(q_me + planes - step, planes)
        remote(src_ref, out_ref.at[z_me, q_me], s1_send.at[step - 1], s1_recv.at[step - 1],
               (plane_peer(q), kv)).wait_send()
        remote(src_ref, out_ref.at[z_me, source], s1_send.at[step - 1], s1_recv.at[step - 1],
               (plane_peer(source), kv)).wait_recv()
        return carry

    lax.fori_loop(1, planes, finish, 0)
    local.wait()

    split = 2 if planes % 2 == 0 else 1
    share = planes // split

    def ring_copy(z_block, h, send, recv, k, z_to):
        part = out_ref.at[z_block, pl.ds(h * share, share)]
        return remote(part, part, send.at[k, h], recv.at[k, h], (ring_peer(z_to), kv))

    if split == 2:
        right_of = (right_hops, left_hops)
        left_of = (left_hops, right_hops)
    else:
        right_of = (right_hops,)
        left_of = (left_hops,)
    sent = []
    for h in range(split):
        if right_of[h] > 0:
            c = ring_copy(z_me, h, r_send, r_recv, 0, z_right)
            c.start()
            sent.append(c)
        if left_of[h] > 0:
            c = ring_copy(z_me, h, l_send, l_recv, 0, z_left)
            c.start()
            sent.append(c)

    def send_kv(step, carry):
        peer = lax.rem(kv + step, kv_count)
        for which, (cache_src, cache_dst) in enumerate(caches):
            remote(cache_src.at[peer], cache_dst.at[kv], kv_send.at[which, step - 1],
                   kv_recv.at[which, step - 1], (me, peer)).start()
        return carry

    lax.fori_loop(1, kv_count, send_kv, 0)
    for k in range(1, max(right_of + left_of) + 1):
        for h in range(split):
            if k <= right_of[h]:
                z_from = lax.rem(z_me + runs - k, runs)
                ring_copy(z_from, h, r_send, r_recv, k - 1, z_right).wait_recv()
                if k < right_of[h]:
                    c = ring_copy(z_from, h, r_send, r_recv, k, z_right)
                    c.start()
                    sent.append(c)
            if k <= left_of[h]:
                z_from = lax.rem(z_me + k, runs)
                ring_copy(z_from, h, l_send, l_recv, k - 1, z_left).wait_recv()
                if k < left_of[h]:
                    c = ring_copy(z_from, h, l_send, l_recv, k, z_left)
                    c.start()
                    sent.append(c)
    for c in sent:
        c.wait_send()

    def finish_kv(step, carry):
        peer = lax.rem(kv + step, kv_count)
        source = lax.rem(kv + kv_count - step, kv_count)
        for which, (cache_src, cache_dst) in enumerate(caches):
            remote(cache_src.at[peer], cache_dst.at[kv], kv_send.at[which, step - 1],
                   kv_recv.at[which, step - 1], (me, peer)).wait_send()
            remote(cache_src.at[kv], cache_dst.at[source], kv_send.at[which, step - 1],
                   kv_recv.at[which, step - 1], (me, source)).wait_recv()
        return carry

    lax.fori_loop(1, kv_count, finish_kv, 0)
    for c in local_cache:
        c.wait()


def gather_req(piece, keys_send, values_send):
    count = lax.axis_size("req")
    kv_count = lax.axis_size("kv")
    runs = min(Z_RUN, count // Y_RUN)
    planes = count // runs
    rows, width = piece.shape
    hops = max(runs - 1, 1)
    anywhere = pl.BlockSpec(memory_space=pl.ANY)
    gathered, keys_old, values_old = pl.pallas_call(
        functools.partial(plane_ring_kernel, planes, runs),
        out_shape=(
            jax.ShapeDtypeStruct((runs, planes, rows, width), piece.dtype),
            jax.ShapeDtypeStruct(keys_send.shape, keys_send.dtype),
            jax.ShapeDtypeStruct(values_send.shape, values_send.dtype),
        ),
        in_specs=[anywhere, anywhere, anywhere],
        out_specs=(anywhere, anywhere, anywhere),
        scratch_shapes=[
            pltpu.SemaphoreType.DMA((planes - 1,)),
            pltpu.SemaphoreType.DMA((planes - 1,)),
            pltpu.SemaphoreType.DMA((hops, 2)),
            pltpu.SemaphoreType.DMA((hops, 2)),
            pltpu.SemaphoreType.DMA((hops, 2)),
            pltpu.SemaphoreType.DMA((hops, 2)),
            pltpu.SemaphoreType.DMA,
            pltpu.SemaphoreType.DMA((2, kv_count - 1)),
            pltpu.SemaphoreType.DMA((2, kv_count - 1)),
            pltpu.SemaphoreType.DMA((2,)),
        ],
        compiler_params=pltpu.CompilerParams(collective_id=0, has_side_effects=True),
    )(piece, keys_send, values_send)
    return gathered.reshape(count * rows, width), keys_old, values_old


def req_order(block, count, piece_rows):
    runs = min(Z_RUN, count // Y_RUN)
    x_count = count // (runs * Y_RUN)
    shaped = block.reshape(runs, x_count, Y_RUN, piece_rows, block.shape[1])
    return jnp.transpose(shaped, (1, 0, 2, 3, 4)).reshape(block.shape)


def gathered_order(normed, count, piece_rows):
    runs = min(Z_RUN, count // Y_RUN)
    x_count = count // (runs * Y_RUN)
    rows = normed.shape[0]
    shaped = normed.reshape(rows, x_count, runs, Y_RUN, piece_rows)
    return jnp.transpose(shaped, (0, 2, 1, 3, 4)).reshape(rows, -1)


BLOCK_Q = 512
BLOCK_K = 512


def flash_kernel(tokens, scale, len_ref, q_ref, kc_ref, vc_ref, kn_ref, vn_ref, o_ref):
    block_q = q_ref.shape[1]
    block_k = kc_ref.shape[2]
    width = q_ref.shape[2]
    i = pl.program_id(1)
    length = len_ref[0]
    first = lax.rem(i * block_q, tokens)
    q = q_ref[0]
    query_index = first + lax.broadcasted_iota(jnp.int32, (block_q, block_k), 0)
    key_offset = lax.broadcasted_iota(jnp.int32, (block_q, block_k), 1)

    def step(keys, values, visible, carry):
        peak, total, acc = carry
        score = lax.dot_general(
            q, keys, (((1,), (1,)), ((), ())), preferred_element_type=jnp.float32
        ) * scale
        score = jnp.where(visible, score, masked_score)
        new_peak = jnp.maximum(peak, jnp.max(score, axis=1, keepdims=True))
        alpha = jnp.exp(peak - new_peak)
        weights = jnp.where(visible, jnp.exp(score - new_peak), 0.0)
        total = alpha * total + jnp.sum(weights, axis=1, keepdims=True)
        acc = alpha * acc + jnp.dot(
            weights.astype(jnp.bfloat16), values, preferred_element_type=jnp.float32
        )
        return new_peak, total, acc

    def cache_step(block, carry):
        start = pl.multiple_of(block * block_k, block_k)
        keys = kc_ref[block, 0]
        values = vc_ref[block, 0]
        visible = start + key_offset < length
        return step(keys, values, visible, carry)

    def new_step(block, carry):
        start = pl.multiple_of(block * block_k, block_k)
        keys = kn_ref[0, pl.ds(start, block_k), :]
        values = vn_ref[0, pl.ds(start, block_k), :]
        visible = start + key_offset <= query_index
        return step(keys, values, visible, carry)

    carry = (
        jnp.full((block_q, 1), -jnp.inf, jnp.float32),
        jnp.zeros((block_q, 1), jnp.float32),
        jnp.zeros((block_q, width), jnp.float32),
    )
    live_blocks = (length + block_k - 1) // block_k
    carry = lax.fori_loop(0, live_blocks, cache_step, carry)
    new_blocks = (first + block_q - 1) // block_k + 1
    peak, total, acc = lax.fori_loop(0, new_blocks, new_step, carry)
    o_ref[0] = (acc / total).astype(o_ref.dtype)


def flash_attention(lengths, queries, keys_old, values_old, keys_new, values_new, tokens, scale):
    heads, rows, width = queries.shape
    blocks, _, block_k, _ = keys_old.shape
    slots = blocks * block_k
    block_q = min(BLOCK_Q, tokens)
    grid = (heads, rows // block_q)
    whole_cache = pl.BlockSpec((blocks, 1, block_k, width), lambda c, i, n: (0, c, 0, 0))
    whole_new = pl.BlockSpec((1, tokens, width), lambda c, i, n: (c, 0, 0))
    return pl.pallas_call(
        functools.partial(flash_kernel, tokens, scale),
        out_shape=jax.ShapeDtypeStruct((heads, rows, width), jnp.bfloat16),
        grid_spec=pltpu.PrefetchScalarGridSpec(
            num_scalar_prefetch=1,
            grid=grid,
            in_specs=[
                pl.BlockSpec((1, block_q, width), lambda c, i, n: (c, i, 0)),
                whole_cache, whole_cache, whole_new, whole_new,
            ],
            out_specs=pl.BlockSpec((1, block_q, width), lambda c, i, n: (c, i, 0)),
        ),
        cost_estimate=pl.CostEstimate(
            flops=4 * heads * rows * (slots + tokens) * width,
            transcendentals=heads * rows * (slots + tokens),
            bytes_accessed=2 * width * heads * (2 * rows + 2 * slots + 2 * tokens),
        ),
    )(lengths, queries, keys_old, values_old, keys_new, values_new)


def body(hidden, lengths, key_cache, value_cache, norm_gain, w_query, w_key, w_value, w_out):
    rows_here = hidden.shape[1]
    kv_count = lax.axis_size("kv")
    appended = rows_here * kv_count
    slots = key_cache.shape[1]
    groups = H // KVH
    scale = HD ** (-0.5)
    length = lengths[0]
    q_cols = w_query.shape[1]
    k_cols = w_key.shape[1]
    v_cols = w_value.shape[1]
    heads_here = q_cols // HD
    kv_heads_here = k_cols // HD

    normed = rms_norm(hidden[0].astype(jnp.float32), norm_gain)
    normed = gathered_order(normed, lax.axis_size("req"), w_query.shape[0])
    normed_all = lax.all_gather(normed, "kv", axis=0, tiled=True)

    pieces = jnp.concatenate([w_query, w_key, w_value, w_out], axis=1)
    def to_peers(cache):
        return jnp.transpose(
            cache.reshape(slots, kv_count, kv_heads_here, HD), (1, 2, 0, 3)
        )

    cols, keys_old, values_old = gather_req(
        pieces, to_peers(key_cache[0]), to_peers(value_cache[0])
    )
    wq = cols[:, :q_cols]
    wk = cols[:, q_cols:q_cols + k_cols]
    wv = cols[:, q_cols + k_cols:q_cols + k_cols + v_cols]
    wo = req_order(cols[:, q_cols + k_cols + v_cols:], lax.axis_size("req"), w_query.shape[0])

    wo_full = lax.all_gather(wo, "kv", axis=1, tiled=True)

    positions = (length + jnp.arange(appended, dtype=jnp.int32)).astype(jnp.float32)
    half = HD // 2
    frequency = rope_base ** (-(jnp.arange(half, dtype=jnp.float32) * 2.0 / HD))
    angle = positions[:, None] * frequency[None, :]
    cosine = jnp.cos(angle)
    sine = jnp.sin(angle)

    def turn(values):
        first = values[..., :half]
        second = values[..., half:]
        return jnp.concatenate(
            [first * cosine - second * sine, second * cosine + first * sine], axis=-1
        )

    width = normed_all.shape[1]
    heads_qkv = (q_cols + k_cols + v_cols) // HD
    proj = jnp.einsum(
        "td,dnh->nth", normed_all, cols[:, :q_cols + k_cols + v_cols].reshape(width, heads_qkv, HD),
        preferred_element_type=jnp.float32,
    )
    proj_q = proj[:heads_here].reshape(kv_heads_here, groups, appended, HD)
    proj_k = proj[heads_here:heads_here + kv_heads_here]
    proj_v = proj[heads_here + kv_heads_here:]
    query_heads = turn(proj_q).astype(jnp.bfloat16).reshape(kv_heads_here, groups * appended, HD)
    keys_new = turn(proj_k).astype(jnp.bfloat16)
    values_new = proj_v.astype(jnp.bfloat16)

    def to_tokens(values):
        parts = values.reshape(kv_heads_here, kv_count, rows_here, HD)
        got = lax.all_to_all(parts, "kv", split_axis=1, concat_axis=1, tiled=True)
        return jnp.transpose(got, (2, 1, 0, 3)).reshape(rows_here, kv_count * kv_heads_here * HD)

    new_keys = to_tokens(keys_new)
    new_values = to_tokens(values_new)

    contexts = flash_attention(
        lengths, query_heads, keys_old, values_old, keys_new, values_new, appended, scale,
    )
    parts = contexts.reshape(kv_heads_here, groups, kv_count, rows_here, HD)
    got = lax.all_to_all(parts, "kv", split_axis=2, concat_axis=2, tiled=True)
    attended = jnp.einsum(
        "cgsth,scghn->tn", got,
        wo_full.reshape(kv_count, kv_heads_here, groups, HD, wo_full.shape[1]),
        preferred_element_type=jnp.float32,
    ).astype(jnp.bfloat16)
    return (attended[None], new_keys[None], new_values[None])


def solution(mesh):
    return jax.shard_map(
        body,
        mesh=mesh,
        in_specs=(
            P("req", "kv", None),
            P("req"),
            P("req", "kv", None),
            P("req", "kv", None),
            P(),
            P("req", "kv"),
            P("req", "kv"),
            P("req", "kv"),
            P("req", "kv"),
        ),
        out_specs=(P("req", "kv", None), P("req", "kv", None), P("req", "kv", None)),
        check_vma=False,
    )
```

```python
import functools

import jax
import jax.numpy as jnp
from jax import lax
from jax.sharding import PartitionSpec as P
from jax.experimental import pallas as pl
from jax.experimental.pallas import tpu as pltpu

H = 16
KVH = 8
HD = 96


rope_base = 100000.0
masked_score = -1e30


def rms_norm(states, gain):
    mean_square = jnp.mean(states * states, axis=-1, keepdims=True)
    scaled = states * lax.rsqrt(mean_square + 1e-05) * gain.astype(jnp.float32)
    return scaled.astype(jnp.bfloat16)


def rotate(values, positions):
    count = values.shape[0]
    heads = values.shape[1] // HD
    half = HD // 2
    frequency = rope_base ** (-(jnp.arange(half, dtype=jnp.float32) * 2.0 / HD))
    angle = positions[:, None] * frequency[None, :]
    cosine = jnp.cos(angle)[:, None, :]
    sine = jnp.sin(angle)[:, None, :]
    shaped = values.reshape(count, heads, HD)
    first = shaped[..., :half]
    second = shaped[..., half:]
    turned = jnp.concatenate(
        [first * cosine - second * sine, second * cosine + first * sine], axis=-1
    )
    return turned.reshape(count, heads * HD)


Z_RUN = 8
Y_RUN = 2
MESH = pl.DeviceIdType.MESH


def remote(src, dst, send, recv, device):
    return pltpu.make_async_remote_copy(
        src_ref=src, dst_ref=dst, send_sem=send, recv_sem=recv,
        device_id=device, device_id_type=MESH,
    )


def plane_ring_kernel(planes, runs, src_ref, kc_ref, vc_ref, out_ref, kc_out, vc_out, s1_send,
                      s1_recv, r_send, r_recv, l_send, l_recv, local_sem, kv_send, kv_recv, kv_local):
    me = lax.axis_index("req")
    kv = lax.axis_index("kv")
    y_me = lax.rem(me, Y_RUN)
    z_me = lax.rem(me // Y_RUN, runs)
    x_me = me // (Y_RUN * runs)
    q_me = x_me * Y_RUN + y_me
    right_hops = runs // 2
    left_hops = runs - 1 - right_hops

    def plane_peer(q):
        return ((q // Y_RUN) * runs + z_me) * Y_RUN + lax.rem(q, Y_RUN)

    def ring_peer(z):
        return (x_me * runs + z) * Y_RUN + y_me

    z_right = lax.rem(z_me + 1, runs)
    z_left = lax.rem(z_me + runs - 1, runs)

    barrier = pltpu.get_barrier_semaphore()

    def greet(step, carry):
        q = lax.rem(q_me + step, planes)
        pl.semaphore_signal(barrier, inc=1, device_id=(plane_peer(q), kv), device_id_type=MESH)
        return carry

    lax.fori_loop(1, planes, greet, 0)
    pl.semaphore_signal(barrier, inc=1, device_id=(ring_peer(z_right), kv), device_id_type=MESH)
    pl.semaphore_signal(barrier, inc=1, device_id=(ring_peer(z_left), kv), device_id_type=MESH)
    kv_count = lax.axis_size("kv")

    def greet_kv(step, carry):
        peer = lax.rem(kv + step, kv_count)
        pl.semaphore_signal(barrier, inc=1, device_id=(me, peer), device_id_type=MESH)
        return carry

    lax.fori_loop(1, kv_count, greet_kv, 0)
    pl.semaphore_wait(barrier, planes + 1 + kv_count - 1)

    local = pltpu.make_async_copy(src_ref, out_ref.at[z_me, q_me], local_sem)
    local.start()
    caches = ((kc_ref, kc_out), (vc_ref, vc_out))
    local_cache = []
    for which, (cache_src, cache_dst) in enumerate(caches):
        c = pltpu.make_async_copy(cache_src.at[kv], cache_dst.at[kv], kv_local.at[which])
        c.start()
        local_cache.append(c)


    def send(step, carry):
        q = lax.rem(q_me + step, planes)
        remote(src_ref, out_ref.at[z_me, q_me], s1_send.at[step - 1], s1_recv.at[step - 1],
               (plane_peer(q), kv)).start()
        return carry

    lax.fori_loop(1, planes, send, 0)

    def finish(step, carry):
        q = lax.rem(q_me + step, planes)
        source = lax.rem(q_me + planes - step, planes)
        remote(src_ref, out_ref.at[z_me, q_me], s1_send.at[step - 1], s1_recv.at[step - 1],
               (plane_peer(q), kv)).wait_send()
        remote(src_ref, out_ref.at[z_me, source], s1_send.at[step - 1], s1_recv.at[step - 1],
               (plane_peer(source), kv)).wait_recv()
        return carry

    lax.fori_loop(1, planes, finish, 0)
    local.wait()

    split = 2 if planes % 2 == 0 else 1
    share = planes // split

    def ring_copy(z_block, h, send, recv, k, z_to):
        part = out_ref.at[z_block, pl.ds(h * share, share)]
        return remote(part, part, send.at[k, h], recv.at[k, h], (ring_peer(z_to), kv))

    if split == 2:
        right_of = (right_hops, left_hops)
        left_of = (left_hops, right_hops)
    else:
        right_of = (right_hops,)
        left_of = (left_hops,)
    sent = []
    for h in range(split):
        if right_of[h] > 0:
            c = ring_copy(z_me, h, r_send, r_recv, 0, z_right)
            c.start()
            sent.append(c)
        if left_of[h] > 0:
            c = ring_copy(z_me, h, l_send, l_recv, 0, z_left)
            c.start()
            sent.append(c)

    def send_kv(step, carry):
        peer = lax.rem(kv + step, kv_count)
        for which, (cache_src, cache_dst) in enumerate(caches):
            remote(cache_src.at[peer], cache_dst.at[kv], kv_send.at[which, step - 1],
                   kv_recv.at[which, step - 1], (me, peer)).start()
        return carry

    for k in range(1, max(right_of + left_of) + 1):
        if k == 2:
            lax.fori_loop(1, kv_count, send_kv, 0)
        for h in range(split):
            if k <= right_of[h]:
                z_from = lax.rem(z_me + runs - k, runs)
                ring_copy(z_from, h, r_send, r_recv, k - 1, z_right).wait_recv()
                if k < right_of[h]:
                    c = ring_copy(z_from, h, r_send, r_recv, k, z_right)
                    c.start()
                    sent.append(c)
            if k <= left_of[h]:
                z_from = lax.rem(z_me + k, runs)
                ring_copy(z_from, h, l_send, l_recv, k - 1, z_left).wait_recv()
                if k < left_of[h]:
                    c = ring_copy(z_from, h, l_send, l_recv, k, z_left)
                    c.start()
                    sent.append(c)
    for c in sent:
        c.wait_send()

    def finish_kv(step, carry):
        peer = lax.rem(kv + step, kv_count)
        source = lax.rem(kv + kv_count - step, kv_count)
        for which, (cache_src, cache_dst) in enumerate(caches):
            remote(cache_src.at[peer], cache_dst.at[kv], kv_send.at[which, step - 1],
                   kv_recv.at[which, step - 1], (me, peer)).wait_send()
            remote(cache_src.at[kv], cache_dst.at[source], kv_send.at[which, step - 1],
                   kv_recv.at[which, step - 1], (me, source)).wait_recv()
        return carry

    lax.fori_loop(1, kv_count, finish_kv, 0)
    for c in local_cache:
        c.wait()


def gather_req(piece, keys_send, values_send):
    count = lax.axis_size("req")
    kv_count = lax.axis_size("kv")
    runs = min(Z_RUN, count // Y_RUN)
    planes = count // runs
    rows, width = piece.shape
    hops = max(runs - 1, 1)
    anywhere = pl.BlockSpec(memory_space=pl.ANY)
    gathered, keys_old, values_old = pl.pallas_call(
        functools.partial(plane_ring_kernel, planes, runs),
        out_shape=(
            jax.ShapeDtypeStruct((runs, planes, rows, width), piece.dtype),
            jax.ShapeDtypeStruct(keys_send.shape, keys_send.dtype),
            jax.ShapeDtypeStruct(values_send.shape, values_send.dtype),
        ),
        in_specs=[anywhere, anywhere, anywhere],
        out_specs=(anywhere, anywhere, anywhere),
        scratch_shapes=[
            pltpu.SemaphoreType.DMA((planes - 1,)),
            pltpu.SemaphoreType.DMA((planes - 1,)),
            pltpu.SemaphoreType.DMA((hops, 2)),
            pltpu.SemaphoreType.DMA((hops, 2)),
            pltpu.SemaphoreType.DMA((hops, 2)),
            pltpu.SemaphoreType.DMA((hops, 2)),
            pltpu.SemaphoreType.DMA,
            pltpu.SemaphoreType.DMA((2, kv_count - 1)),
            pltpu.SemaphoreType.DMA((2, kv_count - 1)),
            pltpu.SemaphoreType.DMA((2,)),
        ],
        compiler_params=pltpu.CompilerParams(collective_id=0, has_side_effects=True),
    )(piece, keys_send, values_send)
    return gathered.reshape(count * rows, width), keys_old, values_old


def req_order(block, count, piece_rows):
    runs = min(Z_RUN, count // Y_RUN)
    x_count = count // (runs * Y_RUN)
    shaped = block.reshape(runs, x_count, Y_RUN, piece_rows, block.shape[1])
    return jnp.transpose(shaped, (1, 0, 2, 3, 4)).reshape(block.shape)


def gathered_order(normed, count, piece_rows):
    runs = min(Z_RUN, count // Y_RUN)
    x_count = count // (runs * Y_RUN)
    rows = normed.shape[0]
    shaped = normed.reshape(rows, x_count, runs, Y_RUN, piece_rows)
    return jnp.transpose(shaped, (0, 2, 1, 3, 4)).reshape(rows, -1)


BLOCK_Q = 512
BLOCK_K = 512


def flash_kernel(tokens, scale, len_ref, q_ref, kc_ref, vc_ref, kn_ref, vn_ref, o_ref):
    block_q = q_ref.shape[1]
    block_k = kc_ref.shape[2]
    width = q_ref.shape[2]
    i = pl.program_id(1)
    length = len_ref[0]
    first = lax.rem(i * block_q, tokens)
    q = q_ref[0]
    query_index = first + lax.broadcasted_iota(jnp.int32, (block_q, block_k), 0)
    key_offset = lax.broadcasted_iota(jnp.int32, (block_q, block_k), 1)

    def step(keys, values, visible, carry):
        peak, total, acc = carry
        score = lax.dot_general(
            q, keys, (((1,), (1,)), ((), ())), preferred_element_type=jnp.float32
        ) * scale
        score = jnp.where(visible, score, masked_score)
        new_peak = jnp.maximum(peak, jnp.max(score, axis=1, keepdims=True))
        alpha = jnp.exp(peak - new_peak)
        weights = jnp.where(visible, jnp.exp(score - new_peak), 0.0)
        total = alpha * total + jnp.sum(weights, axis=1, keepdims=True)
        acc = alpha * acc + jnp.dot(
            weights.astype(jnp.bfloat16), values, preferred_element_type=jnp.float32
        )
        return new_peak, total, acc

    def cache_step(block, carry):
        start = pl.multiple_of(block * block_k, block_k)
        keys = kc_ref[block, 0]
        values = vc_ref[block, 0]
        visible = start + key_offset < length
        return step(keys, values, visible, carry)

    def new_step(block, carry):
        start = pl.multiple_of(block * block_k, block_k)
        keys = kn_ref[0, pl.ds(start, block_k), :]
        values = vn_ref[0, pl.ds(start, block_k), :]
        visible = start + key_offset <= query_index
        return step(keys, values, visible, carry)

    carry = (
        jnp.full((block_q, 1), -jnp.inf, jnp.float32),
        jnp.zeros((block_q, 1), jnp.float32),
        jnp.zeros((block_q, width), jnp.float32),
    )
    live_blocks = (length + block_k - 1) // block_k
    carry = lax.fori_loop(0, live_blocks, cache_step, carry)
    new_blocks = (first + block_q - 1) // block_k + 1
    peak, total, acc = lax.fori_loop(0, new_blocks, new_step, carry)
    o_ref[0] = (acc / total).astype(o_ref.dtype)


def flash_attention(lengths, queries, keys_old, values_old, keys_new, values_new, tokens, scale):
    heads, rows, width = queries.shape
    blocks, _, block_k, _ = keys_old.shape
    slots = blocks * block_k
    block_q = min(BLOCK_Q, tokens)
    grid = (heads, rows // block_q)
    whole_cache = pl.BlockSpec((blocks, 1, block_k, width), lambda c, i, n: (0, c, 0, 0))
    whole_new = pl.BlockSpec((1, tokens, width), lambda c, i, n: (c, 0, 0))
    return pl.pallas_call(
        functools.partial(flash_kernel, tokens, scale),
        out_shape=jax.ShapeDtypeStruct((heads, rows, width), jnp.bfloat16),
        grid_spec=pltpu.PrefetchScalarGridSpec(
            num_scalar_prefetch=1,
            grid=grid,
            in_specs=[
                pl.BlockSpec((1, block_q, width), lambda c, i, n: (c, i, 0)),
                whole_cache, whole_cache, whole_new, whole_new,
            ],
            out_specs=pl.BlockSpec((1, block_q, width), lambda c, i, n: (c, i, 0)),
        ),
        cost_estimate=pl.CostEstimate(
            flops=4 * heads * rows * (slots + tokens) * width,
            transcendentals=heads * rows * (slots + tokens),
            bytes_accessed=2 * width * heads * (2 * rows + 2 * slots + 2 * tokens),
        ),
    )(lengths, queries, keys_old, values_old, keys_new, values_new)


def body(hidden, lengths, key_cache, value_cache, norm_gain, w_query, w_key, w_value, w_out):
    rows_here = hidden.shape[1]
    kv_count = lax.axis_size("kv")
    appended = rows_here * kv_count
    slots = key_cache.shape[1]
    groups = H // KVH
    scale = HD ** (-0.5)
    length = lengths[0]
    q_cols = w_query.shape[1]
    k_cols = w_key.shape[1]
    v_cols = w_value.shape[1]
    heads_here = q_cols // HD
    kv_heads_here = k_cols // HD

    normed = rms_norm(hidden[0].astype(jnp.float32), norm_gain)
    normed = gathered_order(normed, lax.axis_size("req"), w_query.shape[0])
    normed_all = lax.all_gather(normed, "kv", axis=0, tiled=True)

    pieces = jnp.concatenate([w_query, w_key, w_value, w_out], axis=1)
    def to_peers(cache):
        return jnp.transpose(
            cache.reshape(slots, kv_count, kv_heads_here, HD), (1, 2, 0, 3)
        )

    cols, keys_old, values_old = gather_req(
        pieces, to_peers(key_cache[0]), to_peers(value_cache[0])
    )
    wq = cols[:, :q_cols]
    wk = cols[:, q_cols:q_cols + k_cols]
    wv = cols[:, q_cols + k_cols:q_cols + k_cols + v_cols]
    wo = req_order(cols[:, q_cols + k_cols + v_cols:], lax.axis_size("req"), w_query.shape[0])

    wo_full = lax.all_gather(wo, "kv", axis=1, tiled=True)

    positions = (length + jnp.arange(appended, dtype=jnp.int32)).astype(jnp.float32)
    half = HD // 2
    frequency = rope_base ** (-(jnp.arange(half, dtype=jnp.float32) * 2.0 / HD))
    angle = positions[:, None] * frequency[None, :]
    cosine = jnp.cos(angle)
    sine = jnp.sin(angle)

    def turn(values):
        first = values[..., :half]
        second = values[..., half:]
        return jnp.concatenate(
            [first * cosine - second * sine, second * cosine + first * sine], axis=-1
        )

    width = normed_all.shape[1]
    proj_q = jnp.einsum(
        "td,dcgh->cgth", normed_all, wq.reshape(width, kv_heads_here, groups, HD),
        preferred_element_type=jnp.float32,
    )
    proj_k = jnp.einsum(
        "td,dch->cth", normed_all, wk.reshape(width, kv_heads_here, HD),
        preferred_element_type=jnp.float32,
    )
    proj_v = jnp.einsum(
        "td,dch->cth", normed_all, wv.reshape(width, kv_heads_here, HD),
        preferred_element_type=jnp.float32,
    )
    query_heads = turn(proj_q).astype(jnp.bfloat16).reshape(kv_heads_here, groups * appended, HD)
    keys_new = turn(proj_k).astype(jnp.bfloat16)
    values_new = proj_v.astype(jnp.bfloat16)

    def to_tokens(values):
        parts = values.reshape(kv_heads_here, kv_count, rows_here, HD)
        got = lax.all_to_all(parts, "kv", split_axis=1, concat_axis=1, tiled=True)
        return jnp.transpose(got, (2, 1, 0, 3)).reshape(rows_here, kv_count * kv_heads_here * HD)

    new_keys = to_tokens(keys_new)
    new_values = to_tokens(values_new)

    contexts = flash_attention(
        lengths, query_heads, keys_old, values_old, keys_new, values_new, appended, scale,
    )
    parts = contexts.reshape(kv_heads_here, groups, kv_count, rows_here, HD)
    got = lax.all_to_all(parts, "kv", split_axis=2, concat_axis=2, tiled=True)
    attended = jnp.einsum(
        "cgsth,scghn->tn", got,
        wo_full.reshape(kv_count, kv_heads_here, groups, HD, wo_full.shape[1]),
        preferred_element_type=jnp.float32,
    ).astype(jnp.bfloat16)
    return (attended[None], new_keys[None], new_values[None])


def solution(mesh):
    return jax.shard_map(
        body,
        mesh=mesh,
        in_specs=(
            P("req", "kv", None),
            P("req"),
            P("req", "kv", None),
            P("req", "kv", None),
            P(),
            P("req", "kv"),
            P("req", "kv"),
            P("req", "kv"),
            P("req", "kv"),
        ),
        out_specs=(P("req", "kv", None), P("req", "kv", None), P("req", "kv", None)),
        check_vma=False,
    )
```
